32 devices in a mesh: seq: 32 (over z, y, x, core).
Axes of the slice: x: 2, y: 2, z: 4, core: 2. Of those that a mesh axis runs over, the one named last changes fastest.
Arguments:
- x_first: float32 [8192, 1024], P('seq'), may hold values from -6 to 6
- x_second: float32 [8192, 1024], P('seq'), may hold values from -6 to 6
- w_qk: float32 [1024, 1024], P('seq'), may hold values from -3 to 3
- w_value: float32 [1024, 1024], P('seq'), may hold values from -0.1875 to 0.1875
- w_out: float32 [1024, 1024], P('seq'), may hold values from -0.75 to 0.75
- gain_attn: float32 [1024], P('seq'), may hold values from 0.5 to 1.5
- bias_attn: float32 [1024], P('seq'), may hold values from -3 to 3
- gain_ffn: float32 [1024], P('seq'), may hold values from 0.5 to 1.5
- bias_ffn: float32 [1024], P('seq'), may hold values from -3 to 3
- w_up: float32 [1024, 4096], P('seq'), may hold values from -0.1875 to 0.1875
- bias_up: float32 [4096], P('seq'), may hold values from -3 to 3
- w_down: float32 [4096, 1024], P('seq'), may hold values from -0.09375 to 0.09375
- bias_down: float32 [1024], P('seq'), may hold values from -3 to 3
- sort_order: int32 [4, 8192], P(None, 'seq'), may hold values from 0 to 8191, as said below
- inverse: int32 [4, 8192], P(None, 'seq'), may hold values from 0 to 8191, as said below
- lengths: int32 [2], replicated, may hold values from 1 to 6144, 8192 in all
- dy_first: float32 [8192, 1024], P('seq'), may hold values from -6 to 6
- dy_second: float32 [8192, 1024], P('seq'), may hold values from -6 to 6
Outputs:
- y_first: float32 [8192, 1024], P('seq')
- y_second: float32 [8192, 1024], P('seq')
- dx_first: float32 [8192, 1024], P('seq')
- dx_second: float32 [8192, 1024], P('seq')
- grad_qk: float32 [1024, 1024], P('seq')
- grad_value: float32 [1024, 1024], P('seq')
- grad_out: float32 [1024, 1024], P('seq')
- grad_gain_attn: float32 [1024], P('seq')
- grad_bias_attn: float32 [1024], P('seq')
- grad_gain_ffn: float32 [1024], P('seq')
- grad_bias_ffn: float32 [1024], P('seq')
- grad_up: float32 [1024, 4096], P('seq')
- grad_bias_up: float32 [4096], P('seq')
- grad_down: float32 [4096, 1024], P('seq')
- grad_bias_down: float32 [1024], P('seq')
The draws below stay inside these ranges and needn't reach their ends.
Inputs may be any that keep to these rules, and one draw needn't show every extreme that they name: Row r lists the tokens in the order in which hash round r sorts them: sorted position p holds token sort_order[r, p], each row is a permutation of the 8192 tokens. Of the 256 tokens of one device, at most 16 fall into the sorted positions from k * 256 to (k + 1) * 256 - 1 of any one device k, and this most is reached in every round. inverse[r, sort_order[r, p]] = p for every round r and position p. The lengths sum to 8192; the longest is at most 6144.
All inputs are finite; a program needn't handle non-finite values.
Results may differ from the reference program's by a relative error of at most 0.014.
The reference program's roundings to bfloat16 on the way count: a program that leaves them out, or rounds other values in their place, can miss the bound.
Values may be sent and summed in bfloat16 or wider, within the bound.
No kernel may reach another device: no remote copies, remote signals or barrier semaphores. Data moves between devices by JAX's collectives and lax.ppermute only.
A program may use at most 256 MiB of HBM per device.

```python
import math
import jax
import jax.numpy as jnp
import numpy as np
from jax import lax

D = 1024
HEADS = 8
HEAD_DIM = 128
FF = 4096
SPAN = 64
ROUNDS = 4
TOK_DEV = 256
TOKENS = 8192
DOCS = 2
LONGEST = 6144
N_SEQ = 32


def round_orders(key):

    def one_round(round_key):
        split_keys = jax.random.split(round_key, 5)
        outer_map = jax.random.permutation(split_keys[0], N_SEQ)
        inner_map = jax.random.permutation(split_keys[1], N_SEQ)
        classes = jax.random.permutation(split_keys[2], N_SEQ)
        average = TOK_DEV // N_SEQ
        table = jnp.array([2 * average, average, average // 2, average - average // 2], dtype=jnp.int32)
        counts = table[classes * 4 // N_SEQ]
        bounds = jnp.cumsum(counts)
        offset = jnp.sum((jnp.arange(TOK_DEV, dtype=jnp.int32)[:, None] >= bounds[None, :]).astype(jnp.int32), axis=1)
        slot_dest = outer_map[(inner_map[:, None] + offset[None, :]) % N_SEQ]
        local_keys = jax.random.split(split_keys[3], N_SEQ)
        shuffled = jax.vmap(lambda k: jax.random.permutation(k, TOK_DEV))(local_keys)
        placement = jnp.argsort(shuffled, axis=1)
        destination = jnp.take_along_axis(slot_dest, placement, axis=1)
        tiebreak = jax.random.permutation(split_keys[4], TOKENS)
        score = destination.reshape(-1).astype(jnp.int32) * TOKENS + tiebreak.astype(jnp.int32)
        order_row = jnp.argsort(score).astype(jnp.int32)
        return (order_row, jnp.argsort(order_row).astype(jnp.int32))
    return jax.vmap(one_round)(jax.random.split(jax.random.fold_in(key, 7), ROUNDS))


def draw_sort_order(key, part):
    return round_orders(key)[0]


def draw_inverse(key, part):
    return round_orders(key)[1]


def shard_levels(own_key, dims, shards, least, top_value):
    loudness, own = 1.0, jax.random.fold_in(own_key, 6)
    for dim, blocks in shards:
        heights = jnp.exp(jax.random.uniform(jax.random.fold_in(own, dim), (blocks,), jnp.float32, least / len(shards), top_value / len(shards)))
        loudness = loudness * jnp.repeat(heights, dims[dim] // blocks).reshape([-1 if axis == dim else 1 for axis in range(len(dims))])
    return loudness


def length_profile(count, total, most, slope):
    weights = [(1 << 20) // math.isqrt(grade ** slope) + 1 for grade in range(2, count + 1)]
    spare, holding = total - most - (count - 1), [1] * (count - 1)
    while spare > 0:
        movable = [i for i in range(count - 1) if holding[i] < most]
        whole, left = sum([weights[i] for i in movable]), spare
        for i in movable:
            more = min(most - holding[i], max(1, left * weights[i] // whole), spare)
            holding[i] = holding[i] + more
            spare = spare - more
    return np.array([most] + holding)


def uneven(rng, number_of, total, limit, lean):
    if number_of == 2:
        one = jax.random.randint(rng, (), max(1, total - limit), min(limit, total - 1) + 1)
        return jnp.stack([one, total - one])
    sizes = jnp.asarray(length_profile(number_of, total, limit, lean), jnp.int32)
    pairs = (number_of - 1) // 2
    source_of, taker = sizes[1:1 + 2 * pairs:2], sizes[2:2 + 2 * pairs:2]
    slack = jnp.minimum(source_of - 1, limit - taker)
    shifted = jax.random.randint(jax.random.fold_in(rng, 1), (pairs,), 0, 1 << 20) % (slack + 1)
    sizes = sizes.at[1:1 + 2 * pairs:2].set(source_of - shifted).at[2:2 + 2 * pairs:2].set(taker + shifted)
    return sizes[jax.random.permutation(jax.random.fold_in(rng, 2), number_of)]


def scatter_about(key, shape, spread, most, cuts=(), held_as=jnp.bfloat16):
    values = jax.random.normal(key, shape, jnp.float32) * spread
    if len(cuts) > 0:
        values = shard_levels(key, shape, cuts, -0.22, 0.18) * values
    return jnp.clip(values, min=-most, max=most).astype(held_as)


def setup_inputs(seed: int = 0) -> dict:
    key_of = jax.random.split(jax.random.key(seed), 19)
    x_first = scatter_about(key_of[0], (TOKENS, D), 1.0, 6.0, ((0, 32),), jnp.float32)
    x_second = scatter_about(key_of[1], (TOKENS, D), 1.0, 6.0, ((0, 32),), jnp.float32)
    w_qk = scatter_about(key_of[2], (D, D), (max(1, D // (2 * HEAD_DIM))) ** -0.5, 3.0, ((0, 32),), jnp.float32)
    w_value = scatter_about(key_of[3], (D, D), D ** -0.5, 0.1875, ((0, 32),), jnp.float32)
    w_out = scatter_about(key_of[4], (D, D), (D // 16) ** -0.5, 0.75, ((0, 32),), jnp.float32)
    gain_attn = jnp.clip(1.0 + 0.1 * jax.random.normal(key_of[5], (D,), jnp.float32), 0.5, 1.5)
    bias_attn = scatter_about(key_of[6], (D,), 0.5, 3.0, ((0, 32),), jnp.float32)
    gain_ffn = jnp.clip(1.0 + 0.1 * jax.random.normal(key_of[7], (D,), jnp.float32), 0.5, 1.5)
    bias_ffn = scatter_about(key_of[8], (D,), 0.5, 3.0, ((0, 32),), jnp.float32)
    w_up = scatter_about(key_of[9], (D, FF), D ** -0.5, 0.1875, ((0, 32),), jnp.float32)
    bias_up = scatter_about(key_of[10], (FF,), 0.5, 3.0, ((0, 32),), jnp.float32)
    w_down = scatter_about(key_of[11], (FF, D), FF ** -0.5, 0.09375, ((0, 32),), jnp.float32)
    bias_down = scatter_about(key_of[12], (D,), 0.5, 3.0, ((0, 32),), jnp.float32)
    sort_order = draw_sort_order(jax.random.fold_in(key_of[18], 71), 0)
    inverse = draw_inverse(jax.random.fold_in(key_of[18], 71), 0)
    lengths = uneven(key_of[15], DOCS, TOKENS, LONGEST, 2).astype(jnp.int32)
    dy_first = scatter_about(key_of[16], (TOKENS, D), 1.0, 6.0, ((0, 32),), jnp.float32)
    dy_second = scatter_about(key_of[17], (TOKENS, D), 1.0, 6.0, ((0, 32),), jnp.float32)
    return {"x_first": x_first, "x_second": x_second, "w_qk": w_qk, "w_value": w_value, "w_out": w_out, "gain_attn": gain_attn, "bias_attn": bias_attn, "gain_ffn": gain_ffn, "bias_ffn": bias_ffn, "w_up": w_up, "bias_up": bias_up, "w_down": w_down, "bias_down": bias_down, "sort_order": sort_order, "inverse": inverse, "lengths": lengths, "dy_first": dy_first, "dy_second": dy_second}


@jax.custom_vjp
def low(v):
    return lax.optimization_barrier(v.astype(jnp.bfloat16)).astype(jnp.float32)

@jax.custom_vjp
def low_back(v):
    return v

def low_keep(v):
    return (low(v), None)

def low_pass(kept, grad):
    return (grad,)

def back_keep(v):
    return (v, None)

def back_low(kept, grad):
    return (low(grad),)
low.defvjp(low_keep, low_pass)
low_back.defvjp(back_keep, back_low)
EPSILON = 1e-05
HIGHEST = lax.Precision.HIGHEST

def product(matrix_a, matrix_b):
    return jnp.dot(matrix_a, matrix_b, precision=HIGHEST, preferred_element_type=jnp.float32)

def layer_norm(inputs, norm_gain, norm_shift):
    centered = inputs - lax.optimization_barrier(jnp.mean(inputs, axis=-1, keepdims=True))
    inv_std = lax.rsqrt(lax.optimization_barrier(jnp.mean(centered * centered, axis=-1, keepdims=True)) + EPSILON)
    return centered * inv_std * norm_gain + norm_shift

def segment_of(token_ids, doc_ends):
    return lax.optimization_barrier(jnp.sum((token_ids[:, None] >= doc_ends[None, :]).astype(jnp.int32), axis=1)).astype(jnp.int32)

def span_block(pieces):
    queries, key_rows, value_keys, query_ids, key_ids, query_seg, key_seg = pieces
    blocks = queries.shape[0]
    q_heads = queries.reshape(blocks, SPAN, HEADS, HEAD_DIM)
    k_heads = key_rows.reshape(blocks, 2 * SPAN, HEADS, HEAD_DIM)
    v_heads = value_keys.reshape(blocks, 2 * SPAN, HEADS, HEAD_DIM)
    raw_dots = low_back(jnp.einsum('gihd,gjhd->ghij', q_heads, k_heads, precision=HIGHEST))
    key_norm = lax.rsqrt(lax.optimization_barrier(jnp.sum(k_heads * k_heads, axis=-1)))
    factor = jnp.transpose(key_norm, (0, 2, 1))[:, :, None, :] / math.sqrt(HEAD_DIM)
    allowed = ((key_ids[:, None, :] <= query_ids[:, :, None]) & (key_seg[:, None, :] == query_seg[:, :, None]))[:, None]
    itself = (key_ids[:, None, :] == query_ids[:, :, None])[:, None]
    scores = jnp.where(itself, -100000.0, jnp.where(allowed, raw_dots * factor, -1000000000.0))
    log_total = jax.nn.logsumexp(scores, axis=-1)
    attn_probs = low(jnp.exp(scores - log_total[..., None]))
    out_heads = low_back(jnp.einsum('ghij,gjhd->gihd', attn_probs, v_heads, precision=HIGHEST))
    return (out_heads.reshape(blocks, SPAN, HEADS * HEAD_DIM), jnp.transpose(log_total, (0, 2, 1)))

def spanned(inputs):
    blocks = inputs.shape[0] // SPAN
    current = inputs.reshape((blocks, SPAN) + inputs.shape[1:])
    return (current, jnp.concatenate([jnp.roll(current, 1, axis=0), current], axis=1))

def grouped(inputs):
    return inputs.reshape((inputs.shape[0] // 8, 8) + inputs.shape[1:])

def attention_round(qk_rows, value_rows, order_row, inverse_row, segments):
    current, key_rows = spanned(qk_rows[order_row])
    _, value_keys = spanned(value_rows[order_row])
    current_ids, key_ids = spanned(order_row)
    current_seg, key_seg = spanned(segments[order_row])
    block_outs, totals = lax.map(jax.checkpoint(span_block), (grouped(current), grouped(key_rows), grouped(value_keys), grouped(current_ids), grouped(key_ids), grouped(current_seg), grouped(key_seg)))
    return (block_outs.reshape(TOKENS, D)[inverse_row], totals.reshape(TOKENS, HEADS)[inverse_row])

def forward(x_first, x_second, w_qk, w_value, w_out, gain_attn, bias_attn, gain_ffn, bias_ffn, w_up, bias_up, w_down, bias_down, sort_order, inverse, segments):
    w_qk = low(w_qk)
    w_value = low(w_value)
    w_out = low(w_out)
    gain_attn = low(gain_attn)
    bias_attn = low(bias_attn)
    gain_ffn = low(gain_ffn)
    bias_ffn = low(bias_ffn)
    w_up = low(w_up)
    bias_up = low(bias_up)
    w_down = low(w_down)
    bias_down = low(bias_down)
    normed_one = low(layer_norm(x_second, gain_attn, bias_attn))
    qk_rows = low(low_back(product(normed_one, w_qk)))
    value_rows = low(low_back(product(normed_one, w_value)))
    round_outs = []
    round_lse = []
    for turn in range(ROUNDS):
        out_rows, lse_rows = attention_round(qk_rows, value_rows, sort_order[turn], inverse[turn], segments)
        round_outs.append(out_rows)
        round_lse.append(lse_rows)
    lse_all = jnp.stack(round_lse)
    merge = jnp.exp(lse_all - jax.nn.logsumexp(lse_all, axis=0))
    out_all = jnp.stack(round_outs).reshape(ROUNDS, TOKENS, HEADS, HEAD_DIM)
    mixed = low(lax.optimization_barrier(jnp.sum(merge[..., None] * out_all, axis=0)).reshape(TOKENS, D))
    y_first = x_first + low_back(product(mixed, w_out))

    def feed_forward(inputs):
        normed_two = low(layer_norm(inputs, gain_ffn, bias_ffn))
        pre_up = low_back(product(normed_two, w_up) + bias_up)
        hidden = low(jax.nn.gelu(pre_up, approximate=True))
        return low_back(product(hidden, w_down) + bias_down)
    branch = lax.map(jax.checkpoint(feed_forward), y_first.reshape(TOKENS // 4096, 4096, D)).reshape(TOKENS, D)
    return (y_first, x_second + branch)

def reference(x_first, x_second, w_qk, w_value, w_out, gain_attn, bias_attn, gain_ffn, bias_ffn, w_up, bias_up, w_down, bias_down, sort_order, inverse, lengths, dy_first, dy_second):
    segments = segment_of(jnp.arange(TOKENS, dtype=jnp.int32), jnp.cumsum(lengths).astype(jnp.int32))

    def closed(x_first, x_second, w_qk, w_value, w_out, gain_attn, bias_attn, gain_ffn, bias_ffn, w_up, bias_up, w_down, bias_down):
        return forward(x_first, x_second, w_qk, w_value, w_out, gain_attn, bias_attn, gain_ffn, bias_ffn, w_up, bias_up, w_down, bias_down, sort_order, inverse, segments)
    outputs, pullback = jax.vjp(closed, x_first, x_second, w_qk, w_value, w_out, gain_attn, bias_attn, gain_ffn, bias_ffn, w_up, bias_up, w_down, bias_down)
    grads = pullback((dy_first, dy_second))
    return (outputs[0], outputs[1], grads[0], grads[1], grads[2], grads[3], grads[4], grads[5], grads[6], grads[7], grads[8], grads[9], grads[10], grads[11], grads[12])
```

```python
from functools import partial
import math

import jax
import jax.numpy as jnp
from jax import lax
from jax.experimental import pallas as pl
from jax.experimental.pallas import tpu as pltpu
from jax.sharding import PartitionSpec as P

HEADS = 8
HEAD_DIM = 128
SPAN = 64
ROUNDS = 4

EPSILON = 1e-05
SCALE = 1.0 / math.sqrt(HEAD_DIM)
BF = jnp.bfloat16
F32 = jnp.float32


def shifted(x, axis, by):
    size = lax.axis_size(axis)
    return lax.ppermute(x, axis, [(i, (i + by) % size) for i in range(size)])


def as_sent(x):
    return jax.tree.map(lambda a: a.astype(jnp.bfloat16) if a.dtype == jnp.float32 else a, x)


def layer_norm(inputs, norm_gain, norm_shift):
    centered = inputs - jnp.mean(inputs, axis=-1, keepdims=True)
    inv_std = lax.rsqrt(jnp.mean(centered * centered, axis=-1, keepdims=True) + EPSILON)
    normed = centered * inv_std
    return (normed * norm_gain + norm_shift, normed, inv_std)


def norm_back(grad_rows, normed, inv_std, norm_gain):
    grad_hat = grad_rows * norm_gain
    return inv_std * (
        grad_hat
        - jnp.mean(grad_hat, axis=-1, keepdims=True)
        - normed * jnp.mean(grad_hat * normed, axis=-1, keepdims=True)
    )


def linear(matrix_a, matrix_b):
    return jnp.dot(matrix_a, matrix_b, preferred_element_type=jnp.float32)


def inner_rows(matrix_a, matrix_b):
    return lax.dot_general(
        matrix_a, matrix_b, (((0,), (0,)), ((), ())), preferred_element_type=jnp.float32
    )


def outer_cols(matrix_a, matrix_b):
    return lax.dot_general(
        matrix_a, matrix_b, (((1,), (1,)), ((), ())), preferred_element_type=jnp.float32
    )


def segment_of(token_ids, doc_ends):
    return jnp.sum((token_ids[:, None] >= doc_ends[None, :]).astype(jnp.int32), axis=1)


def send_slots(target, tokens, devices, capacity):
    device = target // tokens
    onehot = (device[:, None] == jnp.arange(devices, dtype=jnp.int32)[None, :]).astype(jnp.int32)
    rank_in = jnp.sum(jnp.cumsum(onehot, axis=0) * onehot, axis=1) - 1
    return device * capacity + rank_in


def recv_slots(source_ids, tokens, capacity):
    device = source_ids // tokens
    earlier = (device[:, None] == device[None, :]) & (source_ids[None, :] < source_ids[:, None])
    return device * capacity + jnp.sum(earlier.astype(jnp.int32), axis=1)


def packed(inputs, slot_ids, devices, capacity):
    filled = (
        jnp.zeros((devices * capacity,) + inputs.shape[1:], inputs.dtype).at[slot_ids].set(inputs)
    )
    return filled.reshape((devices, capacity) + inputs.shape[1:])


def unpacked(received, slot_ids):
    return received.reshape((-1,) + received.shape[2:])[slot_ids]


def spanned(inputs, before):
    blocks = inputs.shape[0] // SPAN
    current = inputs.reshape((blocks, SPAN) + inputs.shape[1:])
    earlier = jnp.concatenate([before[None], current[:-1]], axis=0)
    return (current, jnp.concatenate([earlier, current], axis=1))


def arrange(got_qk, got_value, recv_slot):
    sorted_qk = unpacked(got_qk, recv_slot)
    sorted_value = unpacked(got_value, recv_slot)
    last_block = jnp.stack([sorted_qk[-SPAN:], sorted_value[-SPAN:]])
    return (sorted_qk, sorted_value, last_block)


def score_parts(sorted_rows, query_ids, before_ids, doc_ends):
    sorted_qk, sorted_value, before_qk, before_value = sorted_rows
    current, key_rows = spanned(sorted_qk, before_qk)
    _, value_keys = spanned(sorted_value, before_value)
    current_ids, key_ids = spanned(query_ids, before_ids)
    current_seg, key_seg = spanned(
        segment_of(query_ids, doc_ends), segment_of(before_ids, doc_ends)
    )
    blocks = current.shape[0]
    q_heads = current.reshape(blocks, SPAN, HEADS, HEAD_DIM)
    k_heads = key_rows.reshape(blocks, 2 * SPAN, HEADS, HEAD_DIM)
    v_heads = value_keys.reshape(blocks, 2 * SPAN, HEADS, HEAD_DIM)
    raw_dots = jnp.einsum("gihd,gjhd->ghij", q_heads, k_heads, preferred_element_type=jnp.float32)
    k_float = k_heads.astype(jnp.float32)
    key_norm = lax.rsqrt(jnp.sum(k_float * k_float, axis=-1))
    factor = jnp.transpose(key_norm, (0, 2, 1))[:, :, None, :] / math.sqrt(HEAD_DIM)
    allowed = (
        (key_ids[:, None, :] <= current_ids[:, :, None])
        & (key_seg[:, None, :] == current_seg[:, :, None])
    )[:, None]
    itself = (key_ids[:, None, :] == current_ids[:, :, None])[:, None]
    scores = jnp.where(itself, -100000.0, jnp.where(allowed, raw_dots * factor, -1000000000.0))
    log_total = jax.nn.logsumexp(scores, axis=-1)
    attn_probs = jnp.exp(scores - log_total[..., None])
    kept_mask = allowed & jnp.logical_not(itself)
    return (
        q_heads,
        k_heads,
        v_heads,
        k_float,
        key_norm,
        factor,
        kept_mask,
        raw_dots,
        attn_probs,
        log_total,
    )


def attend_out(pieces):
    (
        q_heads,
        k_heads,
        v_heads,
        k_float,
        key_norm,
        factor,
        kept_mask,
        raw_dots,
        attn_probs,
        log_total,
    ) = pieces
    blocks = q_heads.shape[0]
    out_heads = jnp.einsum(
        "ghij,gjhd->gihd",
        attn_probs.astype(jnp.bfloat16),
        v_heads,
        preferred_element_type=jnp.float32,
    )
    return (
        out_heads.reshape(blocks * SPAN, -1),
        jnp.transpose(log_total, (0, 2, 1)).reshape(blocks * SPAN, HEADS),
    )


def attend_back(pieces, grad_rows, grad_total):
    (
        q_heads,
        k_heads,
        v_heads,
        k_float,
        key_norm,
        factor,
        kept_mask,
        raw_dots,
        attn_probs,
        log_total,
    ) = pieces
    blocks = q_heads.shape[0]
    grad_heads = grad_rows.astype(jnp.bfloat16).reshape(blocks, SPAN, HEADS, HEAD_DIM)
    grad_lse = jnp.transpose(grad_total.reshape(blocks, SPAN, HEADS), (0, 2, 1))
    grad_prob = jnp.einsum(
        "gihd,gjhd->ghij", grad_heads, v_heads, preferred_element_type=jnp.float32
    )
    grad_val = jnp.einsum(
        "ghij,gihd->gjhd",
        attn_probs.astype(jnp.bfloat16),
        grad_heads,
        preferred_element_type=jnp.float32,
    )
    row_dot = jnp.sum(attn_probs * grad_prob, axis=-1, keepdims=True)
    grad_score = jnp.where(kept_mask, attn_probs * (grad_prob - row_dot + grad_lse[..., None]), 0.0)
    grad_raw = (grad_score * factor).astype(jnp.bfloat16)
    grad_norm = jnp.transpose(jnp.sum(grad_score * raw_dots, axis=2), (0, 2, 1)) / math.sqrt(
        HEAD_DIM
    )
    norm_cube = key_norm * key_norm * key_norm
    grad_query = jnp.einsum(
        "ghij,gjhd->gihd", grad_raw, k_heads, preferred_element_type=jnp.float32
    )
    grad_key = (
        jnp.einsum("ghij,gihd->gjhd", grad_raw, q_heads, preferred_element_type=jnp.float32)
        - (grad_norm * norm_cube)[..., None] * k_float
    )
    return (
        grad_query.reshape(blocks, SPAN, -1),
        grad_key.reshape(blocks, 2 * SPAN, -1),
        grad_val.reshape(blocks, 2 * SPAN, -1),
    )


def shards(
    x_first,
    x_second,
    w_qk,
    w_value,
    w_out,
    gain_attn,
    bias_attn,
    gain_ffn,
    bias_ffn,
    w_up,
    bias_up,
    w_down,
    bias_down,
    sort_order,
    inverse,
    lengths,
    dy_first,
    dy_second,
):
    devices = lax.axis_size("seq")
    tokens = x_first.shape[0]
    capacity = 2 * tokens // devices
    gathered = (
        lax.all_gather(w_qk.astype(jnp.bfloat16), "seq", axis=0, tiled=True),
        lax.all_gather(w_value.astype(jnp.bfloat16), "seq", axis=0, tiled=True),
        lax.all_gather(w_out.astype(jnp.bfloat16), "seq", axis=0, tiled=True),
        lax.all_gather(gain_attn.astype(jnp.bfloat16), "seq", axis=0, tiled=True),
        lax.all_gather(bias_attn.astype(jnp.bfloat16), "seq", axis=0, tiled=True),
        lax.all_gather(gain_ffn.astype(jnp.bfloat16), "seq", axis=0, tiled=True),
        lax.all_gather(bias_ffn.astype(jnp.bfloat16), "seq", axis=0, tiled=True),
        lax.all_gather(w_up.astype(jnp.bfloat16), "seq", axis=0, tiled=True),
        lax.all_gather(bias_up.astype(jnp.bfloat16), "seq", axis=0, tiled=True),
        lax.all_gather(w_down.astype(jnp.bfloat16), "seq", axis=0, tiled=True),
        lax.all_gather(bias_down.astype(jnp.bfloat16), "seq", axis=0, tiled=True),
    )
    m_qk, m_value, m_out, g_attn, b_attn, g_ffn, b_ffn, m_up, b_up, m_down, b_down = gathered
    gain_one = g_attn.astype(jnp.float32)
    gain_two = g_ffn.astype(jnp.float32)
    doc_ends = jnp.cumsum(lengths)
    send_list = [send_slots(inverse[turn], tokens, devices, capacity) for turn in range(ROUNDS)]
    recv_list = [recv_slots(sort_order[turn], tokens, capacity) for turn in range(ROUNDS)]
    before_ids = shifted(sort_order[:, tokens - SPAN :], "seq", 1)
    normed_one, hat_one, inv_one = layer_norm(x_second, gain_one, b_attn.astype(jnp.float32))
    normed_one = normed_one.astype(jnp.bfloat16)
    qk_rows = linear(normed_one, m_qk).astype(jnp.bfloat16)
    value_rows = linear(normed_one, m_value).astype(jnp.bfloat16)
    stashed = []
    round_outs = []
    round_lse = []
    for turn in range(ROUNDS):
        got_qk, got_value = (
            lax.all_to_all(
                packed(qk_rows, send_list[turn], devices, capacity),
                "seq",
                split_axis=0,
                concat_axis=0,
                tiled=True,
            ),
            lax.all_to_all(
                packed(value_rows, send_list[turn], devices, capacity),
                "seq",
                split_axis=0,
                concat_axis=0,
                tiled=True,
            ),
        )
        sorted_qk, sorted_value, last_block = arrange(got_qk, got_value, recv_list[turn])
        before_block = shifted(last_block, "seq", 1)
        sorted_rows = (sorted_qk, sorted_value, before_block[0], before_block[1])
        pieces = score_parts(sorted_rows, sort_order[turn], before_ids[turn], doc_ends)
        out_sorted, lse_sorted = attend_out(pieces)
        back_out, back_lse = (
            lax.all_to_all(
                packed(out_sorted, recv_list[turn], devices, capacity),
                "seq",
                split_axis=0,
                concat_axis=0,
                tiled=True,
            ),
            lax.all_to_all(
                packed(lse_sorted, recv_list[turn], devices, capacity),
                "seq",
                split_axis=0,
                concat_axis=0,
                tiled=True,
            ),
        )
        round_outs.append(unpacked(back_out, send_list[turn]))
        round_lse.append(unpacked(back_lse, send_list[turn]))
        stashed.append(sorted_rows)
    lse_all = jnp.stack(round_lse)
    out_all = jnp.stack(round_outs).reshape(ROUNDS, tokens, HEADS, HEAD_DIM)
    merge = jnp.exp(lse_all - jax.nn.logsumexp(lse_all, axis=0))
    mixed = jnp.sum(merge[..., None] * out_all, axis=0).reshape(tokens, -1).astype(jnp.bfloat16)
    y_first = x_first + linear(mixed, m_out)
    normed_two, hat_two, inv_two = layer_norm(y_first, gain_two, b_ffn.astype(jnp.float32))
    normed_two = normed_two.astype(jnp.bfloat16)
    pre_up = linear(normed_two, m_up) + b_up.astype(jnp.float32)
    hidden, gelu_back = jax.vjp(partial(jax.nn.gelu, approximate=True), pre_up)
    hidden = hidden.astype(jnp.bfloat16)
    y_second = x_second + (linear(hidden, m_down) + b_down.astype(jnp.float32))
    grad_f = dy_second.astype(jnp.bfloat16)
    grad_down = inner_rows(hidden, grad_f)
    grad_bias_down = jnp.sum(grad_f.astype(jnp.float32), axis=0)
    grad_pre = gelu_back(outer_cols(grad_f, m_down))[0].astype(jnp.bfloat16)
    grad_up = inner_rows(normed_two, grad_pre)
    grad_bias_up = jnp.sum(grad_pre.astype(jnp.float32), axis=0)
    grad_two = outer_cols(grad_pre, m_up)
    grad_gain_ffn = jnp.sum(grad_two * hat_two, axis=0)
    grad_bias_ffn = jnp.sum(grad_two, axis=0)
    dx_first = dy_first + norm_back(grad_two, hat_two, inv_two, gain_two)
    grad_attn = dx_first.astype(jnp.bfloat16)
    grad_out = inner_rows(mixed, grad_attn)
    grad_mixed = outer_cols(grad_attn, m_out).reshape(tokens, HEADS, HEAD_DIM)
    along = jnp.sum(grad_mixed[None] * out_all, axis=-1)
    grad_lse_all = merge * (along - jnp.sum(merge * along, axis=0, keepdims=True))
    grad_qk_sum = jnp.zeros((tokens, HEADS * HEAD_DIM), jnp.float32)
    grad_value_sum = jnp.zeros((tokens, HEADS * HEAD_DIM), jnp.float32)
    for turn in range(ROUNDS):
        grad_round = (merge[turn][..., None] * grad_mixed).reshape(tokens, -1)
        got_out, got_lse = (
            lax.all_to_all(
                packed(grad_round, send_list[turn], devices, capacity),
                "seq",
                split_axis=0,
                concat_axis=0,
                tiled=True,
            ),
            lax.all_to_all(
                packed(grad_lse_all[turn], send_list[turn], devices, capacity),
                "seq",
                split_axis=0,
                concat_axis=0,
                tiled=True,
            ),
        )
        sorted_grad_out = unpacked(got_out, recv_list[turn])
        sorted_grad_lse = unpacked(got_lse, recv_list[turn])
        sorted_rows = stashed[turn]
        pieces = score_parts(sorted_rows, sort_order[turn], before_ids[turn], doc_ends)
        grad_query, grad_key, grad_val = attend_back(pieces, sorted_grad_out, sorted_grad_lse)
        spill = shifted(
            jnp.stack([grad_key[0, :SPAN], grad_val[0, :SPAN]]).astype(jnp.bfloat16), "seq", -1
        ).astype(jnp.float32)
        key_add = jnp.concatenate([grad_key[1:, :SPAN], spill[0][None]], axis=0)
        value_add = jnp.concatenate([grad_val[1:, :SPAN], spill[1][None]], axis=0)
        sorted_grad_qk = (grad_query + grad_key[:, SPAN:] + key_add).reshape(tokens, -1)
        sorted_grad_value = (grad_val[:, SPAN:] + value_add).reshape(tokens, -1)
        back_qk, back_value = (
            lax.all_to_all(
                as_sent(packed(sorted_grad_qk, recv_list[turn], devices, capacity)),
                "seq",
                split_axis=0,
                concat_axis=0,
                tiled=True,
            ),
            lax.all_to_all(
                as_sent(packed(sorted_grad_value, recv_list[turn], devices, capacity)),
                "seq",
                split_axis=0,
                concat_axis=0,
                tiled=True,
            ),
        )
        grad_qk_sum = grad_qk_sum + unpacked(back_qk, send_list[turn])
        grad_value_sum = grad_value_sum + unpacked(back_value, send_list[turn])
    grad_qk_rows = grad_qk_sum.astype(jnp.bfloat16)
    grad_value_rows = grad_value_sum.astype(jnp.bfloat16)
    grad_qk = inner_rows(normed_one, grad_qk_rows)
    grad_value = inner_rows(normed_one, grad_value_rows)
    grad_one = outer_cols(grad_qk_rows, m_qk) + outer_cols(grad_value_rows, m_value)
    grad_gain_attn = jnp.sum(grad_one * hat_one, axis=0)
    grad_bias_attn = jnp.sum(grad_one, axis=0)
    dx_second = dy_second + norm_back(grad_one, hat_one, inv_one, gain_one)
    s_qk, s_value, s_out, s_gattn, s_battn, s_gffn, s_bffn, s_up, s_bup, s_down, s_bdown = (
        lax.psum_scatter(grad_qk, "seq", scatter_dimension=0, tiled=True),
        lax.psum_scatter(grad_value, "seq", scatter_dimension=0, tiled=True),
        lax.psum_scatter(grad_out, "seq", scatter_dimension=0, tiled=True),
        lax.psum_scatter(grad_gain_attn, "seq", scatter_dimension=0, tiled=True),
        lax.psum_scatter(grad_bias_attn, "seq", scatter_dimension=0, tiled=True),
        lax.psum_scatter(grad_gain_ffn, "seq", scatter_dimension=0, tiled=True),
        lax.psum_scatter(grad_bias_ffn, "seq", scatter_dimension=0, tiled=True),
        lax.psum_scatter(grad_up, "seq", scatter_dimension=0, tiled=True),
        lax.psum_scatter(grad_bias_up, "seq", scatter_dimension=0, tiled=True),
        lax.psum_scatter(grad_down, "seq", scatter_dimension=0, tiled=True),
        lax.psum_scatter(grad_bias_down, "seq", scatter_dimension=0, tiled=True),
    )
    return (
        y_first,
        y_second,
        dx_first,
        dx_second,
        s_qk,
        s_value,
        s_out,
        s_gattn,
        s_battn,
        s_gffn,
        s_bffn,
        s_up,
        s_bup,
        s_down,
        s_bdown,
    )


CAP_ROWS = 16
PARTS = 8


def dot_nn(a, b):
    return lax.dot_general(a, b, (((1,), (0,)), ((), ())), preferred_element_type=F32)


def dot_nt(a, b):
    return lax.dot_general(a, b, (((1,), (1,)), ((), ())), preferred_element_type=F32)


def dot_tn(a, b):
    return lax.dot_general(a, b, (((0,), (0,)), ((), ())), preferred_element_type=F32)


def hot_rows(slot_row, slots):
    ids = lax.broadcasted_iota(jnp.int32, (slots, slot_row.shape[1]), 0).astype(F32)
    return jnp.where(ids == slot_row, 1.0, 0.0).astype(BF)


def hot_cols(slot_col, slots):
    ids = lax.broadcasted_iota(jnp.int32, (slot_col.shape[0], slots), 1).astype(F32)
    return jnp.where(ids == slot_col, 1.0, 0.0).astype(BF)


def key_norm(keys):
    wide = keys.astype(F32)
    square = wide * wide
    high = square.astype(BF)
    low = (square - high.astype(F32)).astype(BF)
    ones = jnp.ones((8, keys.shape[1]), BF)
    return lax.rsqrt((dot_nt(ones, high) + dot_nt(ones, low))[0:1])


def span_scores(queries, keys, key_ids, query_ids, query_starts):
    raw = dot_nt(queries, keys)
    norm = key_norm(keys)
    factor = norm * SCALE
    kept = (key_ids < query_ids) & (key_ids >= query_starts)
    score = jnp.where(
        key_ids == query_ids, -100000.0, jnp.where(kept, raw * factor, -1000000000.0)
    )
    top = jnp.max(score, axis=1, keepdims=True)
    weight = jnp.exp(score - top)
    total = jnp.sum(weight, axis=1, keepdims=True)
    return raw, norm, factor, kept, weight, top, total


def three_parts(wide):
    high = wide.astype(BF).astype(F32)
    rest = wide - high
    mid = rest.astype(BF).astype(F32)
    return high, mid, rest - mid


def forward_kernel(place, x_0, x_1, x_2, x_3, info, key_ids, out, kept_rows, lanes, heads_out):
    blocks, tokens = info.shape[0], info.shape[2]
    slots = blocks * CAP_ROWS
    width = x_0.shape[1]
    spans = tokens // SPAN
    turn = place[0]
    rounds = ROUNDS

    for offset, rows in enumerate((x_0, x_1, x_2, x_3)):

        def pack(group, carry, offset=offset, rows=rows):
            source = group * rounds + lax.bitwise_xor(turn, offset)
            hot = hot_rows(info[source, 3:4, :], slots)
            start = pl.multiple_of(group * tokens, tokens)
            part = dot_nn(hot, rows[pl.ds(start, tokens), :]).astype(BF)
            lanes[:, pl.ds(source, 1)] = part.reshape(blocks, 1, CAP_ROWS, width)
            return carry

        lax.fori_loop(0, blocks // rounds, pack, 0)

    def place_rows(block, carry):
        cols = jnp.transpose(info[block])
        hot = hot_cols(cols[:, 2:3], slots)
        part = dot_nn(hot, lanes[block].reshape(slots, width)).astype(BF)
        start = pl.multiple_of(SPAN + block * tokens, SPAN)
        kept_rows[pl.ds(start, tokens), :] = part
        return carry

    lax.fori_loop(0, blocks, place_rows, 0)
    kept_rows[0:SPAN, :] = kept_rows[blocks * tokens : blocks * tokens + SPAN, :]

    def attend(block, carry):
        cols = jnp.transpose(info[block])
        lane = lax.broadcasted_iota(jnp.int32, (SPAN, width - HEAD_DIM), 1)
        pieces = []
        for part in range(spans):
            span = block * spans + part
            start = pl.multiple_of(span * SPAN, SPAN)
            rows = kept_rows[pl.ds(start, 2 * SPAN), :]
            queries = rows[SPAN:, :HEAD_DIM]
            ids = cols[part * SPAN : (part + 1) * SPAN]
            raw, norm, factor, kept, weight, top, total = span_scores(
                queries, rows[:, :HEAD_DIM], key_ids[pl.ds(span, 1), :], ids[:, 0:1], ids[:, 1:2]
            )
            probs = (weight * (1.0 / total)).astype(BF)
            mixed = dot_nn(probs, rows[:, HEAD_DIM:]).astype(BF)
            high, mid, low = three_parts(top + jnp.log(total))
            extra = jnp.where(
                lane == 0, high, jnp.where(lane == 1, mid, jnp.where(lane == 2, low, 0.0))
            ).astype(BF)
            pieces.append(jnp.concatenate([mixed, extra], axis=1))
        heads_out[block] = jnp.concatenate(pieces, axis=0)
        return carry

    lax.fori_loop(0, blocks, attend, 0)

    def unplace(block, carry):
        hot = hot_rows(info[block, 2:3, :], slots)
        part = dot_nn(hot, heads_out[block]).astype(BF)
        lanes[:, pl.ds(block, 1)] = part.reshape(blocks, 1, CAP_ROWS, width)
        return carry

    lax.fori_loop(0, blocks, unplace, 0)

    def unpack(source, carry):
        cols = jnp.transpose(info[source])
        hot = hot_cols(cols[:, 3:4], slots)
        part = dot_nn(hot, lanes[source].reshape(slots, width))
        out[source, 0:tokens, :] = part[:, :HEAD_DIM].astype(BF)
        flat = jnp.transpose(part[:, HEAD_DIM:])[0:PARTS, :].astype(BF)
        for piece in range(tokens // HEAD_DIM):
            first = tokens + piece * PARTS
            out[source, first : first + PARTS, :] = flat[
                :, piece * HEAD_DIM : (piece + 1) * HEAD_DIM
            ]
        return carry

    lax.fori_loop(0, blocks, unpack, 0)


def backward_kernel(grads, kept_rows, info, key_ids, out, lanes, sums):
    blocks, tokens = info.shape[0], info.shape[2]
    slots = blocks * CAP_ROWS
    width = kept_rows.shape[1]
    spans = tokens // SPAN

    def pack(source, carry):
        hot = hot_rows(info[source, 3:4, :], slots)
        flat = jnp.concatenate(
            [
                grads[source, tokens + piece * PARTS : tokens + (piece + 1) * PARTS, :].astype(F32)
                for piece in range(tokens // HEAD_DIM)
            ],
            axis=1,
        )
        tall = jnp.concatenate([flat, jnp.zeros((HEAD_DIM - PARTS, tokens), F32)], axis=0)
        rows = jnp.concatenate(
            [grads[source, 0:tokens, :], jnp.transpose(tall).astype(BF)], axis=1
        )
        part = dot_nn(hot, rows).astype(BF)
        lanes[:, pl.ds(source, 1)] = part.reshape(blocks, 1, CAP_ROWS, width)
        return carry

    lax.fori_loop(0, blocks, pack, 0)
    sums[0:SPAN, :] = jnp.zeros((SPAN, width), F32)

    def attend(block, carry):
        cols = jnp.transpose(info[block])
        hot = hot_cols(cols[:, 2:3], slots)
        part_grads = dot_nn(hot, lanes[block].reshape(slots, width))
        grad_rows = part_grads[:, :HEAD_DIM].astype(BF)
        grad_lse = (
            part_grads[:, HEAD_DIM : HEAD_DIM + 1]
            + part_grads[:, HEAD_DIM + 1 : HEAD_DIM + 2]
            + part_grads[:, HEAD_DIM + 2 : HEAD_DIM + 3]
        )
        held = []
        slopes = []
        for part in range(spans):
            span = block * spans + part
            start = pl.multiple_of(span * SPAN, SPAN)
            rows = kept_rows[pl.ds(start, 2 * SPAN), :]
            keys = rows[:, :HEAD_DIM]
            queries = rows[SPAN:, :HEAD_DIM]
            here = slice(part * SPAN, (part + 1) * SPAN)
            ids = cols[here]
            raw, norm, factor, kept, weight, top, total = span_scores(
                queries, keys, key_ids[pl.ds(span, 1), :], ids[:, 0:1], ids[:, 1:2]
            )
            probs = weight * (1.0 / total)
            grad_out = grad_rows[here]
            grad_prob = dot_nt(grad_out, rows[:, HEAD_DIM:])
            row_dot = jnp.sum(probs * grad_prob, axis=1, keepdims=True)
            grad_score = jnp.where(kept, probs * (grad_prob - row_dot + grad_lse[here]), 0.0)
            grad_raw = (grad_score * factor).astype(BF)
            slopes.append(
                jnp.sum(grad_score * raw, axis=0, keepdims=True) * SCALE * norm * norm * norm
            )
            grad_query = dot_nn(grad_raw, keys)
            grad_key = dot_tn(grad_raw, queries)
            grad_val = dot_tn(probs.astype(BF), grad_out)
            held.append((start, keys, grad_query, grad_key, grad_val))
        slopes.append(jnp.zeros((8 - spans, 2 * SPAN), F32))
        slope_cols = jnp.transpose(jnp.concatenate(slopes, axis=0))
        for part in range(spans):
            start, keys, grad_query, grad_key, grad_val = held[part]
            grad_key = grad_key - slope_cols[:, part : part + 1] * keys.astype(F32)
            sums[pl.ds(start, SPAN), :] += jnp.concatenate(
                [grad_key[:SPAN], grad_val[:SPAN]], axis=1
            )
            after = pl.multiple_of(start + SPAN, SPAN)
            sums[pl.ds(after, SPAN), :] = jnp.concatenate(
                [grad_query + grad_key[SPAN:], grad_val[SPAN:]], axis=1
            )
        return carry

    lax.fori_loop(0, blocks, attend, 0)
    sums[blocks * tokens : blocks * tokens + SPAN, :] += sums[0:SPAN, :]

    def unplace(block, carry):
        hot = hot_rows(info[block, 2:3, :], slots)
        start = pl.multiple_of(SPAN + block * tokens, SPAN)
        part = dot_nn(hot, sums[pl.ds(start, tokens), :].astype(BF)).astype(BF)
        lanes[:, pl.ds(block, 1)] = part.reshape(blocks, 1, CAP_ROWS, width)
        return carry

    lax.fori_loop(0, blocks, unplace, 0)

    def unpack(source, carry):
        cols = jnp.transpose(info[source])
        hot = hot_cols(cols[:, 3:4], slots)
        out[source] = dot_nn(hot, lanes[source].reshape(slots, width)).astype(BF)
        return carry

    lax.fori_loop(0, blocks, unpack, 0)


def in_vmem(count):
    return [pl.BlockSpec(memory_space=pltpu.VMEM)] * count


def run_forward(turn, rows, info, key_ids):
    blocks, _, tokens = info.shape
    width = rows[0].shape[1]
    positions = blocks * tokens
    extra = PARTS * tokens // HEAD_DIM
    return pl.pallas_call(
        forward_kernel,
        out_shape=(
            jax.ShapeDtypeStruct((blocks, tokens + extra, HEAD_DIM), BF),
            jax.ShapeDtypeStruct((SPAN + positions, width), BF),
        ),
        in_specs=[pl.BlockSpec(memory_space=pltpu.SMEM)] + in_vmem(6),
        out_specs=tuple(in_vmem(2)),
        scratch_shapes=[
            pltpu.VMEM((blocks, blocks, CAP_ROWS, width), BF),
            pltpu.VMEM((blocks, tokens, width), BF),
        ],
        compiler_params=pltpu.CompilerParams(vmem_limit_bytes=48 << 20),
        cost_estimate=pl.CostEstimate(
            flops=20 * 10**9, bytes_accessed=12 * 10**6, transcendentals=10**6
        ),
        name="hash_forward",
    )(turn, *rows, info, key_ids)


def run_backward(grads, kept_rows, info, key_ids):
    blocks, _, tokens = info.shape
    width = kept_rows.shape[1]
    positions = blocks * tokens
    return pl.pallas_call(
        backward_kernel,
        out_shape=jax.ShapeDtypeStruct((blocks, tokens, width), BF),
        in_specs=in_vmem(4),
        out_specs=in_vmem(1)[0],
        scratch_shapes=[
            pltpu.VMEM((blocks, blocks, CAP_ROWS, width), BF),
            pltpu.VMEM((SPAN + positions, width), F32),
        ],
        compiler_params=pltpu.CompilerParams(vmem_limit_bytes=48 << 20),
        cost_estimate=pl.CostEstimate(
            flops=20 * 10**9, bytes_accessed=12 * 10**6, transcendentals=10**6
        ),
        name="hash_backward",
    )(grads, kept_rows, info, key_ids)


def peers(mask):
    size = HEADS * ROUNDS
    return [(i, i ^ mask) for i in range(size)]


def swap(x, mask):
    return lax.ppermute(x, "seq", peers(mask))


def columns():
    return [[head * ROUNDS + turn for head in range(HEADS)] for turn in range(ROUNDS)]


def exchange(x, groups=None):
    return lax.all_to_all(
        x, "seq", split_axis=0, concat_axis=0, tiled=True, axis_index_groups=groups
    )


def rounded(x):
    return lax.reduce_precision(x, 8, 7)


def split_three(wide):
    high = rounded(wide)
    rest = wide - high
    mid = rounded(rest)
    return jnp.stack([high, mid, rest - mid])


def slots_sent(target, tokens, capacity):
    device = target // tokens
    early = jnp.arange(tokens)[None, :] < jnp.arange(tokens)[:, None]
    same = (device[:, None] == device[None, :]) & early
    return device * capacity + jnp.sum(same.astype(jnp.int32), axis=1)


def start_of(token_ids, doc_ends):
    ends = doc_ends[None, :]
    return jnp.max(jnp.where(ends <= token_ids[:, None], ends, 0), axis=1)


def shards_fast(
    x_first,
    x_second,
    w_qk,
    w_value,
    w_out,
    gain_attn,
    bias_attn,
    gain_ffn,
    bias_ffn,
    w_up,
    bias_up,
    w_down,
    bias_down,
    sort_order,
    inverse,
    lengths,
    dy_first,
    dy_second,
):
    devices = lax.axis_size("seq")
    tokens, features = x_first.shape
    capacity = 2 * tokens // devices
    shard = features // devices
    place = lax.axis_index("seq")
    doc_ends = jnp.cumsum(lengths)

    per_round = []
    vectors = rounded(
        jnp.concatenate([gain_attn, bias_attn, gain_ffn, bias_ffn, bias_up, bias_down])
    )
    vectors = jnp.pad(vectors, (0, 2 * tokens - vectors.shape[0])).reshape(2, tokens)
    for turn in range(ROUNDS):
        ids = sort_order[turn]
        rows = jnp.stack(
            [
                ids,
                start_of(ids, doc_ends),
                recv_slots(ids, tokens, capacity),
                slots_sent(inverse[turn], tokens, capacity),
            ]
        ).astype(F32)
        per_round.append(jnp.concatenate([rows, vectors, jnp.zeros((2, tokens), F32)]))
    info = jnp.tile(jnp.stack(per_round), (HEADS, 1, 1))
    info = exchange(info)
    got = info[:, 4:6].reshape(devices, 2 * tokens)

    def vector(first, size):
        return got[:, first : first + size].reshape(devices * size)

    gain_one, shift_one = vector(0, shard), vector(shard, shard)
    gain_two, shift_two = vector(2 * shard, shard), vector(3 * shard, shard)
    wide = bias_up.shape[0]
    b_up = vector(4 * shard, wide)
    b_down = vector(4 * shard + wide, shard)
    spans = info[:, 0].reshape(devices * tokens // SPAN, SPAN)
    key_ids = jnp.concatenate([jnp.roll(spans, 1, axis=0), spans], axis=1)

    pair = jnp.stack(
        [w_qk.reshape(shard, HEADS, HEAD_DIM), w_value.reshape(shard, HEADS, HEAD_DIM)], axis=2
    ).reshape(shard, 2 * features)
    m_attn = lax.all_gather(
        jnp.concatenate([pair, w_out], axis=1).astype(BF), "seq", axis=0, tiled=True
    )
    m_pair, m_out = m_attn[:, : 2 * features], m_attn[:, 2 * features :]
    m_up = lax.all_gather(w_up.astype(BF), "seq", axis=0, tiled=True)
    m_down = lax.all_gather(w_down.astype(BF), "seq", axis=0, tiled=True)

    normed_one, hat_one, inv_one = layer_norm(x_second, gain_one, shift_one)
    normed_one = normed_one.astype(BF)
    rows = linear(normed_one, m_pair).astype(BF)
    rows = jnp.transpose(rows.reshape(tokens, HEADS, 2 * HEAD_DIM), (1, 0, 2))
    own = exchange(rows, columns()).reshape(HEADS * tokens, 2 * HEAD_DIM)
    side = swap(own, 2)
    all_rows = (own, swap(own, 1), side, swap(side, 1))
    turn = (place % ROUNDS).astype(jnp.int32).reshape(1)
    sent, kept_rows = run_forward(turn, all_rows, info, key_ids)
    back = exchange(sent).reshape(HEADS, ROUNDS, -1, HEAD_DIM)
    out_all = jnp.transpose(back[:, :, :tokens], (1, 2, 0, 3)).astype(F32)
    pieces = back[:, :, tokens:].reshape(HEADS, ROUNDS, -1, PARTS, HEAD_DIM)[:, :, :, :3]
    lse_all = jnp.sum(pieces.astype(F32), axis=3).reshape(HEADS, ROUNDS, tokens)
    lse_all = jnp.transpose(lse_all, (1, 2, 0))

    merge = jnp.exp(lse_all - jax.nn.logsumexp(lse_all, axis=0))
    mixed = jnp.sum(merge[..., None] * out_all, axis=0).reshape(tokens, -1).astype(BF)
    y_first = x_first + linear(mixed, m_out)
    normed_two, hat_two, inv_two = layer_norm(y_first, gain_two, shift_two)
    normed_two = normed_two.astype(BF)
    pre_up = linear(normed_two, m_up) + b_up
    hidden, gelu_back = jax.vjp(partial(jax.nn.gelu, approximate=True), pre_up)
    hidden = hidden.astype(BF)
    y_second = x_second + (linear(hidden, m_down) + b_down)
    grad_f = dy_second.astype(BF)
    grad_down = inner_rows(hidden, grad_f)
    grad_bias_down = jnp.sum(grad_f.astype(F32), axis=0)
    grad_pre = gelu_back(outer_cols(grad_f, m_down))[0].astype(BF)
    grad_up = inner_rows(normed_two, grad_pre)
    grad_bias_up = jnp.sum(grad_pre.astype(F32), axis=0)
    grad_two = outer_cols(grad_pre, m_up)
    grad_gain_ffn = jnp.sum(grad_two * hat_two, axis=0)
    grad_bias_ffn = jnp.sum(grad_two, axis=0)
    dx_first = dy_first + norm_back(grad_two, hat_two, inv_two, gain_two)
    grad_attn = dx_first.astype(BF)
    grad_out = inner_rows(mixed, grad_attn)
    grad_mixed = outer_cols(grad_attn, m_out).reshape(tokens, HEADS, HEAD_DIM)
    along = jnp.sum(grad_mixed[None] * out_all, axis=-1)
    grad_lse_all = merge * (along - jnp.sum(merge * along, axis=0, keepdims=True))

    grad_round = (merge[..., None] * grad_mixed[None]).astype(BF)
    grad_round = jnp.transpose(grad_round, (2, 0, 1, 3)).reshape(devices, tokens, HEAD_DIM)
    parts = split_three(jnp.transpose(grad_lse_all, (2, 0, 1)).reshape(devices, tokens))
    parts = jnp.pad(parts, ((0, PARTS - 3), (0, 0), (0, 0)))
    parts = jnp.transpose(parts.reshape(PARTS, devices, -1, HEAD_DIM), (1, 2, 0, 3))
    parts = parts.reshape(devices, -1, HEAD_DIM).astype(BF)
    got_grads = exchange(jnp.concatenate([grad_round, parts], axis=1))
    grad_rows = exchange(run_backward(got_grads, kept_rows, info, key_ids))
    grad_rows = grad_rows.reshape(HEADS, ROUNDS, tokens, 2 * HEAD_DIM)
    grad_rows = jnp.sum(grad_rows.astype(F32), axis=1).astype(BF)
    grad_rows = jnp.transpose(grad_rows, (1, 0, 2)).reshape(tokens, 2 * features)

    grad_pair = inner_rows(normed_one, grad_rows)
    grad_one = outer_cols(grad_rows, m_pair)
    grad_gain_attn = jnp.sum(grad_one * hat_one, axis=0)
    grad_bias_attn = jnp.sum(grad_one, axis=0)
    dx_second = dy_second + norm_back(grad_one, hat_one, inv_one, gain_one)

    def scatter(x):
        return lax.psum_scatter(x.astype(BF), "seq", scatter_dimension=0, tiled=True).astype(F32)

    s_pair = scatter(grad_pair).reshape(shard, HEADS, 2, HEAD_DIM)
    s_qk = s_pair[:, :, 0].reshape(shard, features)
    s_value = s_pair[:, :, 1].reshape(shard, features)
    s_out = scatter(grad_out)
    s_up = scatter(grad_up)
    s_down = scatter(grad_down)
    small = jnp.concatenate(
        [
            grad_gain_attn.reshape(devices, -1),
            grad_bias_attn.reshape(devices, -1),
            grad_gain_ffn.reshape(devices, -1),
            grad_bias_ffn.reshape(devices, -1),
            grad_bias_up.reshape(devices, -1),
            grad_bias_down.reshape(devices, -1),
        ],
        axis=1,
    )
    small = jnp.sum(exchange(small[:, None]), axis=(0, 1))
    s_gattn, s_battn, s_gffn, s_bffn = (small[i * shard : (i + 1) * shard] for i in range(4))
    s_bup = small[4 * shard : 4 * shard + wide]
    s_bdown = small[4 * shard + wide :]
    return (
        y_first,
        y_second,
        dx_first,
        dx_second,
        s_qk,
        s_value,
        s_out,
        s_gattn,
        s_battn,
        s_gffn,
        s_bffn,
        s_up,
        s_bup,
        s_down,
        s_bdown,
    )


def solution(mesh):
    in_specs = (
        P("seq", None),
        P("seq", None),
        P("seq", None),
        P("seq", None),
        P("seq", None),
        P("seq"),
        P("seq"),
        P("seq"),
        P("seq"),
        P("seq", None),
        P("seq"),
        P("seq", None),
        P("seq"),
        P(None, "seq"),
        P(None, "seq"),
        P(),
        P("seq", None),
        P("seq", None),
    )
    out_specs = (
        P("seq", None),
        P("seq", None),
        P("seq", None),
        P("seq", None),
        P("seq", None),
        P("seq", None),
        P("seq", None),
        P("seq"),
        P("seq"),
        P("seq"),
        P("seq"),
        P("seq", None),
        P("seq"),
        P("seq", None),
        P("seq"),
    )
    fast = mesh.shape["seq"] == HEADS * ROUNDS
    return jax.shard_map(shards_fast if fast else shards, mesh=mesh, in_specs=in_specs, out_specs=out_specs, check_vma=False)
```

```python
from functools import partial
import math

import jax
import jax.numpy as jnp
from jax import lax
from jax.experimental import pallas as pl
from jax.experimental.pallas import tpu as pltpu
from jax.sharding import PartitionSpec as P

HEADS = 8
HEAD_DIM = 128
SPAN = 64
ROUNDS = 4

EPSILON = 1e-05
SCALE = 1.0 / math.sqrt(HEAD_DIM)
BF = jnp.bfloat16
F32 = jnp.float32


def shifted(x, axis, by):
    size = lax.axis_size(axis)
    return lax.ppermute(x, axis, [(i, (i + by) % size) for i in range(size)])


def as_sent(x):
    return jax.tree.map(lambda a: a.astype(jnp.bfloat16) if a.dtype == jnp.float32 else a, x)


def layer_norm(inputs, norm_gain, norm_shift):
    centered = inputs - jnp.mean(inputs, axis=-1, keepdims=True)
    inv_std = lax.rsqrt(jnp.mean(centered * centered, axis=-1, keepdims=True) + EPSILON)
    normed = centered * inv_std
    return (normed * norm_gain + norm_shift, normed, inv_std)


def norm_back(grad_rows, normed, inv_std, norm_gain):
    grad_hat = grad_rows * norm_gain
    return inv_std * (
        grad_hat
        - jnp.mean(grad_hat, axis=-1, keepdims=True)
        - normed * jnp.mean(grad_hat * normed, axis=-1, keepdims=True)
    )


def linear(matrix_a, matrix_b):
    return jnp.dot(matrix_a, matrix_b, preferred_element_type=jnp.float32)


def inner_rows(matrix_a, matrix_b):
    return lax.dot_general(
        matrix_a, matrix_b, (((0,), (0,)), ((), ())), preferred_element_type=jnp.float32
    )


def outer_cols(matrix_a, matrix_b):
    return lax.dot_general(
        matrix_a, matrix_b, (((1,), (1,)), ((), ())), preferred_element_type=jnp.float32
    )


def segment_of(token_ids, doc_ends):
    return jnp.sum((token_ids[:, None] >= doc_ends[None, :]).astype(jnp.int32), axis=1)


def send_slots(target, tokens, devices, capacity):
    device = target // tokens
    onehot = (device[:, None] == jnp.arange(devices, dtype=jnp.int32)[None, :]).astype(jnp.int32)
    rank_in = jnp.sum(jnp.cumsum(onehot, axis=0) * onehot, axis=1) - 1
    return device * capacity + rank_in


def recv_slots(source_ids, tokens, capacity):
    device = source_ids // tokens
    earlier = (device[:, None] == device[None, :]) & (source_ids[None, :] < source_ids[:, None])
    return device * capacity + jnp.sum(earlier.astype(jnp.int32), axis=1)


def packed(inputs, slot_ids, devices, capacity):
    filled = (
        jnp.zeros((devices * capacity,) + inputs.shape[1:], inputs.dtype).at[slot_ids].set(inputs)
    )
    return filled.reshape((devices, capacity) + inputs.shape[1:])


def unpacked(received, slot_ids):
    return received.reshape((-1,) + received.shape[2:])[slot_ids]


def spanned(inputs, before):
    blocks = inputs.shape[0] // SPAN
    current = inputs.reshape((blocks, SPAN) + inputs.shape[1:])
    earlier = jnp.concatenate([before[None], current[:-1]], axis=0)
    return (current, jnp.concatenate([earlier, current], axis=1))


def arrange(got_qk, got_value, recv_slot):
    sorted_qk = unpacked(got_qk, recv_slot)
    sorted_value = unpacked(got_value, recv_slot)
    last_block = jnp.stack([sorted_qk[-SPAN:], sorted_value[-SPAN:]])
    return (sorted_qk, sorted_value, last_block)


def score_parts(sorted_rows, query_ids, before_ids, doc_ends):
    sorted_qk, sorted_value, before_qk, before_value = sorted_rows
    current, key_rows = spanned(sorted_qk, before_qk)
    _, value_keys = spanned(sorted_value, before_value)
    current_ids, key_ids = spanned(query_ids, before_ids)
    current_seg, key_seg = spanned(
        segment_of(query_ids, doc_ends), segment_of(before_ids, doc_ends)
    )
    blocks = current.shape[0]
    q_heads = current.reshape(blocks, SPAN, HEADS, HEAD_DIM)
    k_heads = key_rows.reshape(blocks, 2 * SPAN, HEADS, HEAD_DIM)
    v_heads = value_keys.reshape(blocks, 2 * SPAN, HEADS, HEAD_DIM)
    raw_dots = jnp.einsum("gihd,gjhd->ghij", q_heads, k_heads, preferred_element_type=jnp.float32)
    k_float = k_heads.astype(jnp.float32)
    key_norm = lax.rsqrt(jnp.sum(k_float * k_float, axis=-1))
    factor = jnp.transpose(key_norm, (0, 2, 1))[:, :, None, :] / math.sqrt(HEAD_DIM)
    allowed = (
        (key_ids[:, None, :] <= current_ids[:, :, None])
        & (key_seg[:, None, :] == current_seg[:, :, None])
    )[:, None]
    itself = (key_ids[:, None, :] == current_ids[:, :, None])[:, None]
    scores = jnp.where(itself, -100000.0, jnp.where(allowed, raw_dots * factor, -1000000000.0))
    log_total = jax.nn.logsumexp(scores, axis=-1)
    attn_probs = jnp.exp(scores - log_total[..., None])
    kept_mask = allowed & jnp.logical_not(itself)
    return (
        q_heads,
        k_heads,
        v_heads,
        k_float,
        key_norm,
        factor,
        kept_mask,
        raw_dots,
        attn_probs,
        log_total,
    )


def attend_out(pieces):
    (
        q_heads,
        k_heads,
        v_heads,
        k_float,
        key_norm,
        factor,
        kept_mask,
        raw_dots,
        attn_probs,
        log_total,
    ) = pieces
    blocks = q_heads.shape[0]
    out_heads = jnp.einsum(
        "ghij,gjhd->gihd",
        attn_probs.astype(jnp.bfloat16),
        v_heads,
        preferred_element_type=jnp.float32,
    )
    return (
        out_heads.reshape(blocks * SPAN, -1),
        jnp.transpose(log_total, (0, 2, 1)).reshape(blocks * SPAN, HEADS),
    )


def attend_back(pieces, grad_rows, grad_total):
    (
        q_heads,
        k_heads,
        v_heads,
        k_float,
        key_norm,
        factor,
        kept_mask,
        raw_dots,
        attn_probs,
        log_total,
    ) = pieces
    blocks = q_heads.shape[0]
    grad_heads = grad_rows.astype(jnp.bfloat16).reshape(blocks, SPAN, HEADS, HEAD_DIM)
    grad_lse = jnp.transpose(grad_total.reshape(blocks, SPAN, HEADS), (0, 2, 1))
    grad_prob = jnp.einsum(
        "gihd,gjhd->ghij", grad_heads, v_heads, preferred_element_type=jnp.float32
    )
    grad_val = jnp.einsum(
        "ghij,gihd->gjhd",
        attn_probs.astype(jnp.bfloat16),
        grad_heads,
        preferred_element_type=jnp.float32,
    )
    row_dot = jnp.sum(attn_probs * grad_prob, axis=-1, keepdims=True)
    grad_score = jnp.where(kept_mask, attn_probs * (grad_prob - row_dot + grad_lse[..., None]), 0.0)
    grad_raw = (grad_score * factor).astype(jnp.bfloat16)
    grad_norm = jnp.transpose(jnp.sum(grad_score * raw_dots, axis=2), (0, 2, 1)) / math.sqrt(
        HEAD_DIM
    )
    norm_cube = key_norm * key_norm * key_norm
    grad_query = jnp.einsum(
        "ghij,gjhd->gihd", grad_raw, k_heads, preferred_element_type=jnp.float32
    )
    grad_key = (
        jnp.einsum("ghij,gihd->gjhd", grad_raw, q_heads, preferred_element_type=jnp.float32)
        - (grad_norm * norm_cube)[..., None] * k_float
    )
    return (
        grad_query.reshape(blocks, SPAN, -1),
        grad_key.reshape(blocks, 2 * SPAN, -1),
        grad_val.reshape(blocks, 2 * SPAN, -1),
    )


def shards(
    x_first,
    x_second,
    w_qk,
    w_value,
    w_out,
    gain_attn,
    bias_attn,
    gain_ffn,
    bias_ffn,
    w_up,
    bias_up,
    w_down,
    bias_down,
    sort_order,
    inverse,
    lengths,
    dy_first,
    dy_second,
):
    devices = lax.axis_size("seq")
    tokens = x_first.shape[0]
    capacity = 2 * tokens // devices
    gathered = (
        lax.all_gather(w_qk.astype(jnp.bfloat16), "seq", axis=0, tiled=True),
        lax.all_gather(w_value.astype(jnp.bfloat16), "seq", axis=0, tiled=True),
        lax.all_gather(w_out.astype(jnp.bfloat16), "seq", axis=0, tiled=True),
        lax.all_gather(gain_attn.astype(jnp.bfloat16), "seq", axis=0, tiled=True),
        lax.all_gather(bias_attn.astype(jnp.bfloat16), "seq", axis=0, tiled=True),
        lax.all_gather(gain_ffn.astype(jnp.bfloat16), "seq", axis=0, tiled=True),
        lax.all_gather(bias_ffn.astype(jnp.bfloat16), "seq", axis=0, tiled=True),
        lax.all_gather(w_up.astype(jnp.bfloat16), "seq", axis=0, tiled=True),
        lax.all_gather(bias_up.astype(jnp.bfloat16), "seq", axis=0, tiled=True),
        lax.all_gather(w_down.astype(jnp.bfloat16), "seq", axis=0, tiled=True),
        lax.all_gather(bias_down.astype(jnp.bfloat16), "seq", axis=0, tiled=True),
    )
    m_qk, m_value, m_out, g_attn, b_attn, g_ffn, b_ffn, m_up, b_up, m_down, b_down = gathered
    gain_one = g_attn.astype(jnp.float32)
    gain_two = g_ffn.astype(jnp.float32)
    doc_ends = jnp.cumsum(lengths)
    send_list = [send_slots(inverse[turn], tokens, devices, capacity) for turn in range(ROUNDS)]
    recv_list = [recv_slots(sort_order[turn], tokens, capacity) for turn in range(ROUNDS)]
    before_ids = shifted(sort_order[:, tokens - SPAN :], "seq", 1)
    normed_one, hat_one, inv_one = layer_norm(x_second, gain_one, b_attn.astype(jnp.float32))
    normed_one = normed_one.astype(jnp.bfloat16)
    qk_rows = linear(normed_one, m_qk).astype(jnp.bfloat16)
    value_rows = linear(normed_one, m_value).astype(jnp.bfloat16)
    stashed = []
    round_outs = []
    round_lse = []
    for turn in range(ROUNDS):
        got_qk, got_value = (
            lax.all_to_all(
                packed(qk_rows, send_list[turn], devices, capacity),
                "seq",
                split_axis=0,
                concat_axis=0,
                tiled=True,
            ),
            lax.all_to_all(
                packed(value_rows, send_list[turn], devices, capacity),
                "seq",
                split_axis=0,
                concat_axis=0,
                tiled=True,
            ),
        )
        sorted_qk, sorted_value, last_block = arrange(got_qk, got_value, recv_list[turn])
        before_block = shifted(last_block, "seq", 1)
        sorted_rows = (sorted_qk, sorted_value, before_block[0], before_block[1])
        pieces = score_parts(sorted_rows, sort_order[turn], before_ids[turn], doc_ends)
        out_sorted, lse_sorted = attend_out(pieces)
        back_out, back_lse = (
            lax.all_to_all(
                packed(out_sorted, recv_list[turn], devices, capacity),
                "seq",
                split_axis=0,
                concat_axis=0,
                tiled=True,
            ),
            lax.all_to_all(
                packed(lse_sorted, recv_list[turn], devices, capacity),
                "seq",
                split_axis=0,
                concat_axis=0,
                tiled=True,
            ),
        )
        round_outs.append(unpacked(back_out, send_list[turn]))
        round_lse.append(unpacked(back_lse, send_list[turn]))
        stashed.append(sorted_rows)
    lse_all = jnp.stack(round_lse)
    out_all = jnp.stack(round_outs).reshape(ROUNDS, tokens, HEADS, HEAD_DIM)
    merge = jnp.exp(lse_all - jax.nn.logsumexp(lse_all, axis=0))
    mixed = jnp.sum(merge[..., None] * out_all, axis=0).reshape(tokens, -1).astype(jnp.bfloat16)
    y_first = x_first + linear(mixed, m_out)
    normed_two, hat_two, inv_two = layer_norm(y_first, gain_two, b_ffn.astype(jnp.float32))
    normed_two = normed_two.astype(jnp.bfloat16)
    pre_up = linear(normed_two, m_up) + b_up.astype(jnp.float32)
    hidden, gelu_back = jax.vjp(partial(jax.nn.gelu, approximate=True), pre_up)
    hidden = hidden.astype(jnp.bfloat16)
    y_second = x_second + (linear(hidden, m_down) + b_down.astype(jnp.float32))
    grad_f = dy_second.astype(jnp.bfloat16)
    grad_down = inner_rows(hidden, grad_f)
    grad_bias_down = jnp.sum(grad_f.astype(jnp.float32), axis=0)
    grad_pre = gelu_back(outer_cols(grad_f, m_down))[0].astype(jnp.bfloat16)
    grad_up = inner_rows(normed_two, grad_pre)
    grad_bias_up = jnp.sum(grad_pre.astype(jnp.float32), axis=0)
    grad_two = outer_cols(grad_pre, m_up)
    grad_gain_ffn = jnp.sum(grad_two * hat_two, axis=0)
    grad_bias_ffn = jnp.sum(grad_two, axis=0)
    dx_first = dy_first + norm_back(grad_two, hat_two, inv_two, gain_two)
    grad_attn = dx_first.astype(jnp.bfloat16)
    grad_out = inner_rows(mixed, grad_attn)
    grad_mixed = outer_cols(grad_attn, m_out).reshape(tokens, HEADS, HEAD_DIM)
    along = jnp.sum(grad_mixed[None] * out_all, axis=-1)
    grad_lse_all = merge * (along - jnp.sum(merge * along, axis=0, keepdims=True))
    grad_qk_sum = jnp.zeros((tokens, HEADS * HEAD_DIM), jnp.float32)
    grad_value_sum = jnp.zeros((tokens, HEADS * HEAD_DIM), jnp.float32)
    for turn in range(ROUNDS):
        grad_round = (merge[turn][..., None] * grad_mixed).reshape(tokens, -1)
        got_out, got_lse = (
            lax.all_to_all(
                packed(grad_round, send_list[turn], devices, capacity),
                "seq",
                split_axis=0,
                concat_axis=0,
                tiled=True,
            ),
            lax.all_to_all(
                packed(grad_lse_all[turn], send_list[turn], devices, capacity),
                "seq",
                split_axis=0,
                concat_axis=0,
                tiled=True,
            ),
        )
        sorted_grad_out = unpacked(got_out, recv_list[turn])
        sorted_grad_lse = unpacked(got_lse, recv_list[turn])
        sorted_rows = stashed[turn]
        pieces = score_parts(sorted_rows, sort_order[turn], before_ids[turn], doc_ends)
        grad_query, grad_key, grad_val = attend_back(pieces, sorted_grad_out, sorted_grad_lse)
        spill = shifted(
            jnp.stack([grad_key[0, :SPAN], grad_val[0, :SPAN]]).astype(jnp.bfloat16), "seq", -1
        ).astype(jnp.float32)
        key_add = jnp.concatenate([grad_key[1:, :SPAN], spill[0][None]], axis=0)
        value_add = jnp.concatenate([grad_val[1:, :SPAN], spill[1][None]], axis=0)
        sorted_grad_qk = (grad_query + grad_key[:, SPAN:] + key_add).reshape(tokens, -1)
        sorted_grad_value = (grad_val[:, SPAN:] + value_add).reshape(tokens, -1)
        back_qk, back_value = (
            lax.all_to_all(
                as_sent(packed(sorted_grad_qk, recv_list[turn], devices, capacity)),
                "seq",
                split_axis=0,
                concat_axis=0,
                tiled=True,
            ),
            lax.all_to_all(
                as_sent(packed(sorted_grad_value, recv_list[turn], devices, capacity)),
                "seq",
                split_axis=0,
                concat_axis=0,
                tiled=True,
            ),
        )
        grad_qk_sum = grad_qk_sum + unpacked(back_qk, send_list[turn])
        grad_value_sum = grad_value_sum + unpacked(back_value, send_list[turn])
    grad_qk_rows = grad_qk_sum.astype(jnp.bfloat16)
    grad_value_rows = grad_value_sum.astype(jnp.bfloat16)
    grad_qk = inner_rows(normed_one, grad_qk_rows)
    grad_value = inner_rows(normed_one, grad_value_rows)
    grad_one = outer_cols(grad_qk_rows, m_qk) + outer_cols(grad_value_rows, m_value)
    grad_gain_attn = jnp.sum(grad_one * hat_one, axis=0)
    grad_bias_attn = jnp.sum(grad_one, axis=0)
    dx_second = dy_second + norm_back(grad_one, hat_one, inv_one, gain_one)
    s_qk, s_value, s_out, s_gattn, s_battn, s_gffn, s_bffn, s_up, s_bup, s_down, s_bdown = (
        lax.psum_scatter(grad_qk, "seq", scatter_dimension=0, tiled=True),
        lax.psum_scatter(grad_value, "seq", scatter_dimension=0, tiled=True),
        lax.psum_scatter(grad_out, "seq", scatter_dimension=0, tiled=True),
        lax.psum_scatter(grad_gain_attn, "seq", scatter_dimension=0, tiled=True),
        lax.psum_scatter(grad_bias_attn, "seq", scatter_dimension=0, tiled=True),
        lax.psum_scatter(grad_gain_ffn, "seq", scatter_dimension=0, tiled=True),
        lax.psum_scatter(grad_bias_ffn, "seq", scatter_dimension=0, tiled=True),
        lax.psum_scatter(grad_up, "seq", scatter_dimension=0, tiled=True),
        lax.psum_scatter(grad_bias_up, "seq", scatter_dimension=0, tiled=True),
        lax.psum_scatter(grad_down, "seq", scatter_dimension=0, tiled=True),
        lax.psum_scatter(grad_bias_down, "seq", scatter_dimension=0, tiled=True),
    )
    return (
        y_first,
        y_second,
        dx_first,
        dx_second,
        s_qk,
        s_value,
        s_out,
        s_gattn,
        s_battn,
        s_gffn,
        s_bffn,
        s_up,
        s_bup,
        s_down,
        s_bdown,
    )


CAP_ROWS = 16
PARTS = 8


def dot_nn(a, b):
    return lax.dot_general(a, b, (((1,), (0,)), ((), ())), preferred_element_type=F32)


def dot_nt(a, b):
    return lax.dot_general(a, b, (((1,), (1,)), ((), ())), preferred_element_type=F32)


def dot_tn(a, b):
    return lax.dot_general(a, b, (((0,), (0,)), ((), ())), preferred_element_type=F32)


def hot_rows(slot_row, slots):
    ids = lax.broadcasted_iota(jnp.int32, (slots, slot_row.shape[1]), 0).astype(F32)
    return jnp.where(ids == slot_row, 1.0, 0.0).astype(BF)


def hot_cols(slot_col, slots):
    ids = lax.broadcasted_iota(jnp.int32, (slot_col.shape[0], slots), 1).astype(F32)
    return jnp.where(ids == slot_col, 1.0, 0.0).astype(BF)


def key_norm(keys):
    wide = keys.astype(F32)
    square = wide * wide
    high = square.astype(BF)
    low = (square - high.astype(F32)).astype(BF)
    ones = jnp.ones((8, keys.shape[1]), BF)
    return lax.rsqrt((dot_nt(ones, high) + dot_nt(ones, low))[0:1])


def span_softmax(raw, norm, key_ids, query_ids, query_starts):
    factor = norm * SCALE
    kept = (key_ids < query_ids) & (key_ids >= query_starts)
    score = jnp.where(
        key_ids == query_ids, -100000.0, jnp.where(kept, raw * factor, -1000000000.0)
    )
    top = jnp.max(score, axis=1, keepdims=True)
    weight = jnp.exp(score - top)
    total = jnp.sum(weight, axis=1, keepdims=True)
    return factor, kept, weight, top, total


def three_parts(wide):
    high = wide.astype(BF).astype(F32)
    rest = wide - high
    mid = rest.astype(BF).astype(F32)
    return high, mid, rest - mid


def forward_kernel(place, x_0, x_1, x_2, x_3, info, key_ids, out, kept_rows, lanes, heads_out):
    blocks, tokens = info.shape[0], info.shape[2]
    slots = blocks * CAP_ROWS
    width = x_0.shape[1]
    spans = tokens // SPAN
    turn = place[0]
    rounds = ROUNDS

    for offset, rows in enumerate((x_0, x_1, x_2, x_3)):

        def pack(group, carry, offset=offset, rows=rows):
            source = group * rounds + lax.bitwise_xor(turn, offset)
            hot = hot_rows(info[source, 3:4, :], slots)
            start = pl.multiple_of(group * tokens, tokens)
            part = dot_nn(hot, rows[pl.ds(start, tokens), :]).astype(BF)
            lanes[:, pl.ds(source, 1)] = part.reshape(blocks, 1, CAP_ROWS, width)
            return carry

        lax.fori_loop(0, blocks // rounds, pack, 0, unroll=4)

    def place_rows(block, carry):
        cols = jnp.transpose(info[block])
        hot = hot_cols(cols[:, 2:3], slots)
        part = dot_nn(hot, lanes[block].reshape(slots, width)).astype(BF)
        start = pl.multiple_of(SPAN + block * tokens, SPAN)
        kept_rows[pl.ds(start, tokens), :] = part
        return carry

    lax.fori_loop(0, blocks, place_rows, 0, unroll=4)
    kept_rows[0:SPAN, :] = kept_rows[blocks * tokens : blocks * tokens + SPAN, :]

    def attend(block, carry):
        cols = jnp.transpose(info[block])
        lane = lax.broadcasted_iota(jnp.int32, (SPAN, width - HEAD_DIM), 1)
        first = []
        for part in range(spans):
            span = block * spans + part
            start = pl.multiple_of(span * SPAN, SPAN)
            rows = kept_rows[pl.ds(start, 2 * SPAN), :]
            keys = rows[:, :HEAD_DIM]
            first.append((rows, dot_nt(rows[SPAN:, :HEAD_DIM], keys), key_norm(keys)))
        second = []
        for part in range(spans):
            rows, raw, norm = first[part]
            ids = cols[part * SPAN : (part + 1) * SPAN]
            factor, kept, weight, top, total = span_softmax(
                raw, norm, key_ids[pl.ds(block * spans + part, 1), :], ids[:, 0:1], ids[:, 1:2]
            )
            high, mid, low = three_parts(top + jnp.log(total))
            extra = jnp.where(
                lane == 0, high, jnp.where(lane == 1, mid, jnp.where(lane == 2, low, 0.0))
            ).astype(BF)
            second.append(((weight * (1.0 / total)).astype(BF), extra))
        for part in range(spans):
            probs, extra = second[part]
            here = slice(part * SPAN, (part + 1) * SPAN)
            heads_out[block, here, :HEAD_DIM] = dot_nn(probs, first[part][0][:, HEAD_DIM:]).astype(BF)
            heads_out[block, here, HEAD_DIM:] = extra
        return carry

    lax.fori_loop(0, blocks, attend, 0)

    def unplace(block, carry):
        hot = hot_rows(info[block, 2:3, :], slots)
        part = dot_nn(hot, heads_out[block]).astype(BF)
        lanes[:, pl.ds(block, 1)] = part.reshape(blocks, 1, CAP_ROWS, width)
        return carry

    lax.fori_loop(0, blocks, unplace, 0, unroll=4)

    def unpack(source, carry):
        cols = jnp.transpose(info[source])
        hot = hot_cols(cols[:, 3:4], slots)
        part = dot_nn(hot, lanes[source].reshape(slots, width))
        out[source, 0:tokens, :] = part[:, :HEAD_DIM].astype(BF)
        flat = jnp.transpose(part[:, HEAD_DIM:])[0:PARTS, :].astype(BF)
        for piece in range(tokens // HEAD_DIM):
            first = tokens + piece * PARTS
            out[source, first : first + PARTS, :] = flat[
                :, piece * HEAD_DIM : (piece + 1) * HEAD_DIM
            ]
        return carry

    lax.fori_loop(0, blocks, unpack, 0, unroll=4)


def backward_kernel(place, grads, kept_rows, info, key_ids, out_0, out_1, out_2, out_3, lanes, sums):
    blocks, tokens = info.shape[0], info.shape[2]
    slots = blocks * CAP_ROWS
    width = kept_rows.shape[1]
    spans = tokens // SPAN

    def pack(source, carry):
        hot = hot_rows(info[source, 3:4, :], slots)
        flat = jnp.concatenate(
            [
                grads[source, tokens + piece * PARTS : tokens + (piece + 1) * PARTS, :].astype(F32)
                for piece in range(tokens // HEAD_DIM)
            ],
            axis=1,
        )
        tall = jnp.concatenate([flat, jnp.zeros((HEAD_DIM - PARTS, tokens), F32)], axis=0)
        rows = jnp.concatenate(
            [grads[source, 0:tokens, :], jnp.transpose(tall).astype(BF)], axis=1
        )
        part = dot_nn(hot, rows).astype(BF)
        lanes[:, pl.ds(source, 1)] = part.reshape(blocks, 1, CAP_ROWS, width)
        return carry

    lax.fori_loop(0, blocks, pack, 0, unroll=4)
    sums[0:SPAN, :] = jnp.zeros((SPAN, width), F32)

    def attend(block, carry):
        cols = jnp.transpose(info[block])
        hot = hot_cols(cols[:, 2:3], slots)
        part_grads = dot_nn(hot, lanes[block].reshape(slots, width))
        grad_rows = part_grads[:, :HEAD_DIM].astype(BF)
        grad_lse = (
            part_grads[:, HEAD_DIM : HEAD_DIM + 1]
            + part_grads[:, HEAD_DIM + 1 : HEAD_DIM + 2]
            + part_grads[:, HEAD_DIM + 2 : HEAD_DIM + 3]
        )
        first = []
        for part in range(spans):
            span = block * spans + part
            start = pl.multiple_of(span * SPAN, SPAN)
            rows = kept_rows[pl.ds(start, 2 * SPAN), :]
            keys = rows[:, :HEAD_DIM]
            queries = rows[SPAN:, :HEAD_DIM]
            grad_out = grad_rows[part * SPAN : (part + 1) * SPAN]
            raw = dot_nt(queries, keys)
            grad_prob = dot_nt(grad_out, rows[:, HEAD_DIM:])
            first.append((start, keys, queries, grad_out, raw, grad_prob, key_norm(keys)))
        second = []
        slopes = []
        for part in range(spans):
            start, keys, queries, grad_out, raw, grad_prob, norm = first[part]
            here = slice(part * SPAN, (part + 1) * SPAN)
            ids = cols[here]
            factor, kept, weight, top, total = span_softmax(
                raw, norm, key_ids[pl.ds(block * spans + part, 1), :], ids[:, 0:1], ids[:, 1:2]
            )
            probs = weight * (1.0 / total)
            row_dot = jnp.sum(probs * grad_prob, axis=1, keepdims=True)
            grad_score = jnp.where(kept, probs * (grad_prob - row_dot + grad_lse[here]), 0.0)
            slopes.append(
                jnp.sum(grad_score * raw, axis=0, keepdims=True) * SCALE * norm * norm * norm
            )
            second.append(((grad_score * factor).astype(BF), probs.astype(BF)))
        held = []
        for part in range(spans):
            start, keys, queries, grad_out = first[part][:4]
            grad_raw, probs = second[part]
            held.append(
                (
                    start,
                    keys,
                    dot_nn(grad_raw, keys),
                    dot_tn(grad_raw, queries),
                    dot_tn(probs, grad_out),
                )
            )
        slopes.append(jnp.zeros((8 - spans, 2 * SPAN), F32))
        slope_cols = jnp.transpose(jnp.concatenate(slopes, axis=0))
        for part in range(spans):
            start, keys, grad_query, grad_key, grad_val = held[part]
            grad_key = grad_key - slope_cols[:, part : part + 1] * keys.astype(F32)
            sums[pl.ds(start, SPAN), :] += jnp.concatenate(
                [grad_key[:SPAN], grad_val[:SPAN]], axis=1
            )
            after = pl.multiple_of(start + SPAN, SPAN)
            sums[pl.ds(after, SPAN), :] = jnp.concatenate(
                [grad_query + grad_key[SPAN:], grad_val[SPAN:]], axis=1
            )
        return carry

    lax.fori_loop(0, blocks, attend, 0)
    sums[blocks * tokens : blocks * tokens + SPAN, :] += sums[0:SPAN, :]

    def unplace(block, carry):
        hot = hot_rows(info[block, 2:3, :], slots)
        start = pl.multiple_of(SPAN + block * tokens, SPAN)
        part = dot_nn(hot, sums[pl.ds(start, tokens), :].astype(BF)).astype(BF)
        lanes[:, pl.ds(block, 1)] = part.reshape(blocks, 1, CAP_ROWS, width)
        return carry

    lax.fori_loop(0, blocks, unplace, 0, unroll=4)

    for offset, out in enumerate((out_0, out_1, out_2, out_3)):

        def unpack(group, carry, offset=offset, out=out):
            source = group * ROUNDS + lax.bitwise_xor(place[0], offset)
            cols = jnp.transpose(info[source])
            hot = hot_cols(cols[:, 3:4], slots)
            start = pl.multiple_of(group * tokens, tokens)
            part = dot_nn(hot, lanes[source].reshape(slots, width))
            out[pl.ds(start, tokens), :] = part.astype(BF)
            return carry

        lax.fori_loop(0, blocks // ROUNDS, unpack, 0, unroll=4)


def in_vmem(count):
    return [pl.BlockSpec(memory_space=pltpu.VMEM)] * count


def run_forward(turn, rows, info, key_ids):
    blocks, _, tokens = info.shape
    width = rows[0].shape[1]
    positions = blocks * tokens
    extra = PARTS * tokens // HEAD_DIM
    return pl.pallas_call(
        forward_kernel,
        out_shape=(
            jax.ShapeDtypeStruct((blocks, tokens + extra, HEAD_DIM), BF),
            jax.ShapeDtypeStruct((SPAN + positions, width), BF),
        ),
        in_specs=[pl.BlockSpec(memory_space=pltpu.SMEM)] + in_vmem(6),
        out_specs=tuple(in_vmem(2)),
        scratch_shapes=[
            pltpu.VMEM((blocks, blocks, CAP_ROWS, width), BF),
            pltpu.VMEM((blocks, tokens, width), BF),
        ],
        compiler_params=pltpu.CompilerParams(vmem_limit_bytes=48 << 20),
        cost_estimate=pl.CostEstimate(
            flops=20 * 10**9, bytes_accessed=12 * 10**6, transcendentals=10**6
        ),
        name="hash_forward",
    )(turn, *rows, info, key_ids)


def run_backward(turn, grads, kept_rows, info, key_ids):
    blocks, _, tokens = info.shape
    width = kept_rows.shape[1]
    positions = blocks * tokens
    return pl.pallas_call(
        backward_kernel,
        out_shape=(jax.ShapeDtypeStruct((positions // ROUNDS, width), BF),) * ROUNDS,
        in_specs=[pl.BlockSpec(memory_space=pltpu.SMEM)] + in_vmem(4),
        out_specs=tuple(in_vmem(ROUNDS)),
        scratch_shapes=[
            pltpu.VMEM((blocks, blocks, CAP_ROWS, width), BF),
            pltpu.VMEM((SPAN + positions, width), F32),
        ],
        compiler_params=pltpu.CompilerParams(vmem_limit_bytes=48 << 20),
        cost_estimate=pl.CostEstimate(
            flops=20 * 10**9, bytes_accessed=12 * 10**6, transcendentals=10**6
        ),
        name="hash_backward",
    )(turn, grads, kept_rows, info, key_ids)


def peers(mask):
    size = HEADS * ROUNDS
    return [(i, i ^ mask) for i in range(size)]


def swap(x, mask):
    return lax.ppermute(x, "seq", peers(mask))


def columns():
    return [[head * ROUNDS + turn for head in range(HEADS)] for turn in range(ROUNDS)]


def rows_of():
    return [[head * ROUNDS + turn for turn in range(ROUNDS)] for head in range(HEADS)]


def gather_group(x):
    side = swap(x, 2)
    return (x, swap(x, 1), side, swap(side, 1))


def sum_group(parts):
    near = parts[0] + swap(parts[1].astype(BF), 1).astype(F32)
    far = parts[2] + swap(parts[3].astype(BF), 1).astype(F32)
    return near + swap(far.astype(BF), 2).astype(F32)


def exchange(x, groups=None):
    return lax.all_to_all(
        x, "seq", split_axis=0, concat_axis=0, tiled=True, axis_index_groups=groups
    )


def rounded(x):
    return lax.reduce_precision(x, 8, 7)


def split_three(wide):
    high = rounded(wide)
    rest = wide - high
    mid = rounded(rest)
    return jnp.stack([high, mid, rest - mid])


def slots_sent(target, tokens, capacity):
    device = target // tokens
    early = jnp.arange(tokens)[None, :] < jnp.arange(tokens)[:, None]
    same = (device[:, None] == device[None, :]) & early
    return device * capacity + jnp.sum(same.astype(jnp.int32), axis=1)


def start_of(token_ids, doc_ends):
    ends = doc_ends[None, :]
    return jnp.max(jnp.where(ends <= token_ids[:, None], ends, 0), axis=1)


def shards_fast(
    x_first,
    x_second,
    w_qk,
    w_value,
    w_out,
    gain_attn,
    bias_attn,
    gain_ffn,
    bias_ffn,
    w_up,
    bias_up,
    w_down,
    bias_down,
    sort_order,
    inverse,
    lengths,
    dy_first,
    dy_second,
):
    devices = lax.axis_size("seq")
    tokens, features = x_first.shape
    capacity = 2 * tokens // devices
    shard = features // devices
    place = lax.axis_index("seq")
    doc_ends = jnp.cumsum(lengths)

    per_round = []
    vectors = rounded(
        jnp.concatenate([gain_attn, bias_attn, gain_ffn, bias_ffn, bias_up, bias_down])
    )
    vectors = jnp.pad(vectors, (0, 2 * tokens - vectors.shape[0])).reshape(2, tokens)
    for turn in range(ROUNDS):
        ids = sort_order[turn]
        rows = jnp.stack(
            [
                ids,
                start_of(ids, doc_ends),
                recv_slots(ids, tokens, capacity),
                slots_sent(inverse[turn], tokens, capacity),
            ]
        ).astype(F32)
        per_round.append(jnp.concatenate([rows, vectors, jnp.zeros((2, tokens), F32)]))
    info = jnp.tile(jnp.stack(per_round), (HEADS, 1, 1))
    info = exchange(info)
    got = info[:, 4:6].reshape(devices, 2 * tokens)

    def vector(first, size):
        return got[:, first : first + size].reshape(devices * size)

    gain_one, shift_one = vector(0, shard), vector(shard, shard)
    gain_two, shift_two = vector(2 * shard, shard), vector(3 * shard, shard)
    wide = bias_up.shape[0]
    b_up = vector(4 * shard, wide)
    b_down = vector(4 * shard + wide, shard)
    spans = info[:, 0].reshape(devices * tokens // SPAN, SPAN)
    key_ids = jnp.concatenate([jnp.roll(spans, 1, axis=0), spans], axis=1)

    pair = jnp.stack(
        [w_qk.reshape(shard, HEADS, HEAD_DIM), w_value.reshape(shard, HEADS, HEAD_DIM)], axis=2
    ).reshape(shard, 2 * features)
    m_pair = lax.all_gather(pair.astype(BF), "seq", axis=0, tiled=True)
    m_out = lax.all_gather(w_out.astype(BF), "seq", axis=0, tiled=True)
    up_cols = jnp.transpose(
        w_up.astype(BF).reshape(shard, HEADS, ROUNDS, wide), (2, 0, 1, 3)
    ).reshape(ROUNDS, shard, HEADS * wide)
    up_cols = exchange(up_cols, rows_of()).reshape(ROUNDS * shard, HEADS * wide)
    m_ffn = lax.all_gather(
        jnp.concatenate([up_cols, w_down.astype(BF)], axis=1),
        "seq",
        axis=0,
        tiled=True,
        axis_index_groups=columns(),
    )
    m_up, m_down = m_ffn[:, : HEADS * wide], m_ffn[:, HEADS * wide :]
    b_up = lax.dynamic_index_in_dim(
        b_up.reshape(HEADS, ROUNDS, wide), place % ROUNDS, axis=1, keepdims=False
    ).reshape(HEADS * wide)

    normed_one, hat_one, inv_one = layer_norm(x_second, gain_one, shift_one)
    normed_one = normed_one.astype(BF)
    rows = linear(normed_one, m_pair).astype(BF)
    rows = jnp.transpose(rows.reshape(tokens, HEADS, 2 * HEAD_DIM), (1, 0, 2))
    own = exchange(rows, columns()).reshape(HEADS * tokens, 2 * HEAD_DIM)
    all_rows = gather_group(own)
    normed_col = lax.all_gather(
        normed_one, "seq", axis=0, tiled=True, axis_index_groups=columns()
    )
    turn = (place % ROUNDS).astype(jnp.int32).reshape(1)
    sent, kept_rows = run_forward(turn, all_rows, info, key_ids)
    back = exchange(sent).reshape(HEADS, ROUNDS, -1, HEAD_DIM)
    out_all = jnp.transpose(back[:, :, :tokens], (1, 2, 0, 3)).astype(F32)
    pieces = back[:, :, tokens:].reshape(HEADS, ROUNDS, -1, PARTS, HEAD_DIM)[:, :, :, :3]
    lse_all = jnp.sum(pieces.astype(F32), axis=3).reshape(HEADS, ROUNDS, tokens)
    lse_all = jnp.transpose(lse_all, (1, 2, 0))

    merge = jnp.exp(lse_all - jax.nn.logsumexp(lse_all, axis=0))
    mixed = jnp.sum(merge[..., None] * out_all, axis=0).reshape(tokens, -1).astype(BF)
    y_first = x_first + linear(mixed, m_out)
    normed_two, hat_two, inv_two = layer_norm(y_first, gain_two, shift_two)
    normed_two = normed_two.astype(BF)
    grad_f = dy_second.astype(BF)
    grad_f_all = jnp.concatenate(gather_group(grad_f))
    normed_all = jnp.concatenate(gather_group(normed_two))
    pre_up = linear(normed_all, m_up) + b_up
    hidden, gelu_back = jax.vjp(partial(jax.nn.gelu, approximate=True), pre_up)
    hidden = hidden.astype(BF)
    branch = sum_group(linear(hidden, m_down).reshape(ROUNDS, tokens, features))
    y_second = x_second + (branch + b_down)
    grad_down = inner_rows(hidden, grad_f_all)
    grad_bias_down = jnp.sum(grad_f.astype(F32), axis=0)
    grad_pre = gelu_back(outer_cols(grad_f_all, m_down))[0].astype(BF)
    grad_up = inner_rows(normed_all, grad_pre)
    grad_bias_up = jnp.sum(grad_pre.astype(F32), axis=0)
    grad_two = sum_group(outer_cols(grad_pre, m_up).reshape(ROUNDS, tokens, features))
    grad_gain_ffn = jnp.sum(grad_two * hat_two, axis=0)
    grad_bias_ffn = jnp.sum(grad_two, axis=0)
    dx_first = dy_first + norm_back(grad_two, hat_two, inv_two, gain_two)
    grad_attn = dx_first.astype(BF)
    grad_out = inner_rows(mixed, grad_attn)
    fourth = features // ROUNDS
    grad_out = sum_group(
        [
            lax.dynamic_slice_in_dim(grad_out, ((place % ROUNDS) ^ near) * fourth, fourth, axis=1)
            for near in range(ROUNDS)
        ]
    )
    merged = jnp.concatenate([x.astype(BF) for x in (grad_up, grad_out, grad_down)], axis=1)
    merged = lax.psum_scatter(
        merged, "seq", scatter_dimension=0, tiled=True, axis_index_groups=columns()
    )
    half = HEADS * wide
    s_down = merged[:, half + fourth :].astype(F32)
    merged = exchange(merged[:, : half + fourth].reshape(ROUNDS, shard, -1), rows_of())
    s_up = jnp.transpose(merged[:, :, :half].reshape(ROUNDS, shard, HEADS, wide), (1, 2, 0, 3))
    s_up = s_up.reshape(shard, ROUNDS * half).astype(F32)
    s_out = jnp.transpose(merged[:, :, half:], (1, 0, 2)).reshape(shard, features).astype(F32)
    grad_mixed = outer_cols(grad_attn, m_out).reshape(tokens, HEADS, HEAD_DIM)
    along = jnp.sum(grad_mixed[None] * out_all, axis=-1)
    grad_lse_all = merge * (along - jnp.sum(merge * along, axis=0, keepdims=True))

    grad_round = (merge[..., None] * grad_mixed[None]).astype(BF)
    grad_round = jnp.transpose(grad_round, (2, 0, 1, 3)).reshape(devices, tokens, HEAD_DIM)
    parts = split_three(jnp.transpose(grad_lse_all, (2, 0, 1)).reshape(devices, tokens))
    parts = jnp.pad(parts, ((0, PARTS - 3), (0, 0), (0, 0)))
    parts = jnp.transpose(parts.reshape(PARTS, devices, -1, HEAD_DIM), (1, 2, 0, 3))
    parts = parts.reshape(devices, -1, HEAD_DIM).astype(BF)
    got_grads = exchange(jnp.concatenate([grad_round, parts], axis=1))
    grad_head = run_backward(turn, got_grads, kept_rows, info, key_ids)
    grad_head = sum_group([x.astype(F32) for x in grad_head]).astype(BF)
    grad_rows = exchange(grad_head.reshape(HEADS, tokens, 2 * HEAD_DIM), columns())
    grad_rows = jnp.transpose(grad_rows, (1, 0, 2)).reshape(tokens, 2 * features)

    s_pair = exchange(
        inner_rows(normed_col, grad_head).astype(BF).reshape(devices, shard, 2 * HEAD_DIM)
    )
    s_pair = jnp.sum(
        s_pair.reshape(HEADS, ROUNDS, shard, 2, HEAD_DIM).astype(F32), axis=1
    ).transpose(2, 1, 0, 3)
    s_qk = s_pair[0].reshape(shard, features)
    s_value = s_pair[1].reshape(shard, features)
    grad_one = outer_cols(grad_rows, m_pair)
    grad_gain_attn = jnp.sum(grad_one * hat_one, axis=0)
    grad_bias_attn = jnp.sum(grad_one, axis=0)
    dx_second = dy_second + norm_back(grad_one, hat_one, inv_one, gain_one)

    is_mine = (jnp.arange(ROUNDS) == place % ROUNDS).astype(F32)
    grad_bias_up = grad_bias_up.reshape(HEADS, 1, wide) * is_mine[None, :, None]
    small = jnp.concatenate(
        [
            grad_gain_attn.reshape(devices, -1),
            grad_bias_attn.reshape(devices, -1),
            grad_gain_ffn.reshape(devices, -1),
            grad_bias_ffn.reshape(devices, -1),
            grad_bias_up.reshape(devices, -1),
            grad_bias_down.reshape(devices, -1),
        ],
        axis=1,
    )
    small = jnp.sum(exchange(small[:, None]), axis=(0, 1))
    s_gattn, s_battn, s_gffn, s_bffn = (small[i * shard : (i + 1) * shard] for i in range(4))
    s_bup = small[4 * shard : 4 * shard + wide]
    s_bdown = small[4 * shard + wide :]
    return (
        y_first,
        y_second,
        dx_first,
        dx_second,
        s_qk,
        s_value,
        s_out,
        s_gattn,
        s_battn,
        s_gffn,
        s_bffn,
        s_up,
        s_bup,
        s_down,
        s_bdown,
    )


def solution(mesh):
    in_specs = (
        P("seq", None),
        P("seq", None),
        P("seq", None),
        P("seq", None),
        P("seq", None),
        P("seq"),
        P("seq"),
        P("seq"),
        P("seq"),
        P("seq", None),
        P("seq"),
        P("seq", None),
        P("seq"),
        P(None, "seq"),
        P(None, "seq"),
        P(),
        P("seq", None),
        P("seq", None),
    )
    out_specs = (
        P("seq", None),
        P("seq", None),
        P("seq", None),
        P("seq", None),
        P("seq", None),
        P("seq", None),
        P("seq", None),
        P("seq"),
        P("seq"),
        P("seq"),
        P("seq"),
        P("seq", None),
        P("seq"),
        P("seq", None),
        P("seq"),
    )
    fast = mesh.shape["seq"] == HEADS * ROUNDS
    return jax.shard_map(shards_fast if fast else shards, mesh=mesh, in_specs=in_specs, out_specs=out_specs, check_vma=False)
```

```python
from functools import partial
import math

import jax
import jax.numpy as jnp
from jax import lax
from jax.experimental import pallas as pl
from jax.experimental.pallas import tpu as pltpu
from jax.sharding import PartitionSpec as P

HEADS = 8
HEAD_DIM = 128
SPAN = 64
ROUNDS = 4

EPSILON = 1e-05
SCALE = 1.0 / math.sqrt(HEAD_DIM)
BF = jnp.bfloat16
F32 = jnp.float32


def shifted(x, axis, by):
    size = lax.axis_size(axis)
    return lax.ppermute(x, axis, [(i, (i + by) % size) for i in range(size)])


def as_sent(x):
    return jax.tree.map(lambda a: a.astype(jnp.bfloat16) if a.dtype == jnp.float32 else a, x)


def layer_norm(inputs, norm_gain, norm_shift):
    centered = inputs - jnp.mean(inputs, axis=-1, keepdims=True)
    inv_std = lax.rsqrt(jnp.mean(centered * centered, axis=-1, keepdims=True) + EPSILON)
    normed = centered * inv_std
    return (normed * norm_gain + norm_shift, normed, inv_std)


def norm_back(grad_rows, normed, inv_std, norm_gain):
    grad_hat = grad_rows * norm_gain
    return inv_std * (
        grad_hat
        - jnp.mean(grad_hat, axis=-1, keepdims=True)
        - normed * jnp.mean(grad_hat * normed, axis=-1, keepdims=True)
    )


def linear(matrix_a, matrix_b):
    return jnp.dot(matrix_a, matrix_b, preferred_element_type=jnp.float32)


def inner_rows(matrix_a, matrix_b):
    return lax.dot_general(
        matrix_a, matrix_b, (((0,), (0,)), ((), ())), preferred_element_type=jnp.float32
    )


def outer_cols(matrix_a, matrix_b):
    return lax.dot_general(
        matrix_a, matrix_b, (((1,), (1,)), ((), ())), preferred_element_type=jnp.float32
    )


def segment_of(token_ids, doc_ends):
    return jnp.sum((token_ids[:, None] >= doc_ends[None, :]).astype(jnp.int32), axis=1)


def send_slots(target, tokens, devices, capacity):
    device = target // tokens
    onehot = (device[:, None] == jnp.arange(devices, dtype=jnp.int32)[None, :]).astype(jnp.int32)
    rank_in = jnp.sum(jnp.cumsum(onehot, axis=0) * onehot, axis=1) - 1
    return device * capacity + rank_in


def recv_slots(source_ids, tokens, capacity):
    device = source_ids // tokens
    earlier = (device[:, None] == device[None, :]) & (source_ids[None, :] < source_ids[:, None])
    return device * capacity + jnp.sum(earlier.astype(jnp.int32), axis=1)


def packed(inputs, slot_ids, devices, capacity):
    filled = (
        jnp.zeros((devices * capacity,) + inputs.shape[1:], inputs.dtype).at[slot_ids].set(inputs)
    )
    return filled.reshape((devices, capacity) + inputs.shape[1:])


def unpacked(received, slot_ids):
    return received.reshape((-1,) + received.shape[2:])[slot_ids]


def spanned(inputs, before):
    blocks = inputs.shape[0] // SPAN
    current = inputs.reshape((blocks, SPAN) + inputs.shape[1:])
    earlier = jnp.concatenate([before[None], current[:-1]], axis=0)
    return (current, jnp.concatenate([earlier, current], axis=1))


def arrange(got_qk, got_value, recv_slot):
    sorted_qk = unpacked(got_qk, recv_slot)
    sorted_value = unpacked(got_value, recv_slot)
    last_block = jnp.stack([sorted_qk[-SPAN:], sorted_value[-SPAN:]])
    return (sorted_qk, sorted_value, last_block)


def score_parts(sorted_rows, query_ids, before_ids, doc_ends):
    sorted_qk, sorted_value, before_qk, before_value = sorted_rows
    current, key_rows = spanned(sorted_qk, before_qk)
    _, value_keys = spanned(sorted_value, before_value)
    current_ids, key_ids = spanned(query_ids, before_ids)
    current_seg, key_seg = spanned(
        segment_of(query_ids, doc_ends), segment_of(before_ids, doc_ends)
    )
    blocks = current.shape[0]
    q_heads = current.reshape(blocks, SPAN, HEADS, HEAD_DIM)
    k_heads = key_rows.reshape(blocks, 2 * SPAN, HEADS, HEAD_DIM)
    v_heads = value_keys.reshape(blocks, 2 * SPAN, HEADS, HEAD_DIM)
    raw_dots = jnp.einsum("gihd,gjhd->ghij", q_heads, k_heads, preferred_element_type=jnp.float32)
    k_float = k_heads.astype(jnp.float32)
    key_norm = lax.rsqrt(jnp.sum(k_float * k_float, axis=-1))
    factor = jnp.transpose(key_norm, (0, 2, 1))[:, :, None, :] / math.sqrt(HEAD_DIM)
    allowed = (
        (key_ids[:, None, :] <= current_ids[:, :, None])
        & (key_seg[:, None, :] == current_seg[:, :, None])
    )[:, None]
    itself = (key_ids[:, None, :] == current_ids[:, :, None])[:, None]
    scores = jnp.where(itself, -100000.0, jnp.where(allowed, raw_dots * factor, -1000000000.0))
    log_total = jax.nn.logsumexp(scores, axis=-1)
    attn_probs = jnp.exp(scores - log_total[..., None])
    kept_mask = allowed & jnp.logical_not(itself)
    return (
        q_heads,
        k_heads,
        v_heads,
        k_float,
        key_norm,
        factor,
        kept_mask,
        raw_dots,
        attn_probs,
        log_total,
    )


def attend_out(pieces):
    (
        q_heads,
        k_heads,
        v_heads,
        k_float,
        key_norm,
        factor,
        kept_mask,
        raw_dots,
        attn_probs,
        log_total,
    ) = pieces
    blocks = q_heads.shape[0]
    out_heads = jnp.einsum(
        "ghij,gjhd->gihd",
        attn_probs.astype(jnp.bfloat16),
        v_heads,
        preferred_element_type=jnp.float32,
    )
    return (
        out_heads.reshape(blocks * SPAN, -1),
        jnp.transpose(log_total, (0, 2, 1)).reshape(blocks * SPAN, HEADS),
    )


def attend_back(pieces, grad_rows, grad_total):
    (
        q_heads,
        k_heads,
        v_heads,
        k_float,
        key_norm,
        factor,
        kept_mask,
        raw_dots,
        attn_probs,
        log_total,
    ) = pieces
    blocks = q_heads.shape[0]
    grad_heads = grad_rows.astype(jnp.bfloat16).reshape(blocks, SPAN, HEADS, HEAD_DIM)
    grad_lse = jnp.transpose(grad_total.reshape(blocks, SPAN, HEADS), (0, 2, 1))
    grad_prob = jnp.einsum(
        "gihd,gjhd->ghij", grad_heads, v_heads, preferred_element_type=jnp.float32
    )
    grad_val = jnp.einsum(
        "ghij,gihd->gjhd",
        attn_probs.astype(jnp.bfloat16),
        grad_heads,
        preferred_element_type=jnp.float32,
    )
    row_dot = jnp.sum(attn_probs * grad_prob, axis=-1, keepdims=True)
    grad_score = jnp.where(kept_mask, attn_probs * (grad_prob - row_dot + grad_lse[..., None]), 0.0)
    grad_raw = (grad_score * factor).astype(jnp.bfloat16)
    grad_norm = jnp.transpose(jnp.sum(grad_score * raw_dots, axis=2), (0, 2, 1)) / math.sqrt(
        HEAD_DIM
    )
    norm_cube = key_norm * key_norm * key_norm
    grad_query = jnp.einsum(
        "ghij,gjhd->gihd", grad_raw, k_heads, preferred_element_type=jnp.float32
    )
    grad_key = (
        jnp.einsum("ghij,gihd->gjhd", grad_raw, q_heads, preferred_element_type=jnp.float32)
        - (grad_norm * norm_cube)[..., None] * k_float
    )
    return (
        grad_query.reshape(blocks, SPAN, -1),
        grad_key.reshape(blocks, 2 * SPAN, -1),
        grad_val.reshape(blocks, 2 * SPAN, -1),
    )


def shards(
    x_first,
    x_second,
    w_qk,
    w_value,
    w_out,
    gain_attn,
    bias_attn,
    gain_ffn,
    bias_ffn,
    w_up,
    bias_up,
    w_down,
    bias_down,
    sort_order,
    inverse,
    lengths,
    dy_first,
    dy_second,
):
    devices = lax.axis_size("seq")
    tokens = x_first.shape[0]
    capacity = 2 * tokens // devices
    gathered = (
        lax.all_gather(w_qk.astype(jnp.bfloat16), "seq", axis=0, tiled=True),
        lax.all_gather(w_value.astype(jnp.bfloat16), "seq", axis=0, tiled=True),
        lax.all_gather(w_out.astype(jnp.bfloat16), "seq", axis=0, tiled=True),
        lax.all_gather(gain_attn.astype(jnp.bfloat16), "seq", axis=0, tiled=True),
        lax.all_gather(bias_attn.astype(jnp.bfloat16), "seq", axis=0, tiled=True),
        lax.all_gather(gain_ffn.astype(jnp.bfloat16), "seq", axis=0, tiled=True),
        lax.all_gather(bias_ffn.astype(jnp.bfloat16), "seq", axis=0, tiled=True),
        lax.all_gather(w_up.astype(jnp.bfloat16), "seq", axis=0, tiled=True),
        lax.all_gather(bias_up.astype(jnp.bfloat16), "seq", axis=0, tiled=True),
        lax.all_gather(w_down.astype(jnp.bfloat16), "seq", axis=0, tiled=True),
        lax.all_gather(bias_down.astype(jnp.bfloat16), "seq", axis=0, tiled=True),
    )
    m_qk, m_value, m_out, g_attn, b_attn, g_ffn, b_ffn, m_up, b_up, m_down, b_down = gathered
    gain_one = g_attn.astype(jnp.float32)
    gain_two = g_ffn.astype(jnp.float32)
    doc_ends = jnp.cumsum(lengths)
    send_list = [send_slots(inverse[turn], tokens, devices, capacity) for turn in range(ROUNDS)]
    recv_list = [recv_slots(sort_order[turn], tokens, capacity) for turn in range(ROUNDS)]
    before_ids = shifted(sort_order[:, tokens - SPAN :], "seq", 1)
    normed_one, hat_one, inv_one = layer_norm(x_second, gain_one, b_attn.astype(jnp.float32))
    normed_one = normed_one.astype(jnp.bfloat16)
    qk_rows = linear(normed_one, m_qk).astype(jnp.bfloat16)
    value_rows = linear(normed_one, m_value).astype(jnp.bfloat16)
    stashed = []
    round_outs = []
    round_lse = []
    for turn in range(ROUNDS):
        got_qk, got_value = (
            lax.all_to_all(
                packed(qk_rows, send_list[turn], devices, capacity),
                "seq",
                split_axis=0,
                concat_axis=0,
                tiled=True,
            ),
            lax.all_to_all(
                packed(value_rows, send_list[turn], devices, capacity),
                "seq",
                split_axis=0,
                concat_axis=0,
                tiled=True,
            ),
        )
        sorted_qk, sorted_value, last_block = arrange(got_qk, got_value, recv_list[turn])
        before_block = shifted(last_block, "seq", 1)
        sorted_rows = (sorted_qk, sorted_value, before_block[0], before_block[1])
        pieces = score_parts(sorted_rows, sort_order[turn], before_ids[turn], doc_ends)
        out_sorted, lse_sorted = attend_out(pieces)
        back_out, back_lse = (
            lax.all_to_all(
                packed(out_sorted, recv_list[turn], devices, capacity),
                "seq",
                split_axis=0,
                concat_axis=0,
                tiled=True,
            ),
            lax.all_to_all(
                packed(lse_sorted, recv_list[turn], devices, capacity),
                "seq",
                split_axis=0,
                concat_axis=0,
                tiled=True,
            ),
        )
        round_outs.append(unpacked(back_out, send_list[turn]))
        round_lse.append(unpacked(back_lse, send_list[turn]))
        stashed.append(sorted_rows)
    lse_all = jnp.stack(round_lse)
    out_all = jnp.stack(round_outs).reshape(ROUNDS, tokens, HEADS, HEAD_DIM)
    merge = jnp.exp(lse_all - jax.nn.logsumexp(lse_all, axis=0))
    mixed = jnp.sum(merge[..., None] * out_all, axis=0).reshape(tokens, -1).astype(jnp.bfloat16)
    y_first = x_first + linear(mixed, m_out)
    normed_two, hat_two, inv_two = layer_norm(y_first, gain_two, b_ffn.astype(jnp.float32))
    normed_two = normed_two.astype(jnp.bfloat16)
    pre_up = linear(normed_two, m_up) + b_up.astype(jnp.float32)
    hidden, gelu_back = jax.vjp(partial(jax.nn.gelu, approximate=True), pre_up)
    hidden = hidden.astype(jnp.bfloat16)
    y_second = x_second + (linear(hidden, m_down) + b_down.astype(jnp.float32))
    grad_f = dy_second.astype(jnp.bfloat16)
    grad_down = inner_rows(hidden, grad_f)
    grad_bias_down = jnp.sum(grad_f.astype(jnp.float32), axis=0)
    grad_pre = gelu_back(outer_cols(grad_f, m_down))[0].astype(jnp.bfloat16)
    grad_up = inner_rows(normed_two, grad_pre)
    grad_bias_up = jnp.sum(grad_pre.astype(jnp.float32), axis=0)
    grad_two = outer_cols(grad_pre, m_up)
    grad_gain_ffn = jnp.sum(grad_two * hat_two, axis=0)
    grad_bias_ffn = jnp.sum(grad_two, axis=0)
    dx_first = dy_first + norm_back(grad_two, hat_two, inv_two, gain_two)
    grad_attn = dx_first.astype(jnp.bfloat16)
    grad_out = inner_rows(mixed, grad_attn)
    grad_mixed = outer_cols(grad_attn, m_out).reshape(tokens, HEADS, HEAD_DIM)
    along = jnp.sum(grad_mixed[None] * out_all, axis=-1)
    grad_lse_all = merge * (along - jnp.sum(merge * along, axis=0, keepdims=True))
    grad_qk_sum = jnp.zeros((tokens, HEADS * HEAD_DIM), jnp.float32)
    grad_value_sum = jnp.zeros((tokens, HEADS * HEAD_DIM), jnp.float32)
    for turn in range(ROUNDS):
        grad_round = (merge[turn][..., None] * grad_mixed).reshape(tokens, -1)
        got_out, got_lse = (
            lax.all_to_all(
                packed(grad_round, send_list[turn], devices, capacity),
                "seq",
                split_axis=0,
                concat_axis=0,
                tiled=True,
            ),
            lax.all_to_all(
                packed(grad_lse_all[turn], send_list[turn], devices, capacity),
                "seq",
                split_axis=0,
                concat_axis=0,
                tiled=True,
            ),
        )
        sorted_grad_out = unpacked(got_out, recv_list[turn])
        sorted_grad_lse = unpacked(got_lse, recv_list[turn])
        sorted_rows = stashed[turn]
        pieces = score_parts(sorted_rows, sort_order[turn], before_ids[turn], doc_ends)
        grad_query, grad_key, grad_val = attend_back(pieces, sorted_grad_out, sorted_grad_lse)
        spill = shifted(
            jnp.stack([grad_key[0, :SPAN], grad_val[0, :SPAN]]).astype(jnp.bfloat16), "seq", -1
        ).astype(jnp.float32)
        key_add = jnp.concatenate([grad_key[1:, :SPAN], spill[0][None]], axis=0)
        value_add = jnp.concatenate([grad_val[1:, :SPAN], spill[1][None]], axis=0)
        sorted_grad_qk = (grad_query + grad_key[:, SPAN:] + key_add).reshape(tokens, -1)
        sorted_grad_value = (grad_val[:, SPAN:] + value_add).reshape(tokens, -1)
        back_qk, back_value = (
            lax.all_to_all(
                as_sent(packed(sorted_grad_qk, recv_list[turn], devices, capacity)),
                "seq",
                split_axis=0,
                concat_axis=0,
                tiled=True,
            ),
            lax.all_to_all(
                as_sent(packed(sorted_grad_value, recv_list[turn], devices, capacity)),
                "seq",
                split_axis=0,
                concat_axis=0,
                tiled=True,
            ),
        )
        grad_qk_sum = grad_qk_sum + unpacked(back_qk, send_list[turn])
        grad_value_sum = grad_value_sum + unpacked(back_value, send_list[turn])
    grad_qk_rows = grad_qk_sum.astype(jnp.bfloat16)
    grad_value_rows = grad_value_sum.astype(jnp.bfloat16)
    grad_qk = inner_rows(normed_one, grad_qk_rows)
    grad_value = inner_rows(normed_one, grad_value_rows)
    grad_one = outer_cols(grad_qk_rows, m_qk) + outer_cols(grad_value_rows, m_value)
    grad_gain_attn = jnp.sum(grad_one * hat_one, axis=0)
    grad_bias_attn = jnp.sum(grad_one, axis=0)
    dx_second = dy_second + norm_back(grad_one, hat_one, inv_one, gain_one)
    s_qk, s_value, s_out, s_gattn, s_battn, s_gffn, s_bffn, s_up, s_bup, s_down, s_bdown = (
        lax.psum_scatter(grad_qk, "seq", scatter_dimension=0, tiled=True),
        lax.psum_scatter(grad_value, "seq", scatter_dimension=0, tiled=True),
        lax.psum_scatter(grad_out, "seq", scatter_dimension=0, tiled=True),
        lax.psum_scatter(grad_gain_attn, "seq", scatter_dimension=0, tiled=True),
        lax.psum_scatter(grad_bias_attn, "seq", scatter_dimension=0, tiled=True),
        lax.psum_scatter(grad_gain_ffn, "seq", scatter_dimension=0, tiled=True),
        lax.psum_scatter(grad_bias_ffn, "seq", scatter_dimension=0, tiled=True),
        lax.psum_scatter(grad_up, "seq", scatter_dimension=0, tiled=True),
        lax.psum_scatter(grad_bias_up, "seq", scatter_dimension=0, tiled=True),
        lax.psum_scatter(grad_down, "seq", scatter_dimension=0, tiled=True),
        lax.psum_scatter(grad_bias_down, "seq", scatter_dimension=0, tiled=True),
    )
    return (
        y_first,
        y_second,
        dx_first,
        dx_second,
        s_qk,
        s_value,
        s_out,
        s_gattn,
        s_battn,
        s_gffn,
        s_bffn,
        s_up,
        s_bup,
        s_down,
        s_bdown,
    )


CAP_ROWS = 16
PARTS = 8


def dot_nn(a, b):
    return lax.dot_general(a, b, (((1,), (0,)), ((), ())), preferred_element_type=F32)


def dot_nt(a, b):
    return lax.dot_general(a, b, (((1,), (1,)), ((), ())), preferred_element_type=F32)


def dot_tn(a, b):
    return lax.dot_general(a, b, (((0,), (0,)), ((), ())), preferred_element_type=F32)


def hot_rows(slot_row, slots):
    ids = lax.broadcasted_iota(jnp.int32, (slots, slot_row.shape[1]), 0).astype(F32)
    return jnp.where(ids == slot_row, 1.0, 0.0).astype(BF)


def hot_cols(slot_col, slots):
    ids = lax.broadcasted_iota(jnp.int32, (slot_col.shape[0], slots), 1).astype(F32)
    return jnp.where(ids == slot_col, 1.0, 0.0).astype(BF)


def key_norm(keys):
    wide = keys.astype(F32)
    square = wide * wide
    high = square.astype(BF)
    low = (square - high.astype(F32)).astype(BF)
    ones = jnp.ones((8, keys.shape[1]), BF)
    return lax.rsqrt((dot_nt(ones, high) + dot_nt(ones, low))[0:1])


def span_softmax(raw, norm, key_ids, query_ids, query_starts):
    factor = norm * SCALE
    kept = (key_ids < query_ids) & (key_ids >= query_starts)
    score = jnp.where(
        key_ids == query_ids, -100000.0, jnp.where(kept, raw * factor, -1000000000.0)
    )
    top = jnp.max(score, axis=1, keepdims=True)
    weight = jnp.exp(score - top)
    total = jnp.sum(weight, axis=1, keepdims=True)
    return factor, kept, weight, top, total


def three_parts(wide):
    high = wide.astype(BF).astype(F32)
    rest = wide - high
    mid = rest.astype(BF).astype(F32)
    return high, mid, rest - mid


def forward_kernel(
    place,
    x_0,
    x_1,
    x_2,
    x_3,
    info,
    key_ids,
    out_0,
    out_1,
    out_2,
    out_3,
    kept_rows,
    lanes,
    heads_out,
):
    blocks, tokens = info.shape[0], info.shape[2]
    slots = blocks * CAP_ROWS
    width = x_0.shape[1]
    spans = tokens // SPAN
    turn = place[0]
    rounds = ROUNDS

    for offset, rows in enumerate((x_0, x_1, x_2, x_3)):

        def pack(group, carry, offset=offset, rows=rows):
            source = group * rounds + lax.bitwise_xor(turn, offset)
            hot = hot_rows(info[source, 3:4, :], slots)
            start = pl.multiple_of(group * tokens, tokens)
            part = dot_nn(hot, rows[pl.ds(start, tokens), :]).astype(BF)
            lanes[:, pl.ds(source, 1)] = part.reshape(blocks, 1, CAP_ROWS, width)
            return carry

        lax.fori_loop(0, blocks // rounds, pack, 0, unroll=4)

    def place_rows(block, carry):
        cols = jnp.transpose(info[block])
        hot = hot_cols(cols[:, 2:3], slots)
        part = dot_nn(hot, lanes[block].reshape(slots, width)).astype(BF)
        start = pl.multiple_of(SPAN + block * tokens, SPAN)
        kept_rows[pl.ds(start, tokens), :] = part
        return carry

    lax.fori_loop(0, blocks, place_rows, 0, unroll=4)
    kept_rows[0:SPAN, :] = kept_rows[blocks * tokens : blocks * tokens + SPAN, :]

    def attend(block, carry):
        cols = jnp.transpose(info[block])
        lane = lax.broadcasted_iota(jnp.int32, (SPAN, width - HEAD_DIM), 1)
        first = []
        for part in range(spans):
            span = block * spans + part
            start = pl.multiple_of(span * SPAN, SPAN)
            rows = kept_rows[pl.ds(start, 2 * SPAN), :]
            keys = rows[:, :HEAD_DIM]
            first.append((rows, dot_nt(rows[SPAN:, :HEAD_DIM], keys), key_norm(keys)))
        second = []
        for part in range(spans):
            rows, raw, norm = first[part]
            ids = cols[part * SPAN : (part + 1) * SPAN]
            factor, kept, weight, top, total = span_softmax(
                raw, norm, key_ids[pl.ds(block * spans + part, 1), :], ids[:, 0:1], ids[:, 1:2]
            )
            high, mid, low = three_parts(top + jnp.log(total))
            extra = jnp.where(
                lane == 0, high, jnp.where(lane == 1, mid, jnp.where(lane == 2, low, 0.0))
            ).astype(BF)
            second.append(((weight * (1.0 / total)).astype(BF), extra))
        for part in range(spans):
            probs, extra = second[part]
            here = slice(part * SPAN, (part + 1) * SPAN)
            heads_out[block, here, :HEAD_DIM] = dot_nn(probs, first[part][0][:, HEAD_DIM:]).astype(BF)
            heads_out[block, here, HEAD_DIM:] = extra
        return carry

    lax.fori_loop(0, blocks, attend, 0)

    def unplace(block, carry):
        hot = hot_rows(info[block, 2:3, :], slots)
        part = dot_nn(hot, heads_out[block]).astype(BF)
        lanes[:, pl.ds(block, 1)] = part.reshape(blocks, 1, CAP_ROWS, width)
        return carry

    lax.fori_loop(0, blocks, unplace, 0, unroll=4)

    for offset, out in enumerate((out_0, out_1, out_2, out_3)):

        def unpack(group, carry, offset=offset, out=out):
            source = group * rounds + lax.bitwise_xor(turn, offset)
            cols = jnp.transpose(info[source])
            hot = hot_cols(cols[:, 3:4], slots)
            part = dot_nn(hot, lanes[source].reshape(slots, width))
            out[group, 0:tokens, :] = part[:, :HEAD_DIM].astype(BF)
            flat = jnp.transpose(part[:, HEAD_DIM:])[0:PARTS, :].astype(BF)
            for piece in range(tokens // HEAD_DIM):
                first = tokens + piece * PARTS
                out[group, first : first + PARTS, :] = flat[
                    :, piece * HEAD_DIM : (piece + 1) * HEAD_DIM
                ]
            return carry

        lax.fori_loop(0, blocks // rounds, unpack, 0, unroll=4)


def tall_parts(ref, group, first, tokens):
    flat = jnp.concatenate(
        [
            ref[group, first + piece * PARTS : first + (piece + 1) * PARTS, :].astype(F32)
            for piece in range(tokens // HEAD_DIM)
        ],
        axis=1,
    )
    return jnp.transpose(flat)


def put_parts(ref, group, first, column):
    tokens = column.shape[0]
    high, mid, low = three_parts(column)
    lane = lax.broadcasted_iota(jnp.int32, (tokens, PARTS), 1)
    tall = jnp.where(lane == 0, high, jnp.where(lane == 1, mid, jnp.where(lane == 2, low, 0.0)))
    flat = jnp.transpose(tall).astype(BF)
    for piece in range(tokens // HEAD_DIM):
        at = first + piece * PARTS
        ref[group, at : at + PARTS, :] = flat[:, piece * HEAD_DIM : (piece + 1) * HEAD_DIM]


def combined(refs, group):
    tokens = refs[0].shape[1] // (HEAD_DIM + PARTS) * HEAD_DIM
    lse = []
    for ref in refs:
        tall = tall_parts(ref, group, tokens, tokens)
        lse.append(tall[:, 0:1] + tall[:, 1:2] + tall[:, 2:3])
    top = lse[0]
    for other in lse[1:]:
        top = jnp.maximum(top, other)
    weights = [jnp.exp(one - top) for one in lse]
    total = sum(weights[1:], weights[0])
    scale = 1.0 / total
    rows = [
        (weight * scale) * ref[group, 0:tokens, :].astype(F32)
        for weight, ref in zip(weights, refs)
    ]
    return sum(rows[1:], rows[0]), top + jnp.log(total)


def pair_kernel(a, b, out):
    tokens = out.shape[1] // (HEAD_DIM + PARTS) * HEAD_DIM
    for group in range(out.shape[0]):
        rows, lse = combined((a, b), group)
        out[group, 0:tokens, :] = rows.astype(BF)
        put_parts(out, group, tokens, lse)


def final_kernel(a, b, c, mixed, total_lse):
    for group in range(mixed.shape[0]):
        rows, lse = combined((a, b, c), group)
        mixed[group] = rows.astype(BF)
        put_parts(total_lse, group, 0, lse)


def backward_kernel(
    place,
    g_0,
    g_1,
    g_2,
    g_3,
    l_0,
    l_1,
    l_2,
    l_3,
    kept_rows,
    info,
    key_ids,
    out_0,
    out_1,
    out_2,
    out_3,
    lanes,
    sums,
):
    blocks, tokens = info.shape[0], info.shape[2]
    slots = blocks * CAP_ROWS
    width = kept_rows.shape[1]
    spans = tokens // SPAN

    for offset, grads, lse in ((0, g_0, l_0), (1, g_1, l_1), (2, g_2, l_2), (3, g_3, l_3)):

        def pack(group, carry, offset=offset, grads=grads, lse=lse):
            source = group * ROUNDS + lax.bitwise_xor(place[0], offset)
            hot = hot_rows(info[source, 3:4, :], slots)
            tall = [tall_parts(grads, group, tokens, tokens), tall_parts(lse, group, 0, tokens)]
            tall.append(jnp.zeros((tokens, HEAD_DIM - 2 * PARTS), F32))
            rows = jnp.concatenate(
                [grads[group, 0:tokens, :], jnp.concatenate(tall, axis=1).astype(BF)], axis=1
            )
            part = dot_nn(hot, rows).astype(BF)
            lanes[:, pl.ds(source, 1)] = part.reshape(blocks, 1, CAP_ROWS, width)
            return carry

        lax.fori_loop(0, blocks // ROUNDS, pack, 0, unroll=4)

    sums[0:SPAN, :] = jnp.zeros((SPAN, width), F32)

    def attend(block, carry):
        cols = jnp.transpose(info[block])
        hot = hot_cols(cols[:, 2:3], slots)
        part_grads = dot_nn(hot, lanes[block].reshape(slots, width))
        grad_rows = part_grads[:, :HEAD_DIM]

        def summed(first):
            return sum(
                (part_grads[:, first + at : first + at + 1] for at in (1, 2)),
                part_grads[:, first : first + 1],
            )

        pull = summed(HEAD_DIM)
        total_lse = summed(HEAD_DIM + PARTS)
        first = []
        for part in range(spans):
            span = block * spans + part
            start = pl.multiple_of(span * SPAN, SPAN)
            rows = kept_rows[pl.ds(start, 2 * SPAN), :]
            keys = rows[:, :HEAD_DIM]
            queries = rows[SPAN:, :HEAD_DIM]
            raw = dot_nt(queries, keys)
            first.append((start, keys, queries, rows[:, HEAD_DIM:], raw, key_norm(keys)))
        middle = []
        for part in range(spans):
            start, keys, queries, values, raw, norm = first[part]
            here = slice(part * SPAN, (part + 1) * SPAN)
            ids = cols[here]
            factor, kept, weight, top, total = span_softmax(
                raw, norm, key_ids[pl.ds(block * spans + part, 1), :], ids[:, 0:1], ids[:, 1:2]
            )
            merge = jnp.exp(top + jnp.log(total) - total_lse[here])
            grad_out = (merge * grad_rows[here]).astype(BF)
            middle.append((factor, kept, weight * (1.0 / total), grad_out, merge * pull[here]))
        back = [dot_nt(middle[part][3], first[part][3]) for part in range(spans)]
        second = []
        slopes = []
        for part in range(spans):
            raw, norm = first[part][4:]
            factor, kept, probs, grad_out, pulled = middle[part]
            grad_score = jnp.where(kept, probs * (back[part] - pulled), 0.0)
            slopes.append(
                jnp.sum(grad_score * raw, axis=0, keepdims=True) * SCALE * norm * norm * norm
            )
            second.append(((grad_score * factor).astype(BF), probs.astype(BF)))
        held = []
        for part in range(spans):
            start, keys, queries = first[part][:3]
            grad_raw, probs = second[part]
            held.append(
                (
                    start,
                    keys,
                    dot_nn(grad_raw, keys),
                    dot_tn(grad_raw, queries),
                    dot_tn(probs, middle[part][3]),
                )
            )
        slopes.append(jnp.zeros((8 - spans, 2 * SPAN), F32))
        slope_cols = jnp.transpose(jnp.concatenate(slopes, axis=0))
        for part in range(spans):
            start, keys, grad_query, grad_key, grad_val = held[part]
            grad_key = grad_key - slope_cols[:, part : part + 1] * keys.astype(F32)
            sums[pl.ds(start, SPAN), :] += jnp.concatenate(
                [grad_key[:SPAN], grad_val[:SPAN]], axis=1
            )
            after = pl.multiple_of(start + SPAN, SPAN)
            sums[pl.ds(after, SPAN), :] = jnp.concatenate(
                [grad_query + grad_key[SPAN:], grad_val[SPAN:]], axis=1
            )
        return carry

    lax.fori_loop(0, blocks, attend, 0)
    sums[blocks * tokens : blocks * tokens + SPAN, :] += sums[0:SPAN, :]

    def unplace(block, carry):
        hot = hot_rows(info[block, 2:3, :], slots)
        start = pl.multiple_of(SPAN + block * tokens, SPAN)
        part = dot_nn(hot, sums[pl.ds(start, tokens), :].astype(BF)).astype(BF)
        lanes[:, pl.ds(block, 1)] = part.reshape(blocks, 1, CAP_ROWS, width)
        return carry

    lax.fori_loop(0, blocks, unplace, 0, unroll=4)

    for offset, out in enumerate((out_0, out_1, out_2, out_3)):

        def unpack(group, carry, offset=offset, out=out):
            source = group * ROUNDS + lax.bitwise_xor(place[0], offset)
            cols = jnp.transpose(info[source])
            hot = hot_cols(cols[:, 3:4], slots)
            start = pl.multiple_of(group * tokens, tokens)
            part = dot_nn(hot, lanes[source].reshape(slots, width))
            out[pl.ds(start, tokens), :] = part.astype(BF)
            return carry

        lax.fori_loop(0, blocks // ROUNDS, unpack, 0, unroll=4)


def in_vmem(count):
    return [pl.BlockSpec(memory_space=pltpu.VMEM)] * count


def run_kernel(kernel, name, operands, shapes, scratch, scalar):
    first = [pl.BlockSpec(memory_space=pltpu.SMEM)] if scalar else []
    return pl.pallas_call(
        kernel,
        out_shape=tuple(jax.ShapeDtypeStruct(shape, BF) for shape in shapes),
        in_specs=first + in_vmem(len(operands) - len(first)),
        out_specs=tuple(in_vmem(len(shapes))),
        scratch_shapes=[pltpu.VMEM(shape, dtype) for shape, dtype in scratch],
        compiler_params=pltpu.CompilerParams(vmem_limit_bytes=48 << 20),
        cost_estimate=pl.CostEstimate(
            flops=20 * 10**9 if scalar else 10**7,
            bytes_accessed=12 * 10**6 if scalar else 2 * 10**6,
            transcendentals=10**6 if scalar else 10**4,
        ),
        name=name,
    )(*operands)


def run_forward(turn, rows, info, key_ids):
    blocks, _, tokens = info.shape
    width = rows[0].shape[1]
    tall = tokens + PARTS * tokens // HEAD_DIM
    return run_kernel(
        forward_kernel,
        "hash_forward",
        (turn, *rows, info, key_ids),
        [(blocks // ROUNDS, tall, HEAD_DIM)] * ROUNDS + [(SPAN + blocks * tokens, width)],
        [((blocks, blocks, CAP_ROWS, width), BF), ((blocks, tokens, width), BF)],
        True,
    )


def run_backward(turn, grads, lse, kept_rows, info, key_ids):
    blocks, _, tokens = info.shape
    width = kept_rows.shape[1]
    return run_kernel(
        backward_kernel,
        "hash_backward",
        (turn, *grads, *lse, kept_rows, info, key_ids),
        [(blocks * tokens // ROUNDS, width)] * ROUNDS,
        [((blocks, blocks, CAP_ROWS, width), BF), ((SPAN + blocks * tokens, width), F32)],
        True,
    )


def merge_pair(a, b):
    return run_kernel(pair_kernel, "merge_pair", (a, b), [a.shape], [], False)[0]


def merge_final(a, b, c):
    groups, tall, width = a.shape
    tokens = tall // (HEAD_DIM + PARTS) * HEAD_DIM
    shapes = [(groups, tokens, width), (groups, tall - tokens, width)]
    return run_kernel(final_kernel, "merge_final", (a, b, c), shapes, [], False)


def peers(mask):
    size = HEADS * ROUNDS
    return [(i, i ^ mask) for i in range(size)]


def swap(x, mask):
    return lax.ppermute(x, "seq", peers(mask))


def columns():
    return [[head * ROUNDS + turn for head in range(HEADS)] for turn in range(ROUNDS)]


def rows_of():
    return [[head * ROUNDS + turn for turn in range(ROUNDS)] for head in range(HEADS)]


def gather_group(x):
    side = swap(x, 2)
    return (x, swap(x, 1), side, swap(side, 1))


def sum_group(parts):
    near = parts[0] + swap(parts[1].astype(BF), 1).astype(F32)
    far = parts[2] + swap(parts[3].astype(BF), 1).astype(F32)
    return near + swap(far.astype(BF), 2).astype(F32)


def exchange(x, groups=None):
    return lax.all_to_all(
        x, "seq", split_axis=0, concat_axis=0, tiled=True, axis_index_groups=groups
    )


def rounded(x):
    return lax.reduce_precision(x, 8, 7)


def split_three(wide):
    high = rounded(wide)
    rest = wide - high
    mid = rounded(rest)
    return jnp.stack([high, mid, rest - mid])


def slots_sent(target, tokens, capacity):
    device = target // tokens
    early = jnp.arange(tokens)[None, :] < jnp.arange(tokens)[:, None]
    same = (device[:, None] == device[None, :]) & early
    return device * capacity + jnp.sum(same.astype(jnp.int32), axis=1)


def start_of(token_ids, doc_ends):
    ends = doc_ends[None, :]
    return jnp.max(jnp.where(ends <= token_ids[:, None], ends, 0), axis=1)


def shards_fast(
    x_first,
    x_second,
    w_qk,
    w_value,
    w_out,
    gain_attn,
    bias_attn,
    gain_ffn,
    bias_ffn,
    w_up,
    bias_up,
    w_down,
    bias_down,
    sort_order,
    inverse,
    lengths,
    dy_first,
    dy_second,
):
    devices = lax.axis_size("seq")
    tokens, features = x_first.shape
    capacity = 2 * tokens // devices
    shard = features // devices
    place = lax.axis_index("seq")
    doc_ends = jnp.cumsum(lengths)

    per_round = []
    vectors = rounded(
        jnp.concatenate([gain_attn, bias_attn, gain_ffn, bias_ffn, bias_up, bias_down])
    )
    vectors = jnp.pad(vectors, (0, 2 * tokens - vectors.shape[0])).reshape(2, tokens)
    for turn in range(ROUNDS):
        ids = sort_order[turn]
        rows = jnp.stack(
            [
                ids,
                start_of(ids, doc_ends),
                recv_slots(ids, tokens, capacity),
                slots_sent(inverse[turn], tokens, capacity),
            ]
        ).astype(F32)
        per_round.append(jnp.concatenate([rows, vectors, jnp.zeros((2, tokens), F32)]))
    info = jnp.tile(jnp.stack(per_round), (HEADS, 1, 1))
    info = exchange(info)
    got = info[:, 4:6].reshape(devices, 2 * tokens)

    def vector(first, size):
        return got[:, first : first + size].reshape(devices * size)

    gain_one, shift_one = vector(0, shard), vector(shard, shard)
    gain_two, shift_two = vector(2 * shard, shard), vector(3 * shard, shard)
    wide = bias_up.shape[0]
    b_up = vector(4 * shard, wide)
    b_down = vector(4 * shard + wide, shard)
    spans = info[:, 0].reshape(devices * tokens // SPAN, SPAN)
    key_ids = jnp.concatenate([jnp.roll(spans, 1, axis=0), spans], axis=1)

    pair = jnp.stack(
        [w_qk.reshape(shard, HEADS, HEAD_DIM), w_value.reshape(shard, HEADS, HEAD_DIM)], axis=2
    ).reshape(shard, 2 * features)
    m_pair = lax.all_gather(pair.astype(BF), "seq", axis=0, tiled=True)
    half = HEADS * wide
    up_cols = jnp.transpose(
        w_up.astype(BF).reshape(shard, HEADS, ROUNDS, wide), (2, 0, 1, 3)
    ).reshape(ROUNDS, shard, half)
    out_rows = jnp.broadcast_to(w_out.astype(BF), (ROUNDS, shard, features))
    near_rows = exchange(jnp.concatenate([up_cols, out_rows], axis=2), rows_of())
    near_rows = near_rows.reshape(ROUNDS * shard, half + features)
    b_up = lax.dynamic_index_in_dim(
        b_up.reshape(HEADS, ROUNDS, wide), place % ROUNDS, axis=1, keepdims=False
    ).reshape(HEADS * wide)

    normed_one, hat_one, inv_one = layer_norm(x_second, gain_one, shift_one)
    normed_one, near_rows = lax.optimization_barrier((normed_one.astype(BF), near_rows))
    rows = linear(normed_one, m_pair).astype(BF)
    rows = jnp.transpose(rows.reshape(tokens, HEADS, 2 * HEAD_DIM), (1, 0, 2))
    own = exchange(rows, columns()).reshape(HEADS * tokens, 2 * HEAD_DIM)
    own, near_rows = lax.optimization_barrier((own, near_rows))
    m_ffn = lax.all_gather(
        jnp.concatenate([near_rows, w_down.astype(BF)], axis=1),
        "seq",
        axis=0,
        tiled=True,
        axis_index_groups=columns(),
    )
    m_up, m_out, m_down = (m_ffn[:, at : at + features] for at in (0, half, half + features))
    turn = (place % ROUNDS).astype(jnp.int32).reshape(1)
    *sent, kept_rows = run_forward(turn, gather_group(own), info, key_ids)
    far = merge_pair(sent[2], swap(sent[3], 1))
    mixed, total_lse = merge_final(sent[0], swap(sent[1], 1), swap(far, 2))
    mixed = exchange(mixed, columns())
    mixed, normed_one = lax.optimization_barrier((mixed, normed_one))
    normed_col = lax.all_gather(
        normed_one, "seq", axis=0, tiled=True, axis_index_groups=columns()
    )
    mixed = jnp.transpose(mixed, (1, 0, 2)).reshape(tokens, features)
    y_first = x_first + linear(mixed, m_out)
    normed_two, hat_two, inv_two = layer_norm(y_first, gain_two, shift_two)
    normed_two = normed_two.astype(BF)
    grad_f = dy_second.astype(BF)
    grad_f_all = jnp.concatenate(gather_group(grad_f))
    normed_all = jnp.concatenate(gather_group(normed_two))
    pre_up = linear(normed_all, m_up) + b_up
    hidden, gelu_back = jax.vjp(partial(jax.nn.gelu, approximate=True), pre_up)
    hidden = hidden.astype(BF)
    branch = sum_group(linear(hidden, m_down).reshape(ROUNDS, tokens, features))
    y_second = x_second + (branch + b_down)
    grad_down = inner_rows(hidden, grad_f_all)
    grad_bias_down = jnp.sum(grad_f.astype(F32), axis=0)
    grad_pre = gelu_back(outer_cols(grad_f_all, m_down))[0].astype(BF)
    grad_up = inner_rows(normed_all, grad_pre)
    grad_bias_up = jnp.sum(grad_pre.astype(F32), axis=0)
    grad_two = sum_group(outer_cols(grad_pre, m_up).reshape(ROUNDS, tokens, features))
    grad_gain_ffn = jnp.sum(grad_two * hat_two, axis=0)
    grad_bias_ffn = jnp.sum(grad_two, axis=0)
    dx_first = dy_first + norm_back(grad_two, hat_two, inv_two, gain_two)
    grad_attn = dx_first.astype(BF)
    grad_out = inner_rows(mixed, grad_attn)
    fourth = features // ROUNDS
    grad_mixed = outer_cols(grad_attn, m_out).astype(BF)
    pull = jnp.sum(
        (grad_mixed.astype(F32) * mixed.astype(F32)).reshape(tokens, HEADS, HEAD_DIM), axis=-1
    )
    parts = split_three(jnp.transpose(pull))
    parts = jnp.pad(parts, ((0, PARTS - 3), (0, 0), (0, 0)))
    parts = jnp.transpose(parts.reshape(PARTS, HEADS, -1, HEAD_DIM), (1, 2, 0, 3))
    parts = parts.reshape(HEADS, -1, HEAD_DIM).astype(BF)
    grad_mixed = jnp.transpose(grad_mixed.reshape(tokens, HEADS, HEAD_DIM), (1, 0, 2))
    grad_mixed = exchange(jnp.concatenate([grad_mixed, parts], axis=1), columns())
    grad_mixed, grad_up, grad_down, grad_out = lax.optimization_barrier(
        (grad_mixed, grad_up, grad_down, grad_out)
    )
    grad_out = sum_group(
        [
            lax.dynamic_slice_in_dim(grad_out, ((place % ROUNDS) ^ near) * fourth, fourth, axis=1)
            for near in range(ROUNDS)
        ]
    )
    merged = jnp.concatenate([x.astype(BF) for x in (grad_up, grad_out, grad_down)], axis=1)
    merged = lax.psum_scatter(
        merged, "seq", scatter_dimension=0, tiled=True, axis_index_groups=columns()
    )
    s_down = merged[:, half + fourth :].astype(F32)
    merged = exchange(merged[:, : half + fourth].reshape(ROUNDS, shard, -1), rows_of())
    s_up = jnp.transpose(merged[:, :, :half].reshape(ROUNDS, shard, HEADS, wide), (1, 2, 0, 3))
    s_up = s_up.reshape(shard, ROUNDS * half).astype(F32)
    s_out = jnp.transpose(merged[:, :, half:], (1, 0, 2)).reshape(shard, features).astype(F32)

    grad_head = run_backward(
        turn, gather_group(grad_mixed), gather_group(total_lse), kept_rows, info, key_ids
    )
    grad_head = sum_group([x.astype(F32) for x in grad_head]).astype(BF)
    grad_rows = exchange(grad_head.reshape(HEADS, tokens, 2 * HEAD_DIM), columns())
    grad_rows, grad_head = lax.optimization_barrier((grad_rows, grad_head))
    grad_rows = jnp.transpose(grad_rows, (1, 0, 2)).reshape(tokens, 2 * features)

    s_pair = exchange(
        inner_rows(normed_col, grad_head).astype(BF).reshape(devices, shard, 2 * HEAD_DIM)
    )
    s_pair = jnp.sum(
        s_pair.reshape(HEADS, ROUNDS, shard, 2, HEAD_DIM).astype(F32), axis=1
    ).transpose(2, 1, 0, 3)
    s_qk = s_pair[0].reshape(shard, features)
    s_value = s_pair[1].reshape(shard, features)
    grad_one = outer_cols(grad_rows, m_pair)
    grad_gain_attn = jnp.sum(grad_one * hat_one, axis=0)
    grad_bias_attn = jnp.sum(grad_one, axis=0)
    dx_second = dy_second + norm_back(grad_one, hat_one, inv_one, gain_one)
    is_mine = (jnp.arange(ROUNDS) == place % ROUNDS).astype(F32)
    grad_bias_up = grad_bias_up.reshape(HEADS, 1, wide) * is_mine[None, :, None]
    small = jnp.concatenate(
        [
            grad_gain_attn.reshape(devices, -1),
            grad_bias_attn.reshape(devices, -1),
            grad_gain_ffn.reshape(devices, -1),
            grad_bias_ffn.reshape(devices, -1),
            grad_bias_up.reshape(devices, -1),
            grad_bias_down.reshape(devices, -1),
        ],
        axis=1,
    )
    small = jnp.sum(exchange(small[:, None]), axis=(0, 1))
    s_gattn, s_battn, s_gffn, s_bffn = (small[i * shard : (i + 1) * shard] for i in range(4))
    s_bup = small[4 * shard : 4 * shard + wide]
    s_bdown = small[4 * shard + wide :]
    return (
        y_first,
        y_second,
        dx_first,
        dx_second,
        s_qk,
        s_value,
        s_out,
        s_gattn,
        s_battn,
        s_gffn,
        s_bffn,
        s_up,
        s_bup,
        s_down,
        s_bdown,
    )


def solution(mesh):
    in_specs = (
        P("seq", None),
        P("seq", None),
        P("seq", None),
        P("seq", None),
        P("seq", None),
        P("seq"),
        P("seq"),
        P("seq"),
        P("seq"),
        P("seq", None),
        P("seq"),
        P("seq", None),
        P("seq"),
        P(None, "seq"),
        P(None, "seq"),
        P(),
        P("seq", None),
        P("seq", None),
    )
    out_specs = (
        P("seq", None),
        P("seq", None),
        P("seq", None),
        P("seq", None),
        P("seq", None),
        P("seq", None),
        P("seq", None),
        P("seq"),
        P("seq"),
        P("seq"),
        P("seq"),
        P("seq", None),
        P("seq"),
        P("seq", None),
        P("seq"),
    )
    fast = mesh.shape["seq"] == HEADS * ROUNDS
    return jax.shard_map(shards_fast if fast else shards, mesh=mesh, in_specs=in_specs, out_specs=out_specs, check_vma=False)
```

```python
from functools import partial
import math

import jax
import jax.numpy as jnp
from jax import lax
from jax.experimental import pallas as pl
from jax.experimental.pallas import tpu as pltpu
from jax.sharding import PartitionSpec as P

HEADS = 8
HEAD_DIM = 128
SPAN = 64
ROUNDS = 4

EPSILON = 1e-05
SCALE = 1.0 / math.sqrt(HEAD_DIM)
BF = jnp.bfloat16
F32 = jnp.float32


def shifted(x, axis, by):
    size = lax.axis_size(axis)
    return lax.ppermute(x, axis, [(i, (i + by) % size) for i in range(size)])


def as_sent(x):
    return jax.tree.map(lambda a: a.astype(jnp.bfloat16) if a.dtype == jnp.float32 else a, x)


def layer_norm(inputs, norm_gain, norm_shift):
    centered = inputs - jnp.mean(inputs, axis=-1, keepdims=True)
    inv_std = lax.rsqrt(jnp.mean(centered * centered, axis=-1, keepdims=True) + EPSILON)
    normed = centered * inv_std
    return (normed * norm_gain + norm_shift, normed, inv_std)


def norm_back(grad_rows, normed, inv_std, norm_gain):
    grad_hat = grad_rows * norm_gain
    return inv_std * (
        grad_hat
        - jnp.mean(grad_hat, axis=-1, keepdims=True)
        - normed * jnp.mean(grad_hat * normed, axis=-1, keepdims=True)
    )


def linear(matrix_a, matrix_b):
    return jnp.dot(matrix_a, matrix_b, preferred_element_type=jnp.float32)


def inner_rows(matrix_a, matrix_b):
    return lax.dot_general(
        matrix_a, matrix_b, (((0,), (0,)), ((), ())), preferred_element_type=jnp.float32
    )


def outer_cols(matrix_a, matrix_b):
    return lax.dot_general(
        matrix_a, matrix_b, (((1,), (1,)), ((), ())), preferred_element_type=jnp.float32
    )


def segment_of(token_ids, doc_ends):
    return jnp.sum((token_ids[:, None] >= doc_ends[None, :]).astype(jnp.int32), axis=1)


def send_slots(target, tokens, devices, capacity):
    device = target // tokens
    onehot = (device[:, None] == jnp.arange(devices, dtype=jnp.int32)[None, :]).astype(jnp.int32)
    rank_in = jnp.sum(jnp.cumsum(onehot, axis=0) * onehot, axis=1) - 1
    return device * capacity + rank_in


def recv_slots(source_ids, tokens, capacity):
    device = source_ids // tokens
    earlier = (device[:, None] == device[None, :]) & (source_ids[None, :] < source_ids[:, None])
    return device * capacity + jnp.sum(earlier.astype(jnp.int32), axis=1)


def packed(inputs, slot_ids, devices, capacity):
    filled = (
        jnp.zeros((devices * capacity,) + inputs.shape[1:], inputs.dtype).at[slot_ids].set(inputs)
    )
    return filled.reshape((devices, capacity) + inputs.shape[1:])


def unpacked(received, slot_ids):
    return received.reshape((-1,) + received.shape[2:])[slot_ids]


def spanned(inputs, before):
    blocks = inputs.shape[0] // SPAN
    current = inputs.reshape((blocks, SPAN) + inputs.shape[1:])
    earlier = jnp.concatenate([before[None], current[:-1]], axis=0)
    return (current, jnp.concatenate([earlier, current], axis=1))


def arrange(got_qk, got_value, recv_slot):
    sorted_qk = unpacked(got_qk, recv_slot)
    sorted_value = unpacked(got_value, recv_slot)
    last_block = jnp.stack([sorted_qk[-SPAN:], sorted_value[-SPAN:]])
    return (sorted_qk, sorted_value, last_block)


def score_parts(sorted_rows, query_ids, before_ids, doc_ends):
    sorted_qk, sorted_value, before_qk, before_value = sorted_rows
    current, key_rows = spanned(sorted_qk, before_qk)
    _, value_keys = spanned(sorted_value, before_value)
    current_ids, key_ids = spanned(query_ids, before_ids)
    current_seg, key_seg = spanned(
        segment_of(query_ids, doc_ends), segment_of(before_ids, doc_ends)
    )
    blocks = current.shape[0]
    q_heads = current.reshape(blocks, SPAN, HEADS, HEAD_DIM)
    k_heads = key_rows.reshape(blocks, 2 * SPAN, HEADS, HEAD_DIM)
    v_heads = value_keys.reshape(blocks, 2 * SPAN, HEADS, HEAD_DIM)
    raw_dots = jnp.einsum("gihd,gjhd->ghij", q_heads, k_heads, preferred_element_type=jnp.float32)
    k_float = k_heads.astype(jnp.float32)
    key_norm = lax.rsqrt(jnp.sum(k_float * k_float, axis=-1))
    factor = jnp.transpose(key_norm, (0, 2, 1))[:, :, None, :] / math.sqrt(HEAD_DIM)
    allowed = (
        (key_ids[:, None, :] <= current_ids[:, :, None])
        & (key_seg[:, None, :] == current_seg[:, :, None])
    )[:, None]
    itself = (key_ids[:, None, :] == current_ids[:, :, None])[:, None]
    scores = jnp.where(itself, -100000.0, jnp.where(allowed, raw_dots * factor, -1000000000.0))
    log_total = jax.nn.logsumexp(scores, axis=-1)
    attn_probs = jnp.exp(scores - log_total[..., None])
    kept_mask = allowed & jnp.logical_not(itself)
    return (
        q_heads,
        k_heads,
        v_heads,
        k_float,
        key_norm,
        factor,
        kept_mask,
        raw_dots,
        attn_probs,
        log_total,
    )


def attend_out(pieces):
    (
        q_heads,
        k_heads,
        v_heads,
        k_float,
        key_norm,
        factor,
        kept_mask,
        raw_dots,
        attn_probs,
        log_total,
    ) = pieces
    blocks = q_heads.shape[0]
    out_heads = jnp.einsum(
        "ghij,gjhd->gihd",
        attn_probs.astype(jnp.bfloat16),
        v_heads,
        preferred_element_type=jnp.float32,
    )
    return (
        out_heads.reshape(blocks * SPAN, -1),
        jnp.transpose(log_total, (0, 2, 1)).reshape(blocks * SPAN, HEADS),
    )


def attend_back(pieces, grad_rows, grad_total):
    (
        q_heads,
        k_heads,
        v_heads,
        k_float,
        key_norm,
        factor,
        kept_mask,
        raw_dots,
        attn_probs,
        log_total,
    ) = pieces
    blocks = q_heads.shape[0]
    grad_heads = grad_rows.astype(jnp.bfloat16).reshape(blocks, SPAN, HEADS, HEAD_DIM)
    grad_lse = jnp.transpose(grad_total.reshape(blocks, SPAN, HEADS), (0, 2, 1))
    grad_prob = jnp.einsum(
        "gihd,gjhd->ghij", grad_heads, v_heads, preferred_element_type=jnp.float32
    )
    grad_val = jnp.einsum(
        "ghij,gihd->gjhd",
        attn_probs.astype(jnp.bfloat16),
        grad_heads,
        preferred_element_type=jnp.float32,
    )
    row_dot = jnp.sum(attn_probs * grad_prob, axis=-1, keepdims=True)
    grad_score = jnp.where(kept_mask, attn_probs * (grad_prob - row_dot + grad_lse[..., None]), 0.0)
    grad_raw = (grad_score * factor).astype(jnp.bfloat16)
    grad_norm = jnp.transpose(jnp.sum(grad_score * raw_dots, axis=2), (0, 2, 1)) / math.sqrt(
        HEAD_DIM
    )
    norm_cube = key_norm * key_norm * key_norm
    grad_query = jnp.einsum(
        "ghij,gjhd->gihd", grad_raw, k_heads, preferred_element_type=jnp.float32
    )
    grad_key = (
        jnp.einsum("ghij,gihd->gjhd", grad_raw, q_heads, preferred_element_type=jnp.float32)
        - (grad_norm * norm_cube)[..., None] * k_float
    )
    return (
        grad_query.reshape(blocks, SPAN, -1),
        grad_key.reshape(blocks, 2 * SPAN, -1),
        grad_val.reshape(blocks, 2 * SPAN, -1),
    )


def shards(
    x_first,
    x_second,
    w_qk,
    w_value,
    w_out,
    gain_attn,
    bias_attn,
    gain_ffn,
    bias_ffn,
    w_up,
    bias_up,
    w_down,
    bias_down,
    sort_order,
    inverse,
    lengths,
    dy_first,
    dy_second,
):
    devices = lax.axis_size("seq")
    tokens = x_first.shape[0]
    capacity = 2 * tokens // devices
    gathered = (
        lax.all_gather(w_qk.astype(jnp.bfloat16), "seq", axis=0, tiled=True),
        lax.all_gather(w_value.astype(jnp.bfloat16), "seq", axis=0, tiled=True),
        lax.all_gather(w_out.astype(jnp.bfloat16), "seq", axis=0, tiled=True),
        lax.all_gather(gain_attn.astype(jnp.bfloat16), "seq", axis=0, tiled=True),
        lax.all_gather(bias_attn.astype(jnp.bfloat16), "seq", axis=0, tiled=True),
        lax.all_gather(gain_ffn.astype(jnp.bfloat16), "seq", axis=0, tiled=True),
        lax.all_gather(bias_ffn.astype(jnp.bfloat16), "seq", axis=0, tiled=True),
        lax.all_gather(w_up.astype(jnp.bfloat16), "seq", axis=0, tiled=True),
        lax.all_gather(bias_up.astype(jnp.bfloat16), "seq", axis=0, tiled=True),
        lax.all_gather(w_down.astype(jnp.bfloat16), "seq", axis=0, tiled=True),
        lax.all_gather(bias_down.astype(jnp.bfloat16), "seq", axis=0, tiled=True),
    )
    m_qk, m_value, m_out, g_attn, b_attn, g_ffn, b_ffn, m_up, b_up, m_down, b_down = gathered
    gain_one = g_attn.astype(jnp.float32)
    gain_two = g_ffn.astype(jnp.float32)
    doc_ends = jnp.cumsum(lengths)
    send_list = [send_slots(inverse[turn], tokens, devices, capacity) for turn in range(ROUNDS)]
    recv_list = [recv_slots(sort_order[turn], tokens, capacity) for turn in range(ROUNDS)]
    before_ids = shifted(sort_order[:, tokens - SPAN :], "seq", 1)
    normed_one, hat_one, inv_one = layer_norm(x_second, gain_one, b_attn.astype(jnp.float32))
    normed_one = normed_one.astype(jnp.bfloat16)
    qk_rows = linear(normed_one, m_qk).astype(jnp.bfloat16)
    value_rows = linear(normed_one, m_value).astype(jnp.bfloat16)
    stashed = []
    round_outs = []
    round_lse = []
    for turn in range(ROUNDS):
        got_qk, got_value = (
            lax.all_to_all(
                packed(qk_rows, send_list[turn], devices, capacity),
                "seq",
                split_axis=0,
                concat_axis=0,
                tiled=True,
            ),
            lax.all_to_all(
                packed(value_rows, send_list[turn], devices, capacity),
                "seq",
                split_axis=0,
                concat_axis=0,
                tiled=True,
            ),
        )
        sorted_qk, sorted_value, last_block = arrange(got_qk, got_value, recv_list[turn])
        before_block = shifted(last_block, "seq", 1)
        sorted_rows = (sorted_qk, sorted_value, before_block[0], before_block[1])
        pieces = score_parts(sorted_rows, sort_order[turn], before_ids[turn], doc_ends)
        out_sorted, lse_sorted = attend_out(pieces)
        back_out, back_lse = (
            lax.all_to_all(
                packed(out_sorted, recv_list[turn], devices, capacity),
                "seq",
                split_axis=0,
                concat_axis=0,
                tiled=True,
            ),
            lax.all_to_all(
                packed(lse_sorted, recv_list[turn], devices, capacity),
                "seq",
                split_axis=0,
                concat_axis=0,
                tiled=True,
            ),
        )
        round_outs.append(unpacked(back_out, send_list[turn]))
        round_lse.append(unpacked(back_lse, send_list[turn]))
        stashed.append(sorted_rows)
    lse_all = jnp.stack(round_lse)
    out_all = jnp.stack(round_outs).reshape(ROUNDS, tokens, HEADS, HEAD_DIM)
    merge = jnp.exp(lse_all - jax.nn.logsumexp(lse_all, axis=0))
    mixed = jnp.sum(merge[..., None] * out_all, axis=0).reshape(tokens, -1).astype(jnp.bfloat16)
    y_first = x_first + linear(mixed, m_out)
    normed_two, hat_two, inv_two = layer_norm(y_first, gain_two, b_ffn.astype(jnp.float32))
    normed_two = normed_two.astype(jnp.bfloat16)
    pre_up = linear(normed_two, m_up) + b_up.astype(jnp.float32)
    hidden, gelu_back = jax.vjp(partial(jax.nn.gelu, approximate=True), pre_up)
    hidden = hidden.astype(jnp.bfloat16)
    y_second = x_second + (linear(hidden, m_down) + b_down.astype(jnp.float32))
    grad_f = dy_second.astype(jnp.bfloat16)
    grad_down = inner_rows(hidden, grad_f)
    grad_bias_down = jnp.sum(grad_f.astype(jnp.float32), axis=0)
    grad_pre = gelu_back(outer_cols(grad_f, m_down))[0].astype(jnp.bfloat16)
    grad_up = inner_rows(normed_two, grad_pre)
    grad_bias_up = jnp.sum(grad_pre.astype(jnp.float32), axis=0)
    grad_two = outer_cols(grad_pre, m_up)
    grad_gain_ffn = jnp.sum(grad_two * hat_two, axis=0)
    grad_bias_ffn = jnp.sum(grad_two, axis=0)
    dx_first = dy_first + norm_back(grad_two, hat_two, inv_two, gain_two)
    grad_attn = dx_first.astype(jnp.bfloat16)
    grad_out = inner_rows(mixed, grad_attn)
    grad_mixed = outer_cols(grad_attn, m_out).reshape(tokens, HEADS, HEAD_DIM)
    along = jnp.sum(grad_mixed[None] * out_all, axis=-1)
    grad_lse_all = merge * (along - jnp.sum(merge * along, axis=0, keepdims=True))
    grad_qk_sum = jnp.zeros((tokens, HEADS * HEAD_DIM), jnp.float32)
    grad_value_sum = jnp.zeros((tokens, HEADS * HEAD_DIM), jnp.float32)
    for turn in range(ROUNDS):
        grad_round = (merge[turn][..., None] * grad_mixed).reshape(tokens, -1)
        got_out, got_lse = (
            lax.all_to_all(
                packed(grad_round, send_list[turn], devices, capacity),
                "seq",
                split_axis=0,
                concat_axis=0,
                tiled=True,
            ),
            lax.all_to_all(
                packed(grad_lse_all[turn], send_list[turn], devices, capacity),
                "seq",
                split_axis=0,
                concat_axis=0,
                tiled=True,
            ),
        )
        sorted_grad_out = unpacked(got_out, recv_list[turn])
        sorted_grad_lse = unpacked(got_lse, recv_list[turn])
        sorted_rows = stashed[turn]
        pieces = score_parts(sorted_rows, sort_order[turn], before_ids[turn], doc_ends)
        grad_query, grad_key, grad_val = attend_back(pieces, sorted_grad_out, sorted_grad_lse)
        spill = shifted(
            jnp.stack([grad_key[0, :SPAN], grad_val[0, :SPAN]]).astype(jnp.bfloat16), "seq", -1
        ).astype(jnp.float32)
        key_add = jnp.concatenate([grad_key[1:, :SPAN], spill[0][None]], axis=0)
        value_add = jnp.concatenate([grad_val[1:, :SPAN], spill[1][None]], axis=0)
        sorted_grad_qk = (grad_query + grad_key[:, SPAN:] + key_add).reshape(tokens, -1)
        sorted_grad_value = (grad_val[:, SPAN:] + value_add).reshape(tokens, -1)
        back_qk, back_value = (
            lax.all_to_all(
                as_sent(packed(sorted_grad_qk, recv_list[turn], devices, capacity)),
                "seq",
                split_axis=0,
                concat_axis=0,
                tiled=True,
            ),
            lax.all_to_all(
                as_sent(packed(sorted_grad_value, recv_list[turn], devices, capacity)),
                "seq",
                split_axis=0,
                concat_axis=0,
                tiled=True,
            ),
        )
        grad_qk_sum = grad_qk_sum + unpacked(back_qk, send_list[turn])
        grad_value_sum = grad_value_sum + unpacked(back_value, send_list[turn])
    grad_qk_rows = grad_qk_sum.astype(jnp.bfloat16)
    grad_value_rows = grad_value_sum.astype(jnp.bfloat16)
    grad_qk = inner_rows(normed_one, grad_qk_rows)
    grad_value = inner_rows(normed_one, grad_value_rows)
    grad_one = outer_cols(grad_qk_rows, m_qk) + outer_cols(grad_value_rows, m_value)
    grad_gain_attn = jnp.sum(grad_one * hat_one, axis=0)
    grad_bias_attn = jnp.sum(grad_one, axis=0)
    dx_second = dy_second + norm_back(grad_one, hat_one, inv_one, gain_one)
    s_qk, s_value, s_out, s_gattn, s_battn, s_gffn, s_bffn, s_up, s_bup, s_down, s_bdown = (
        lax.psum_scatter(grad_qk, "seq", scatter_dimension=0, tiled=True),
        lax.psum_scatter(grad_value, "seq", scatter_dimension=0, tiled=True),
        lax.psum_scatter(grad_out, "seq", scatter_dimension=0, tiled=True),
        lax.psum_scatter(grad_gain_attn, "seq", scatter_dimension=0, tiled=True),
        lax.psum_scatter(grad_bias_attn, "seq", scatter_dimension=0, tiled=True),
        lax.psum_scatter(grad_gain_ffn, "seq", scatter_dimension=0, tiled=True),
        lax.psum_scatter(grad_bias_ffn, "seq", scatter_dimension=0, tiled=True),
        lax.psum_scatter(grad_up, "seq", scatter_dimension=0, tiled=True),
        lax.psum_scatter(grad_bias_up, "seq", scatter_dimension=0, tiled=True),
        lax.psum_scatter(grad_down, "seq", scatter_dimension=0, tiled=True),
        lax.psum_scatter(grad_bias_down, "seq", scatter_dimension=0, tiled=True),
    )
    return (
        y_first,
        y_second,
        dx_first,
        dx_second,
        s_qk,
        s_value,
        s_out,
        s_gattn,
        s_battn,
        s_gffn,
        s_bffn,
        s_up,
        s_bup,
        s_down,
        s_bdown,
    )


CAP_ROWS = 16
PARTS = 8


def dot_nn(a, b):
    return lax.dot_general(a, b, (((1,), (0,)), ((), ())), preferred_element_type=F32)


def dot_nt(a, b):
    return lax.dot_general(a, b, (((1,), (1,)), ((), ())), preferred_element_type=F32)


def dot_tn(a, b):
    return lax.dot_general(a, b, (((0,), (0,)), ((), ())), preferred_element_type=F32)


def hot_rows(slot_row, slots):
    ids = lax.broadcasted_iota(jnp.int32, (slots, slot_row.shape[1]), 0).astype(F32)
    return jnp.where(ids == slot_row, 1.0, 0.0).astype(BF)


def hot_cols(slot_col, slots):
    ids = lax.broadcasted_iota(jnp.int32, (slot_col.shape[0], slots), 1).astype(F32)
    return jnp.where(ids == slot_col, 1.0, 0.0).astype(BF)


def key_factor(keys):
    wide = keys.astype(F32)
    return lax.rsqrt(jnp.sum(wide * wide, axis=1, keepdims=True)) * SCALE


def keep_columns(factors, ids, start, keys, id_column):
    shape = keys.shape
    factors[pl.ds(start, shape[0]), :] = jnp.broadcast_to(key_factor(keys), shape)
    ids[pl.ds(start, shape[0]), :] = jnp.broadcast_to(id_column, shape)


def pair_scores(raw, factor, key_ids, query_ids, query_starts):
    lane = lax.broadcasted_iota(jnp.int32, query_ids.shape, 1)
    first = jnp.where(lane < SPAN, query_ids, -1.0)
    second = jnp.where(lane >= SPAN, query_ids, -1.0)
    scores, masks = [], []
    for chunk, limits in enumerate((first, query_ids, second)):
        here = slice(chunk * SPAN, (chunk + 1) * SPAN)
        ids = key_ids[here]
        kept = (ids < limits) & (ids >= query_starts)
        score = jnp.where(kept, raw[here] * factor[here], -1000000000.0)
        if chunk > 0:
            score = jnp.where(ids == query_ids, -100000.0, score)
        scores.append(score)
        masks.append(kept)
    return scores, masks


def three_parts(wide):
    high = wide.astype(BF).astype(F32)
    rest = wide - high
    mid = rest.astype(BF).astype(F32)
    return high, mid, rest - mid


def forward_kernel(
    place,
    x_0,
    x_1,
    x_2,
    x_3,
    info,
    out_0,
    out_1,
    out_2,
    out_3,
    kept_rows,
    lanes,
    heads_out,
    factors,
    ids,
):
    blocks, tokens = info.shape[0], info.shape[2]
    slots = blocks * CAP_ROWS
    width = x_0.shape[1]
    pairs = tokens // (2 * SPAN)
    turn = place[0]
    rounds = ROUNDS

    for offset, rows in enumerate((x_0, x_1, x_2, x_3)):

        def pack(group, carry, offset=offset, rows=rows):
            source = group * rounds + lax.bitwise_xor(turn, offset)
            hot = hot_rows(info[source, 3:4, :], slots)
            start = pl.multiple_of(group * tokens, tokens)
            part = dot_nn(hot, rows[pl.ds(start, tokens), :]).astype(BF)
            lanes[:, pl.ds(source, 1)] = part.reshape(blocks, 1, CAP_ROWS, width)
            return carry

        lax.fori_loop(0, blocks // rounds, pack, 0, unroll=4)

    def place_rows(block, carry):
        cols = jnp.transpose(info[block])
        hot = hot_cols(cols[:, 2:3], slots)
        part = dot_nn(hot, lanes[block].reshape(slots, width)).astype(BF)
        start = pl.multiple_of(SPAN + block * tokens, SPAN)
        kept_rows[pl.ds(start, tokens), :] = part
        keep_columns(factors, ids, start, part[:, :HEAD_DIM], cols[:, 0:1])
        return carry

    lax.fori_loop(0, blocks, place_rows, 0, unroll=4)
    for held in (kept_rows, factors, ids):
        held[0:SPAN, :] = held[blocks * tokens : blocks * tokens + SPAN, :]
    heads_out[:, :, HEAD_DIM:] = jnp.zeros((blocks, tokens, width - HEAD_DIM), BF)

    def attend(block, carry):
        first = []
        for pair in range(pairs):
            start = pl.multiple_of(block * tokens + pair * 2 * SPAN, SPAN)
            rows = kept_rows[pl.ds(start, 3 * SPAN), :]
            raw = dot_nt(rows[:, :HEAD_DIM], rows[SPAN:, :HEAD_DIM])
            first.append((start, rows[:, HEAD_DIM:], raw))
        second = []
        lse = []
        for pair in range(pairs):
            start, values, raw = first[pair]
            here = slice(pair * 2 * SPAN, (pair + 1) * 2 * SPAN)
            scores, _ = pair_scores(
                raw,
                factors[pl.ds(start, 3 * SPAN), :],
                ids[pl.ds(start, 3 * SPAN), :],
                info[block, 0:1, here],
                info[block, 1:2, here],
            )
            top = jnp.max(
                jnp.maximum(jnp.maximum(scores[0], scores[1]), scores[2]), axis=0, keepdims=True
            )
            weights = [jnp.exp(score - top) for score in scores]
            total = jnp.sum(weights[0] + weights[1] + weights[2], axis=0, keepdims=True)
            scale = 1.0 / total
            second.append(jnp.concatenate([weight * scale for weight in weights]).astype(BF))
            lse.append(top + jnp.log(total))
        for pair in range(pairs):
            here = slice(pair * 2 * SPAN, (pair + 1) * 2 * SPAN)
            heads_out[block, here, :HEAD_DIM] = dot_tn(second[pair], first[pair][1]).astype(BF)
        high, mid, low = three_parts(jnp.concatenate(lse, axis=1))
        row = lax.broadcasted_iota(jnp.int32, (PARTS, tokens), 0)
        flat = jnp.where(row == 0, high, jnp.where(row == 1, mid, jnp.where(row == 2, low, 0.0)))
        heads_out[block, :, HEAD_DIM : HEAD_DIM + PARTS] = jnp.transpose(flat).astype(BF)
        return carry

    lax.fori_loop(0, blocks, attend, 0)

    def unplace(block, carry):
        hot = hot_rows(info[block, 2:3, :], slots)
        part = dot_nn(hot, heads_out[block]).astype(BF)
        lanes[:, pl.ds(block, 1)] = part.reshape(blocks, 1, CAP_ROWS, width)
        return carry

    lax.fori_loop(0, blocks, unplace, 0, unroll=4)

    for offset, out in enumerate((out_0, out_1, out_2, out_3)):

        def unpack(group, carry, offset=offset, out=out):
            source = group * rounds + lax.bitwise_xor(turn, offset)
            cols = jnp.transpose(info[source])
            hot = hot_cols(cols[:, 3:4], slots)
            part = dot_nn(hot, lanes[source].reshape(slots, width))
            out[group, 0:tokens, :] = part[:, :HEAD_DIM].astype(BF)
            flat = jnp.transpose(part[:, HEAD_DIM:])[0:PARTS, :].astype(BF)
            for piece in range(tokens // HEAD_DIM):
                first = tokens + piece * PARTS
                out[group, first : first + PARTS, :] = flat[
                    :, piece * HEAD_DIM : (piece + 1) * HEAD_DIM
                ]
            return carry

        lax.fori_loop(0, blocks // rounds, unpack, 0, unroll=4)


def tall_parts(ref, group, first, tokens):
    flat = jnp.concatenate(
        [
            ref[group, first + piece * PARTS : first + (piece + 1) * PARTS, :].astype(F32)
            for piece in range(tokens // HEAD_DIM)
        ],
        axis=1,
    )
    return jnp.transpose(flat)


def put_parts(ref, group, first, column):
    tokens = column.shape[0]
    high, mid, low = three_parts(column)
    lane = lax.broadcasted_iota(jnp.int32, (tokens, PARTS), 1)
    tall = jnp.where(lane == 0, high, jnp.where(lane == 1, mid, jnp.where(lane == 2, low, 0.0)))
    flat = jnp.transpose(tall).astype(BF)
    for piece in range(tokens // HEAD_DIM):
        at = first + piece * PARTS
        ref[group, at : at + PARTS, :] = flat[:, piece * HEAD_DIM : (piece + 1) * HEAD_DIM]


def combined(refs, group):
    tokens = refs[0].shape[1] // (HEAD_DIM + PARTS) * HEAD_DIM
    lse = []
    for ref in refs:
        tall = tall_parts(ref, group, tokens, tokens)
        lse.append(tall[:, 0:1] + tall[:, 1:2] + tall[:, 2:3])
    top = lse[0]
    for other in lse[1:]:
        top = jnp.maximum(top, other)
    weights = [jnp.exp(one - top) for one in lse]
    total = sum(weights[1:], weights[0])
    scale = 1.0 / total
    rows = [
        (weight * scale) * ref[group, 0:tokens, :].astype(F32)
        for weight, ref in zip(weights, refs)
    ]
    return sum(rows[1:], rows[0]), top + jnp.log(total)


def pair_kernel(a, b, out):
    tokens = out.shape[1] // (HEAD_DIM + PARTS) * HEAD_DIM
    for group in range(out.shape[0]):
        rows, lse = combined((a, b), group)
        out[group, 0:tokens, :] = rows.astype(BF)
        put_parts(out, group, tokens, lse)


def final_kernel(a, b, c, mixed, total_lse):
    for group in range(mixed.shape[0]):
        rows, lse = combined((a, b, c), group)
        mixed[group] = rows.astype(BF)
        put_parts(total_lse, group, 0, lse)


def backward_kernel(
    place,
    g_0,
    g_1,
    g_2,
    g_3,
    l_0,
    l_1,
    l_2,
    l_3,
    kept_rows,
    info,
    out_0,
    out_1,
    out_2,
    out_3,
    lanes,
    sums,
    factors,
    ids,
    rows_in,
    stats,
):
    blocks, tokens = info.shape[0], info.shape[2]
    slots = blocks * CAP_ROWS
    width = kept_rows.shape[1]
    pairs = tokens // (2 * SPAN)

    for offset, grads, lse in ((0, g_0, l_0), (1, g_1, l_1), (2, g_2, l_2), (3, g_3, l_3)):

        def pack(group, carry, offset=offset, grads=grads, lse=lse):
            source = group * ROUNDS + lax.bitwise_xor(place[0], offset)
            hot = hot_rows(info[source, 3:4, :], slots)
            tall = [tall_parts(grads, group, tokens, tokens), tall_parts(lse, group, 0, tokens)]
            tall.append(jnp.zeros((tokens, HEAD_DIM - 2 * PARTS), F32))
            rows = jnp.concatenate(
                [grads[group, 0:tokens, :], jnp.concatenate(tall, axis=1).astype(BF)], axis=1
            )
            part = dot_nn(hot, rows).astype(BF)
            lanes[:, pl.ds(source, 1)] = part.reshape(blocks, 1, CAP_ROWS, width)
            return carry

        lax.fori_loop(0, blocks // ROUNDS, pack, 0, unroll=4)

    sums[0:SPAN, :] = jnp.zeros((SPAN, width), F32)

    def place_rows(block, carry):
        cols = jnp.transpose(info[block])
        hot = hot_cols(cols[:, 2:3], slots)
        part = dot_nn(hot, lanes[block].reshape(slots, width))
        rows_in[block] = part[:, :HEAD_DIM].astype(BF)
        flat = jnp.transpose(part[:, HEAD_DIM:])
        stats[block, 0:1, :] = flat[0:1] + flat[1:2] + flat[2:3]
        stats[block, 1:2, :] = flat[PARTS : PARTS + 1] + (
            flat[PARTS + 1 : PARTS + 2] + flat[PARTS + 2 : PARTS + 3]
        )
        start = pl.multiple_of(SPAN + block * tokens, SPAN)
        keys = kept_rows[pl.ds(start, tokens), :HEAD_DIM]
        keep_columns(factors, ids, start, keys, cols[:, 0:1])
        return carry

    lax.fori_loop(0, blocks, place_rows, 0, unroll=4)
    for held in (factors, ids):
        held[0:SPAN, :] = held[blocks * tokens : blocks * tokens + SPAN, :]

    def attend(block, carry):
        first = []
        for pair in range(pairs):
            start = pl.multiple_of(block * tokens + pair * 2 * SPAN, SPAN)
            here = slice(pair * 2 * SPAN, (pair + 1) * 2 * SPAN)
            rows = kept_rows[pl.ds(start, 3 * SPAN), :]
            keys = rows[:, :HEAD_DIM]
            queries = rows[SPAN:, :HEAD_DIM]
            grads = rows_in[block, here, :]
            raw = dot_nt(keys, queries)
            back = dot_nt(rows[:, HEAD_DIM:], grads)
            first.append((start, keys, queries, grads, raw, back))
        second = []
        for pair in range(pairs):
            start, keys, queries, grads, raw, back = first[pair]
            here = slice(pair * 2 * SPAN, (pair + 1) * 2 * SPAN)
            factor = factors[pl.ds(start, 3 * SPAN), :]
            scores, masks = pair_scores(
                raw,
                factor,
                ids[pl.ds(start, 3 * SPAN), :],
                info[block, 0:1, here],
                info[block, 1:2, here],
            )
            pull = stats[block, 0:1, here]
            total_lse = stats[block, 1:2, here]
            weights = [jnp.exp(score - total_lse) for score in scores]
            weights_all = jnp.concatenate(weights).astype(BF)
            grad_score = jnp.concatenate(
                [
                    jnp.where(
                        mask, weight * (back[chunk * SPAN : (chunk + 1) * SPAN] - pull), 0.0
                    )
                    for chunk, (mask, weight) in enumerate(zip(masks, weights))
                ]
            )
            slope = jnp.sum(grad_score * raw, axis=1, keepdims=True)
            drift = slope * (factor * factor * factor * HEAD_DIM) * keys.astype(F32)
            second.append(((grad_score * factor).astype(BF), weights_all, drift))
        for pair in range(pairs):
            start, keys, queries, grads = first[pair][:4]
            grad_raw, weights_all, drift = second[pair]
            grad_val = dot_nn(weights_all, grads)
            grad_key = dot_nn(grad_raw, queries) - drift
            grad_query = dot_tn(grad_raw, keys)
            sums[pl.ds(start, SPAN), :] += jnp.concatenate(
                [grad_key[:SPAN], grad_val[:SPAN]], axis=1
            )
            after = pl.multiple_of(start + SPAN, SPAN)
            sums[pl.ds(after, 2 * SPAN), :] = jnp.concatenate(
                [grad_query + grad_key[SPAN:], grad_val[SPAN:]], axis=1
            )
        return carry

    lax.fori_loop(0, blocks, attend, 0)
    sums[blocks * tokens : blocks * tokens + SPAN, :] += sums[0:SPAN, :]

    def unplace(block, carry):
        hot = hot_rows(info[block, 2:3, :], slots)
        start = pl.multiple_of(SPAN + block * tokens, SPAN)
        part = dot_nn(hot, sums[pl.ds(start, tokens), :].astype(BF)).astype(BF)
        lanes[:, pl.ds(block, 1)] = part.reshape(blocks, 1, CAP_ROWS, width)
        return carry

    lax.fori_loop(0, blocks, unplace, 0, unroll=4)

    for offset, out in enumerate((out_0, out_1, out_2, out_3)):

        def unpack(group, carry, offset=offset, out=out):
            source = group * ROUNDS + lax.bitwise_xor(place[0], offset)
            cols = jnp.transpose(info[source])
            hot = hot_cols(cols[:, 3:4], slots)
            start = pl.multiple_of(group * tokens, tokens)
            part = dot_nn(hot, lanes[source].reshape(slots, width))
            out[pl.ds(start, tokens), :] = part.astype(BF)
            return carry

        lax.fori_loop(0, blocks // ROUNDS, unpack, 0, unroll=4)


def in_vmem(count):
    return [pl.BlockSpec(memory_space=pltpu.VMEM)] * count


def run_kernel(kernel, name, operands, shapes, scratch, scalar):
    first = [pl.BlockSpec(memory_space=pltpu.SMEM)] if scalar else []
    return pl.pallas_call(
        kernel,
        out_shape=tuple(jax.ShapeDtypeStruct(shape, BF) for shape in shapes),
        in_specs=first + in_vmem(len(operands) - len(first)),
        out_specs=tuple(in_vmem(len(shapes))),
        scratch_shapes=[pltpu.VMEM(shape, dtype) for shape, dtype in scratch],
        compiler_params=pltpu.CompilerParams(vmem_limit_bytes=48 << 20),
        cost_estimate=pl.CostEstimate(
            flops=20 * 10**9 if scalar else 10**7,
            bytes_accessed=12 * 10**6 if scalar else 2 * 10**6,
            transcendentals=10**6 if scalar else 10**4,
        ),
        name=name,
    )(*operands)


def run_forward(turn, rows, info):
    blocks, _, tokens = info.shape
    width = rows[0].shape[1]
    tall = tokens + PARTS * tokens // HEAD_DIM
    return run_kernel(
        forward_kernel,
        "hash_forward",
        (turn, *rows, info),
        [(blocks // ROUNDS, tall, HEAD_DIM)] * ROUNDS + [(SPAN + blocks * tokens, width)],
        [((blocks, blocks, CAP_ROWS, width), BF), ((blocks, tokens, width), BF)]
        + [((SPAN + blocks * tokens, HEAD_DIM), F32)] * 2,
        True,
    )


def run_backward(turn, grads, lse, kept_rows, info):
    blocks, _, tokens = info.shape
    width = kept_rows.shape[1]
    return run_kernel(
        backward_kernel,
        "hash_backward",
        (turn, *grads, *lse, kept_rows, info),
        [(blocks * tokens // ROUNDS, width)] * ROUNDS,
        [((blocks, blocks, CAP_ROWS, width), BF), ((SPAN + blocks * tokens, width), F32)]
        + [((SPAN + blocks * tokens, HEAD_DIM), F32)] * 2
        + [((blocks, tokens, HEAD_DIM), BF), ((blocks, 8, tokens), F32)],
        True,
    )


def merge_pair(a, b):
    return run_kernel(pair_kernel, "merge_pair", (a, b), [a.shape], [], False)[0]


def merge_final(a, b, c):
    groups, tall, width = a.shape
    tokens = tall // (HEAD_DIM + PARTS) * HEAD_DIM
    shapes = [(groups, tokens, width), (groups, tall - tokens, width)]
    return run_kernel(final_kernel, "merge_final", (a, b, c), shapes, [], False)


def peers(mask):
    size = HEADS * ROUNDS
    return [(i, i ^ mask) for i in range(size)]


def swap(x, mask):
    return lax.ppermute(x, "seq", peers(mask))


def columns():
    return [[head * ROUNDS + turn for head in range(HEADS)] for turn in range(ROUNDS)]


def rows_of():
    return [[head * ROUNDS + turn for turn in range(ROUNDS)] for head in range(HEADS)]


def gather_group(x):
    side = swap(x, 2)
    return (x, swap(x, 1), side, swap(side, 1))


def sum_group(parts):
    near = parts[0] + swap(parts[1].astype(BF), 1).astype(F32)
    far = parts[2] + swap(parts[3].astype(BF), 1).astype(F32)
    return near + swap(far.astype(BF), 2).astype(F32)


def exchange(x, groups=None):
    return lax.all_to_all(
        x, "seq", split_axis=0, concat_axis=0, tiled=True, axis_index_groups=groups
    )


def rounded(x):
    return lax.reduce_precision(x, 8, 7)


def split_three(wide):
    high = rounded(wide)
    rest = wide - high
    mid = rounded(rest)
    return jnp.stack([high, mid, rest - mid])


def slots_sent(target, tokens, capacity):
    device = target // tokens
    early = jnp.arange(tokens)[None, :] < jnp.arange(tokens)[:, None]
    same = (device[:, None] == device[None, :]) & early
    return device * capacity + jnp.sum(same.astype(jnp.int32), axis=1)


def start_of(token_ids, doc_ends):
    ends = doc_ends[None, :]
    return jnp.max(jnp.where(ends <= token_ids[:, None], ends, 0), axis=1)


def shards_fast(
    x_first,
    x_second,
    w_qk,
    w_value,
    w_out,
    gain_attn,
    bias_attn,
    gain_ffn,
    bias_ffn,
    w_up,
    bias_up,
    w_down,
    bias_down,
    sort_order,
    inverse,
    lengths,
    dy_first,
    dy_second,
):
    devices = lax.axis_size("seq")
    tokens, features = x_first.shape
    capacity = 2 * tokens // devices
    shard = features // devices
    place = lax.axis_index("seq")
    doc_ends = jnp.cumsum(lengths)

    per_round = []
    vectors = rounded(
        jnp.concatenate([gain_attn, bias_attn, gain_ffn, bias_ffn, bias_up, bias_down])
    )
    vectors = jnp.pad(vectors, (0, 2 * tokens - vectors.shape[0])).reshape(2, tokens)
    for turn in range(ROUNDS):
        ids = sort_order[turn]
        rows = jnp.stack(
            [
                ids,
                start_of(ids, doc_ends),
                recv_slots(ids, tokens, capacity),
                slots_sent(inverse[turn], tokens, capacity),
            ]
        ).astype(F32)
        per_round.append(jnp.concatenate([rows, vectors, jnp.zeros((2, tokens), F32)]))
    info = jnp.tile(jnp.stack(per_round), (HEADS, 1, 1))
    info = exchange(info)
    got = info[:, 4:6].reshape(devices, 2 * tokens)

    def vector(first, size):
        return got[:, first : first + size].reshape(devices * size)

    gain_one, shift_one = vector(0, shard), vector(shard, shard)
    gain_two, shift_two = vector(2 * shard, shard), vector(3 * shard, shard)
    wide = bias_up.shape[0]
    b_up = vector(4 * shard, wide)
    b_down = vector(4 * shard + wide, shard)
    pair = jnp.stack(
        [w_qk.reshape(shard, HEADS, HEAD_DIM), w_value.reshape(shard, HEADS, HEAD_DIM)], axis=2
    ).reshape(shard, 2 * features)
    m_pair = lax.all_gather(pair.astype(BF), "seq", axis=0, tiled=True)
    half = HEADS * wide
    up_cols = jnp.transpose(
        w_up.astype(BF).reshape(shard, HEADS, ROUNDS, wide), (2, 0, 1, 3)
    ).reshape(ROUNDS, shard, half)
    out_rows = jnp.broadcast_to(w_out.astype(BF), (ROUNDS, shard, features))
    near_rows = exchange(jnp.concatenate([up_cols, out_rows], axis=2), rows_of())
    near_rows = near_rows.reshape(ROUNDS * shard, half + features)
    b_up = lax.dynamic_index_in_dim(
        b_up.reshape(HEADS, ROUNDS, wide), place % ROUNDS, axis=1, keepdims=False
    ).reshape(HEADS * wide)

    normed_one, hat_one, inv_one = layer_norm(x_second, gain_one, shift_one)
    grad_f = dy_second.astype(BF)
    normed_one, near_rows, grad_f_all = lax.optimization_barrier(
        (normed_one.astype(BF), near_rows, gather_group(grad_f))
    )
    grad_f_all = jnp.concatenate(grad_f_all)
    rows = linear(normed_one, m_pair).astype(BF)
    rows = jnp.transpose(rows.reshape(tokens, HEADS, 2 * HEAD_DIM), (1, 0, 2))
    own = exchange(rows, columns()).reshape(HEADS * tokens, 2 * HEAD_DIM)
    own, near_rows = lax.optimization_barrier((own, near_rows))
    m_ffn = lax.all_gather(
        jnp.concatenate([near_rows, w_down.astype(BF)], axis=1),
        "seq",
        axis=0,
        tiled=True,
        axis_index_groups=columns(),
    )
    m_up, m_out, m_down = (m_ffn[:, at : at + features] for at in (0, half, half + features))
    turn = (place % ROUNDS).astype(jnp.int32).reshape(1)
    *sent, kept_rows = run_forward(turn, gather_group(own), info)
    far = merge_pair(sent[2], swap(sent[3], 1))
    mixed, total_lse = merge_final(sent[0], swap(sent[1], 1), swap(far, 2))
    mixed = exchange(mixed, columns())
    grad_hidden = outer_cols(grad_f_all, m_down)
    mixed, normed_one, grad_hidden = lax.optimization_barrier((mixed, normed_one, grad_hidden))
    normed_col = lax.all_gather(
        normed_one, "seq", axis=0, tiled=True, axis_index_groups=columns()
    )
    mixed = jnp.transpose(mixed, (1, 0, 2)).reshape(tokens, features)
    y_first = x_first + linear(mixed, m_out)
    normed_two, hat_two, inv_two = layer_norm(y_first, gain_two, shift_two)
    normed_two = normed_two.astype(BF)
    normed_all = jnp.concatenate(gather_group(normed_two))
    pre_up = linear(normed_all, m_up) + b_up
    hidden, gelu_back = jax.vjp(partial(jax.nn.gelu, approximate=True), pre_up)
    hidden = hidden.astype(BF)
    branch = sum_group(linear(hidden, m_down).reshape(ROUNDS, tokens, features))
    y_second = x_second + (branch + b_down)
    grad_down = inner_rows(hidden, grad_f_all)
    grad_bias_down = jnp.sum(grad_f.astype(F32), axis=0)
    grad_pre = gelu_back(grad_hidden)[0].astype(BF)
    grad_up = inner_rows(normed_all, grad_pre)
    grad_bias_up = jnp.sum(grad_pre.astype(F32), axis=0)
    grad_two = sum_group(outer_cols(grad_pre, m_up).reshape(ROUNDS, tokens, features))
    grad_gain_ffn = jnp.sum(grad_two * hat_two, axis=0)
    grad_bias_ffn = jnp.sum(grad_two, axis=0)
    dx_first = dy_first + norm_back(grad_two, hat_two, inv_two, gain_two)
    grad_attn = dx_first.astype(BF)
    grad_out = inner_rows(mixed, grad_attn)
    fourth = features // ROUNDS
    grad_mixed = outer_cols(grad_attn, m_out).astype(BF)
    pull = jnp.sum(
        (grad_mixed.astype(F32) * mixed.astype(F32)).reshape(tokens, HEADS, HEAD_DIM), axis=-1
    )
    parts = split_three(jnp.transpose(pull))
    parts = jnp.pad(parts, ((0, PARTS - 3), (0, 0), (0, 0)))
    parts = jnp.transpose(parts.reshape(PARTS, HEADS, -1, HEAD_DIM), (1, 2, 0, 3))
    parts = parts.reshape(HEADS, -1, HEAD_DIM).astype(BF)
    grad_mixed = jnp.transpose(grad_mixed.reshape(tokens, HEADS, HEAD_DIM), (1, 0, 2))
    grad_mixed = exchange(jnp.concatenate([grad_mixed, parts], axis=1), columns())
    grad_out = sum_group(
        [
            lax.dynamic_slice_in_dim(grad_out, ((place % ROUNDS) ^ near) * fourth, fourth, axis=1)
            for near in range(ROUNDS)
        ]
    )
    merged = jnp.concatenate([x.astype(BF) for x in (grad_up, grad_out, grad_down)], axis=1)
    grad_mixed, merged = lax.optimization_barrier((grad_mixed, merged))
    merged = lax.psum_scatter(
        merged, "seq", scatter_dimension=0, tiled=True, axis_index_groups=columns()
    )
    s_down = merged[:, half + fourth :].astype(F32)
    merged = merged[:, : half + fourth].reshape(ROUNDS, shard, -1)
    s_up = jnp.zeros((shard, HEADS, ROUNDS, wide), F32)
    s_out = jnp.zeros((shard, features), F32)
    for near in range(ROUNDS):
        peer = (place % ROUNDS) ^ near
        piece = lax.dynamic_index_in_dim(merged, peer, axis=0, keepdims=False)
        piece = (swap(piece, near) if near else piece).astype(F32)
        s_up = lax.dynamic_update_slice(
            s_up, piece[:, :half].reshape(shard, HEADS, 1, wide), (0, 0, peer, 0)
        )
        s_out = lax.dynamic_update_slice(s_out, piece[:, half:], (0, peer * fourth))
    s_up = s_up.reshape(shard, ROUNDS * half)

    grad_head = run_backward(
        turn, gather_group(grad_mixed), gather_group(total_lse), kept_rows, info
    )
    grad_head = sum_group([x.astype(F32) for x in grad_head]).astype(BF)
    grad_rows = exchange(grad_head.reshape(HEADS, tokens, 2 * HEAD_DIM), columns())
    s_pair = inner_rows(normed_col, grad_head).astype(BF).reshape(devices, shard, 2 * HEAD_DIM)
    grad_rows, s_pair = lax.optimization_barrier((grad_rows, s_pair))
    grad_rows = jnp.transpose(grad_rows, (1, 0, 2)).reshape(tokens, 2 * features)
    s_pair = exchange(s_pair)
    s_pair = jnp.sum(
        s_pair.reshape(HEADS, ROUNDS, shard, 2, HEAD_DIM).astype(F32), axis=1
    ).transpose(2, 1, 0, 3)
    s_qk = s_pair[0].reshape(shard, features)
    s_value = s_pair[1].reshape(shard, features)
    grad_one = outer_cols(grad_rows, m_pair)
    grad_gain_attn = jnp.sum(grad_one * hat_one, axis=0)
    grad_bias_attn = jnp.sum(grad_one, axis=0)
    dx_second = dy_second + norm_back(grad_one, hat_one, inv_one, gain_one)
    is_mine = (jnp.arange(ROUNDS) == place % ROUNDS).astype(F32)
    grad_bias_up = grad_bias_up.reshape(HEADS, 1, wide) * is_mine[None, :, None]
    small = jnp.concatenate(
        [
            grad_gain_attn.reshape(devices, -1),
            grad_bias_attn.reshape(devices, -1),
            grad_gain_ffn.reshape(devices, -1),
            grad_bias_ffn.reshape(devices, -1),
            grad_bias_up.reshape(devices, -1),
            grad_bias_down.reshape(devices, -1),
        ],
        axis=1,
    )
    small, s_qk, s_value = lax.optimization_barrier((small, s_qk, s_value))
    small = jnp.sum(exchange(small[:, None]), axis=(0, 1))
    s_gattn, s_battn, s_gffn, s_bffn = (small[i * shard : (i + 1) * shard] for i in range(4))
    s_bup = small[4 * shard : 4 * shard + wide]
    s_bdown = small[4 * shard + wide :]
    return (
        y_first,
        y_second,
        dx_first,
        dx_second,
        s_qk,
        s_value,
        s_out,
        s_gattn,
        s_battn,
        s_gffn,
        s_bffn,
        s_up,
        s_bup,
        s_down,
        s_bdown,
    )


def solution(mesh):
    in_specs = (
        P("seq", None),
        P("seq", None),
        P("seq", None),
        P("seq", None),
        P("seq", None),
        P("seq"),
        P("seq"),
        P("seq"),
        P("seq"),
        P("seq", None),
        P("seq"),
        P("seq", None),
        P("seq"),
        P(None, "seq"),
        P(None, "seq"),
        P(),
        P("seq", None),
        P("seq", None),
    )
    out_specs = (
        P("seq", None),
        P("seq", None),
        P("seq", None),
        P("seq", None),
        P("seq", None),
        P("seq", None),
        P("seq", None),
        P("seq"),
        P("seq"),
        P("seq"),
        P("seq"),
        P("seq", None),
        P("seq"),
        P("seq", None),
        P("seq"),
    )
    fast = mesh.shape["seq"] == HEADS * ROUNDS
    return jax.shard_map(shards_fast if fast else shards, mesh=mesh, in_specs=in_specs, out_specs=out_specs, check_vma=False)
```

```python
from functools import partial
import math

import jax
import jax.numpy as jnp
from jax import lax
from jax.experimental import pallas as pl
from jax.experimental.layout import Layout, with_layout_constraint
from jax.experimental.pallas import tpu as pltpu
from jax.sharding import PartitionSpec as P

HEADS = 8
HEAD_DIM = 128
SPAN = 64
ROUNDS = 4

EPSILON = 1e-05
SCALE = 1.0 / math.sqrt(HEAD_DIM)
BF = jnp.bfloat16
F32 = jnp.float32


def shifted(x, axis, by):
    size = lax.axis_size(axis)
    return lax.ppermute(x, axis, [(i, (i + by) % size) for i in range(size)])


def as_sent(x):
    return jax.tree.map(lambda a: a.astype(jnp.bfloat16) if a.dtype == jnp.float32 else a, x)


def layer_norm(inputs, norm_gain, norm_shift):
    centered = inputs - jnp.mean(inputs, axis=-1, keepdims=True)
    inv_std = lax.rsqrt(jnp.mean(centered * centered, axis=-1, keepdims=True) + EPSILON)
    normed = centered * inv_std
    return (normed * norm_gain + norm_shift, normed, inv_std)


def norm_back(grad_rows, normed, inv_std, norm_gain):
    grad_hat = grad_rows * norm_gain
    return inv_std * (
        grad_hat
        - jnp.mean(grad_hat, axis=-1, keepdims=True)
        - normed * jnp.mean(grad_hat * normed, axis=-1, keepdims=True)
    )


def linear(matrix_a, matrix_b):
    return jnp.dot(matrix_a, matrix_b, preferred_element_type=jnp.float32)


def inner_rows(matrix_a, matrix_b):
    return lax.dot_general(
        matrix_a, matrix_b, (((0,), (0,)), ((), ())), preferred_element_type=jnp.float32
    )


def outer_cols(matrix_a, matrix_b):
    return lax.dot_general(
        matrix_a, matrix_b, (((1,), (1,)), ((), ())), preferred_element_type=jnp.float32
    )


def segment_of(token_ids, doc_ends):
    return jnp.sum((token_ids[:, None] >= doc_ends[None, :]).astype(jnp.int32), axis=1)


def send_slots(target, tokens, devices, capacity):
    device = target // tokens
    onehot = (device[:, None] == jnp.arange(devices, dtype=jnp.int32)[None, :]).astype(jnp.int32)
    rank_in = jnp.sum(jnp.cumsum(onehot, axis=0) * onehot, axis=1) - 1
    return device * capacity + rank_in


def recv_slots(source_ids, tokens, capacity):
    device = source_ids // tokens
    earlier = (device[:, None] == device[None, :]) & (source_ids[None, :] < source_ids[:, None])
    return device * capacity + jnp.sum(earlier.astype(jnp.int32), axis=1)


def packed(inputs, slot_ids, devices, capacity):
    filled = (
        jnp.zeros((devices * capacity,) + inputs.shape[1:], inputs.dtype).at[slot_ids].set(inputs)
    )
    return filled.reshape((devices, capacity) + inputs.shape[1:])


def unpacked(received, slot_ids):
    return received.reshape((-1,) + received.shape[2:])[slot_ids]


def spanned(inputs, before):
    blocks = inputs.shape[0] // SPAN
    current = inputs.reshape((blocks, SPAN) + inputs.shape[1:])
    earlier = jnp.concatenate([before[None], current[:-1]], axis=0)
    return (current, jnp.concatenate([earlier, current], axis=1))


def arrange(got_qk, got_value, recv_slot):
    sorted_qk = unpacked(got_qk, recv_slot)
    sorted_value = unpacked(got_value, recv_slot)
    last_block = jnp.stack([sorted_qk[-SPAN:], sorted_value[-SPAN:]])
    return (sorted_qk, sorted_value, last_block)


def score_parts(sorted_rows, query_ids, before_ids, doc_ends):
    sorted_qk, sorted_value, before_qk, before_value = sorted_rows
    current, key_rows = spanned(sorted_qk, before_qk)
    _, value_keys = spanned(sorted_value, before_value)
    current_ids, key_ids = spanned(query_ids, before_ids)
    current_seg, key_seg = spanned(
        segment_of(query_ids, doc_ends), segment_of(before_ids, doc_ends)
    )
    blocks = current.shape[0]
    q_heads = current.reshape(blocks, SPAN, HEADS, HEAD_DIM)
    k_heads = key_rows.reshape(blocks, 2 * SPAN, HEADS, HEAD_DIM)
    v_heads = value_keys.reshape(blocks, 2 * SPAN, HEADS, HEAD_DIM)
    raw_dots = jnp.einsum("gihd,gjhd->ghij", q_heads, k_heads, preferred_element_type=jnp.float32)
    k_float = k_heads.astype(jnp.float32)
    key_norm = lax.rsqrt(jnp.sum(k_float * k_float, axis=-1))
    factor = jnp.transpose(key_norm, (0, 2, 1))[:, :, None, :] / math.sqrt(HEAD_DIM)
    allowed = (
        (key_ids[:, None, :] <= current_ids[:, :, None])
        & (key_seg[:, None, :] == current_seg[:, :, None])
    )[:, None]
    itself = (key_ids[:, None, :] == current_ids[:, :, None])[:, None]
    scores = jnp.where(itself, -100000.0, jnp.where(allowed, raw_dots * factor, -1000000000.0))
    log_total = jax.nn.logsumexp(scores, axis=-1)
    attn_probs = jnp.exp(scores - log_total[..., None])
    kept_mask = allowed & jnp.logical_not(itself)
    return (
        q_heads,
        k_heads,
        v_heads,
        k_float,
        key_norm,
        factor,
        kept_mask,
        raw_dots,
        attn_probs,
        log_total,
    )


def attend_out(pieces):
    (
        q_heads,
        k_heads,
        v_heads,
        k_float,
        key_norm,
        factor,
        kept_mask,
        raw_dots,
        attn_probs,
        log_total,
    ) = pieces
    blocks = q_heads.shape[0]
    out_heads = jnp.einsum(
        "ghij,gjhd->gihd",
        attn_probs.astype(jnp.bfloat16),
        v_heads,
        preferred_element_type=jnp.float32,
    )
    return (
        out_heads.reshape(blocks * SPAN, -1),
        jnp.transpose(log_total, (0, 2, 1)).reshape(blocks * SPAN, HEADS),
    )


def attend_back(pieces, grad_rows, grad_total):
    (
        q_heads,
        k_heads,
        v_heads,
        k_float,
        key_norm,
        factor,
        kept_mask,
        raw_dots,
        attn_probs,
        log_total,
    ) = pieces
    blocks = q_heads.shape[0]
    grad_heads = grad_rows.astype(jnp.bfloat16).reshape(blocks, SPAN, HEADS, HEAD_DIM)
    grad_lse = jnp.transpose(grad_total.reshape(blocks, SPAN, HEADS), (0, 2, 1))
    grad_prob = jnp.einsum(
        "gihd,gjhd->ghij", grad_heads, v_heads, preferred_element_type=jnp.float32
    )
    grad_val = jnp.einsum(
        "ghij,gihd->gjhd",
        attn_probs.astype(jnp.bfloat16),
        grad_heads,
        preferred_element_type=jnp.float32,
    )
    row_dot = jnp.sum(attn_probs * grad_prob, axis=-1, keepdims=True)
    grad_score = jnp.where(kept_mask, attn_probs * (grad_prob - row_dot + grad_lse[..., None]), 0.0)
    grad_raw = (grad_score * factor).astype(jnp.bfloat16)
    grad_norm = jnp.transpose(jnp.sum(grad_score * raw_dots, axis=2), (0, 2, 1)) / math.sqrt(
        HEAD_DIM
    )
    norm_cube = key_norm * key_norm * key_norm
    grad_query = jnp.einsum(
        "ghij,gjhd->gihd", grad_raw, k_heads, preferred_element_type=jnp.float32
    )
    grad_key = (
        jnp.einsum("ghij,gihd->gjhd", grad_raw, q_heads, preferred_element_type=jnp.float32)
        - (grad_norm * norm_cube)[..., None] * k_float
    )
    return (
        grad_query.reshape(blocks, SPAN, -1),
        grad_key.reshape(blocks, 2 * SPAN, -1),
        grad_val.reshape(blocks, 2 * SPAN, -1),
    )


def shards(
    x_first,
    x_second,
    w_qk,
    w_value,
    w_out,
    gain_attn,
    bias_attn,
    gain_ffn,
    bias_ffn,
    w_up,
    bias_up,
    w_down,
    bias_down,
    sort_order,
    inverse,
    lengths,
    dy_first,
    dy_second,
):
    devices = lax.axis_size("seq")
    tokens = x_first.shape[0]
    capacity = 2 * tokens // devices
    gathered = (
        lax.all_gather(w_qk.astype(jnp.bfloat16), "seq", axis=0, tiled=True),
        lax.all_gather(w_value.astype(jnp.bfloat16), "seq", axis=0, tiled=True),
        lax.all_gather(w_out.astype(jnp.bfloat16), "seq", axis=0, tiled=True),
        lax.all_gather(gain_attn.astype(jnp.bfloat16), "seq", axis=0, tiled=True),
        lax.all_gather(bias_attn.astype(jnp.bfloat16), "seq", axis=0, tiled=True),
        lax.all_gather(gain_ffn.astype(jnp.bfloat16), "seq", axis=0, tiled=True),
        lax.all_gather(bias_ffn.astype(jnp.bfloat16), "seq", axis=0, tiled=True),
        lax.all_gather(w_up.astype(jnp.bfloat16), "seq", axis=0, tiled=True),
        lax.all_gather(bias_up.astype(jnp.bfloat16), "seq", axis=0, tiled=True),
        lax.all_gather(w_down.astype(jnp.bfloat16), "seq", axis=0, tiled=True),
        lax.all_gather(bias_down.astype(jnp.bfloat16), "seq", axis=0, tiled=True),
    )
    m_qk, m_value, m_out, g_attn, b_attn, g_ffn, b_ffn, m_up, b_up, m_down, b_down = gathered
    gain_one = g_attn.astype(jnp.float32)
    gain_two = g_ffn.astype(jnp.float32)
    doc_ends = jnp.cumsum(lengths)
    send_list = [send_slots(inverse[turn], tokens, devices, capacity) for turn in range(ROUNDS)]
    recv_list = [recv_slots(sort_order[turn], tokens, capacity) for turn in range(ROUNDS)]
    before_ids = shifted(sort_order[:, tokens - SPAN :], "seq", 1)
    normed_one, hat_one, inv_one = layer_norm(x_second, gain_one, b_attn.astype(jnp.float32))
    normed_one = normed_one.astype(jnp.bfloat16)
    qk_rows = linear(normed_one, m_qk).astype(jnp.bfloat16)
    value_rows = linear(normed_one, m_value).astype(jnp.bfloat16)
    stashed = []
    round_outs = []
    round_lse = []
    for turn in range(ROUNDS):
        got_qk, got_value = (
            lax.all_to_all(
                packed(qk_rows, send_list[turn], devices, capacity),
                "seq",
                split_axis=0,
                concat_axis=0,
                tiled=True,
            ),
            lax.all_to_all(
                packed(value_rows, send_list[turn], devices, capacity),
                "seq",
                split_axis=0,
                concat_axis=0,
                tiled=True,
            ),
        )
        sorted_qk, sorted_value, last_block = arrange(got_qk, got_value, recv_list[turn])
        before_block = shifted(last_block, "seq", 1)
        sorted_rows = (sorted_qk, sorted_value, before_block[0], before_block[1])
        pieces = score_parts(sorted_rows, sort_order[turn], before_ids[turn], doc_ends)
        out_sorted, lse_sorted = attend_out(pieces)
        back_out, back_lse = (
            lax.all_to_all(
                packed(out_sorted, recv_list[turn], devices, capacity),
                "seq",
                split_axis=0,
                concat_axis=0,
                tiled=True,
            ),
            lax.all_to_all(
                packed(lse_sorted, recv_list[turn], devices, capacity),
                "seq",
                split_axis=0,
                concat_axis=0,
                tiled=True,
            ),
        )
        round_outs.append(unpacked(back_out, send_list[turn]))
        round_lse.append(unpacked(back_lse, send_list[turn]))
        stashed.append(sorted_rows)
    lse_all = jnp.stack(round_lse)
    out_all = jnp.stack(round_outs).reshape(ROUNDS, tokens, HEADS, HEAD_DIM)
    merge = jnp.exp(lse_all - jax.nn.logsumexp(lse_all, axis=0))
    mixed = jnp.sum(merge[..., None] * out_all, axis=0).reshape(tokens, -1).astype(jnp.bfloat16)
    y_first = x_first + linear(mixed, m_out)
    normed_two, hat_two, inv_two = layer_norm(y_first, gain_two, b_ffn.astype(jnp.float32))
    normed_two = normed_two.astype(jnp.bfloat16)
    pre_up = linear(normed_two, m_up) + b_up.astype(jnp.float32)
    hidden, gelu_back = jax.vjp(partial(jax.nn.gelu, approximate=True), pre_up)
    hidden = hidden.astype(jnp.bfloat16)
    y_second = x_second + (linear(hidden, m_down) + b_down.astype(jnp.float32))
    grad_f = dy_second.astype(jnp.bfloat16)
    grad_down = inner_rows(hidden, grad_f)
    grad_bias_down = jnp.sum(grad_f.astype(jnp.float32), axis=0)
    grad_pre = gelu_back(outer_cols(grad_f, m_down))[0].astype(jnp.bfloat16)
    grad_up = inner_rows(normed_two, grad_pre)
    grad_bias_up = jnp.sum(grad_pre.astype(jnp.float32), axis=0)
    grad_two = outer_cols(grad_pre, m_up)
    grad_gain_ffn = jnp.sum(grad_two * hat_two, axis=0)
    grad_bias_ffn = jnp.sum(grad_two, axis=0)
    dx_first = dy_first + norm_back(grad_two, hat_two, inv_two, gain_two)
    grad_attn = dx_first.astype(jnp.bfloat16)
    grad_out = inner_rows(mixed, grad_attn)
    grad_mixed = outer_cols(grad_attn, m_out).reshape(tokens, HEADS, HEAD_DIM)
    along = jnp.sum(grad_mixed[None] * out_all, axis=-1)
    grad_lse_all = merge * (along - jnp.sum(merge * along, axis=0, keepdims=True))
    grad_qk_sum = jnp.zeros((tokens, HEADS * HEAD_DIM), jnp.float32)
    grad_value_sum = jnp.zeros((tokens, HEADS * HEAD_DIM), jnp.float32)
    for turn in range(ROUNDS):
        grad_round = (merge[turn][..., None] * grad_mixed).reshape(tokens, -1)
        got_out, got_lse = (
            lax.all_to_all(
                packed(grad_round, send_list[turn], devices, capacity),
                "seq",
                split_axis=0,
                concat_axis=0,
                tiled=True,
            ),
            lax.all_to_all(
                packed(grad_lse_all[turn], send_list[turn], devices, capacity),
                "seq",
                split_axis=0,
                concat_axis=0,
                tiled=True,
            ),
        )
        sorted_grad_out = unpacked(got_out, recv_list[turn])
        sorted_grad_lse = unpacked(got_lse, recv_list[turn])
        sorted_rows = stashed[turn]
        pieces = score_parts(sorted_rows, sort_order[turn], before_ids[turn], doc_ends)
        grad_query, grad_key, grad_val = attend_back(pieces, sorted_grad_out, sorted_grad_lse)
        spill = shifted(
            jnp.stack([grad_key[0, :SPAN], grad_val[0, :SPAN]]).astype(jnp.bfloat16), "seq", -1
        ).astype(jnp.float32)
        key_add = jnp.concatenate([grad_key[1:, :SPAN], spill[0][None]], axis=0)
        value_add = jnp.concatenate([grad_val[1:, :SPAN], spill[1][None]], axis=0)
        sorted_grad_qk = (grad_query + grad_key[:, SPAN:] + key_add).reshape(tokens, -1)
        sorted_grad_value = (grad_val[:, SPAN:] + value_add).reshape(tokens, -1)
        back_qk, back_value = (
            lax.all_to_all(
                as_sent(packed(sorted_grad_qk, recv_list[turn], devices, capacity)),
                "seq",
                split_axis=0,
                concat_axis=0,
                tiled=True,
            ),
            lax.all_to_all(
                as_sent(packed(sorted_grad_value, recv_list[turn], devices, capacity)),
                "seq",
                split_axis=0,
                concat_axis=0,
                tiled=True,
            ),
        )
        grad_qk_sum = grad_qk_sum + unpacked(back_qk, send_list[turn])
        grad_value_sum = grad_value_sum + unpacked(back_value, send_list[turn])
    grad_qk_rows = grad_qk_sum.astype(jnp.bfloat16)
    grad_value_rows = grad_value_sum.astype(jnp.bfloat16)
    grad_qk = inner_rows(normed_one, grad_qk_rows)
    grad_value = inner_rows(normed_one, grad_value_rows)
    grad_one = outer_cols(grad_qk_rows, m_qk) + outer_cols(grad_value_rows, m_value)
    grad_gain_attn = jnp.sum(grad_one * hat_one, axis=0)
    grad_bias_attn = jnp.sum(grad_one, axis=0)
    dx_second = dy_second + norm_back(grad_one, hat_one, inv_one, gain_one)
    s_qk, s_value, s_out, s_gattn, s_battn, s_gffn, s_bffn, s_up, s_bup, s_down, s_bdown = (
        lax.psum_scatter(grad_qk, "seq", scatter_dimension=0, tiled=True),
        lax.psum_scatter(grad_value, "seq", scatter_dimension=0, tiled=True),
        lax.psum_scatter(grad_out, "seq", scatter_dimension=0, tiled=True),
        lax.psum_scatter(grad_gain_attn, "seq", scatter_dimension=0, tiled=True),
        lax.psum_scatter(grad_bias_attn, "seq", scatter_dimension=0, tiled=True),
        lax.psum_scatter(grad_gain_ffn, "seq", scatter_dimension=0, tiled=True),
        lax.psum_scatter(grad_bias_ffn, "seq", scatter_dimension=0, tiled=True),
        lax.psum_scatter(grad_up, "seq", scatter_dimension=0, tiled=True),
        lax.psum_scatter(grad_bias_up, "seq", scatter_dimension=0, tiled=True),
        lax.psum_scatter(grad_down, "seq", scatter_dimension=0, tiled=True),
        lax.psum_scatter(grad_bias_down, "seq", scatter_dimension=0, tiled=True),
    )
    return (
        y_first,
        y_second,
        dx_first,
        dx_second,
        s_qk,
        s_value,
        s_out,
        s_gattn,
        s_battn,
        s_gffn,
        s_bffn,
        s_up,
        s_bup,
        s_down,
        s_bdown,
    )


CAP_ROWS = 16
FORWARD_BATCH = 4
BACKWARD_BATCH = 2
PARTS = 8


def dot_nn(a, b):
    return lax.dot_general(a, b, (((1,), (0,)), ((), ())), preferred_element_type=F32)


def dot_nt(a, b):
    return lax.dot_general(a, b, (((1,), (1,)), ((), ())), preferred_element_type=F32)


def dot_tn(a, b):
    return lax.dot_general(a, b, (((0,), (0,)), ((), ())), preferred_element_type=F32)


def hot_rows(slot_row, slots):
    ids = lax.broadcasted_iota(jnp.int32, (slots, slot_row.shape[1]), 0).astype(F32)
    return jnp.where(ids == slot_row, 1.0, 0.0).astype(BF)


def hot_cols(slot_col, slots):
    ids = lax.broadcasted_iota(jnp.int32, (slot_col.shape[0], slots), 1).astype(F32)
    return jnp.where(ids == slot_col, 1.0, 0.0).astype(BF)


def keep_columns(factors, ids, start, keys, cols):
    rows = keys.shape[0]
    wide = keys.astype(F32)
    square = wide * wide
    high = square.astype(BF)
    low = (square - high.astype(F32)).astype(BF)
    ones = jnp.ones((HEAD_DIM, HEAD_DIM), BF)
    total = dot_nn(high, ones) + dot_nn(low, ones)
    factors[pl.ds(start, rows), :] = lax.rsqrt(total) * SCALE
    pick = lax.broadcasted_iota(jnp.int32, (PARTS, HEAD_DIM), 0) >= 6
    ids[pl.ds(start, rows), :] = dot_nn(cols.astype(BF), jnp.where(pick, 1.0, 0.0).astype(BF))


def pair_scores(raw, factor, key_ids, query_ids, query_starts):
    lane = lax.broadcasted_iota(jnp.int32, query_ids.shape, 1)
    first = jnp.where(lane < SPAN, query_ids, -1.0)
    second = jnp.where(lane >= SPAN, query_ids, -1.0)
    scores, masks = [], []
    for chunk, limits in enumerate((first, query_ids, second)):
        here = slice(chunk * SPAN, (chunk + 1) * SPAN)
        ids = key_ids[here]
        kept = (ids < limits) & (ids >= query_starts)
        score = jnp.where(kept, raw[here] * factor[here], -1000000000.0)
        if chunk > 0:
            score = jnp.where(ids == query_ids, -100000.0, score)
        scores.append(score)
        masks.append(kept)
    return scores, masks


def three_parts(wide):
    high = wide.astype(BF).astype(F32)
    rest = wide - high
    mid = rest.astype(BF).astype(F32)
    return high, mid, rest - mid


def forward_kernel(
    place,
    x_0,
    x_1,
    x_2,
    x_3,
    info,
    out_0,
    out_1,
    out_2,
    out_3,
    kept_rows,
    lanes,
    heads_out,
    factors,
    ids,
):
    blocks, tokens = info.shape[0], info.shape[2]
    slots = blocks * CAP_ROWS
    width = x_0.shape[1]
    pairs = tokens // (2 * SPAN)
    turn = place[0]
    rounds = ROUNDS

    for offset, rows in enumerate((x_0, x_1, x_2, x_3)):

        def pack(group, carry, offset=offset, rows=rows):
            source = group * rounds + lax.bitwise_xor(turn, offset)
            hot = hot_rows(info[source, 3:4, :], slots)
            start = pl.multiple_of(group * tokens, tokens)
            part = dot_nn(hot, rows[pl.ds(start, tokens), :]).astype(BF)
            lanes[:, pl.ds(source, 1)] = part.reshape(blocks, 1, CAP_ROWS, width)
            return carry

        lax.fori_loop(0, blocks // rounds, pack, 0, unroll=4)

    def place_rows(block, carry):
        cols = jnp.transpose(info[block])
        hot = hot_cols(cols[:, 2:3], slots)
        part = dot_nn(hot, lanes[block].reshape(slots, width)).astype(BF)
        start = pl.multiple_of(SPAN + block * tokens, SPAN)
        kept_rows[pl.ds(start, tokens), :] = part
        keep_columns(factors, ids, start, part[:, :HEAD_DIM], cols)
        return carry

    lax.fori_loop(0, blocks, place_rows, 0, unroll=4)
    for held in (kept_rows, factors, ids):
        held[0:SPAN, :] = held[blocks * tokens : blocks * tokens + SPAN, :]
    heads_out[:, :, HEAD_DIM:] = jnp.zeros((blocks, tokens, width - HEAD_DIM), BF)

    def attend(step, carry):
        todo = [(step * FORWARD_BATCH + at // pairs, at % pairs) for at in range(FORWARD_BATCH * pairs)]
        first = []
        for block, pair in todo:
            start = pl.multiple_of(block * tokens + pair * 2 * SPAN, SPAN)
            rows = kept_rows[pl.ds(start, 3 * SPAN), :]
            raw = dot_nt(rows[:, :HEAD_DIM], rows[SPAN:, :HEAD_DIM])
            first.append((start, rows[:, HEAD_DIM:], raw))
        second = []
        lse = []
        for (block, pair), (start, values, raw) in zip(todo, first):
            here = slice(pair * 2 * SPAN, (pair + 1) * 2 * SPAN)
            scores, _ = pair_scores(
                raw,
                factors[pl.ds(start, 3 * SPAN), :],
                ids[pl.ds(start, 3 * SPAN), :],
                info[block, 0:1, here],
                info[block, 1:2, here],
            )
            top = jnp.max(
                jnp.maximum(jnp.maximum(scores[0], scores[1]), scores[2]), axis=0, keepdims=True
            )
            weights = [jnp.exp(score - top) for score in scores]
            total = jnp.sum(weights[0] + weights[1] + weights[2], axis=0, keepdims=True)
            scale = 1.0 / total
            second.append(jnp.concatenate([weight * scale for weight in weights]).astype(BF))
            lse.append(top + jnp.log(total))
        for (block, pair), (start, values, raw), probs in zip(todo, first, second):
            here = slice(pair * 2 * SPAN, (pair + 1) * 2 * SPAN)
            heads_out[block, here, :HEAD_DIM] = dot_tn(probs, values).astype(BF)
        row = lax.broadcasted_iota(jnp.int32, (PARTS, tokens), 0)
        for at in range(FORWARD_BATCH):
            block = step * FORWARD_BATCH + at
            high, mid, low = three_parts(
                jnp.concatenate(lse[at * pairs : (at + 1) * pairs], axis=1)
            )
            flat = jnp.where(
                row == 0, high, jnp.where(row == 1, mid, jnp.where(row == 2, low, 0.0))
            )
            heads_out[block, :, HEAD_DIM : HEAD_DIM + PARTS] = jnp.transpose(flat).astype(BF)
        return carry

    lax.fori_loop(0, blocks // FORWARD_BATCH, attend, 0)

    def unplace(block, carry):
        hot = hot_rows(info[block, 2:3, :], slots)
        part = dot_nn(hot, heads_out[block]).astype(BF)
        lanes[:, pl.ds(block, 1)] = part.reshape(blocks, 1, CAP_ROWS, width)
        return carry

    lax.fori_loop(0, blocks, unplace, 0, unroll=4)

    for offset, out in enumerate((out_0, out_1, out_2, out_3)):

        def unpack(group, carry, offset=offset, out=out):
            source = group * rounds + lax.bitwise_xor(turn, offset)
            cols = jnp.transpose(info[source])
            hot = hot_cols(cols[:, 3:4], slots)
            part = dot_nn(hot, lanes[source].reshape(slots, width))
            out[group, 0:tokens, :] = part[:, :HEAD_DIM].astype(BF)
            flat = jnp.transpose(part[:, HEAD_DIM:])[0:PARTS, :].astype(BF)
            for piece in range(tokens // HEAD_DIM):
                first = tokens + piece * PARTS
                out[group, first : first + PARTS, :] = flat[
                    :, piece * HEAD_DIM : (piece + 1) * HEAD_DIM
                ]
            return carry

        lax.fori_loop(0, blocks // rounds, unpack, 0, unroll=4)


def tall_parts(ref, group, first, tokens):
    flat = jnp.concatenate(
        [
            ref[group, first + piece * PARTS : first + (piece + 1) * PARTS, :].astype(F32)
            for piece in range(tokens // HEAD_DIM)
        ],
        axis=1,
    )
    return jnp.transpose(flat)


def put_parts(ref, group, first, column):
    tokens = column.shape[0]
    high, mid, low = three_parts(column)
    lane = lax.broadcasted_iota(jnp.int32, (tokens, PARTS), 1)
    tall = jnp.where(lane == 0, high, jnp.where(lane == 1, mid, jnp.where(lane == 2, low, 0.0)))
    flat = jnp.transpose(tall).astype(BF)
    for piece in range(tokens // HEAD_DIM):
        at = first + piece * PARTS
        ref[group, at : at + PARTS, :] = flat[:, piece * HEAD_DIM : (piece + 1) * HEAD_DIM]


def combined(refs, group):
    tokens = refs[0].shape[1] // (HEAD_DIM + PARTS) * HEAD_DIM
    lse = []
    for ref in refs:
        tall = tall_parts(ref, group, tokens, tokens)
        lse.append(tall[:, 0:1] + tall[:, 1:2] + tall[:, 2:3])
    top = lse[0]
    for other in lse[1:]:
        top = jnp.maximum(top, other)
    weights = [jnp.exp(one - top) for one in lse]
    total = sum(weights[1:], weights[0])
    scale = 1.0 / total
    rows = [
        (weight * scale) * ref[group, 0:tokens, :].astype(F32)
        for weight, ref in zip(weights, refs)
    ]
    return sum(rows[1:], rows[0]), top + jnp.log(total)


def pair_kernel(a, b, out):
    tokens = out.shape[1] // (HEAD_DIM + PARTS) * HEAD_DIM
    for group in range(out.shape[0]):
        rows, lse = combined((a, b), group)
        out[group, 0:tokens, :] = rows.astype(BF)
        put_parts(out, group, tokens, lse)


def final_kernel(a, b, c, mixed, total_lse):
    for group in range(mixed.shape[0]):
        rows, lse = combined((a, b, c), group)
        mixed[group] = rows.astype(BF)
        put_parts(total_lse, group, 0, lse)


def backward_kernel(
    place,
    g_0,
    g_1,
    g_2,
    g_3,
    l_0,
    l_1,
    l_2,
    l_3,
    kept_rows,
    info,
    out_0,
    out_1,
    out_2,
    out_3,
    lanes,
    sums,
    factors,
    ids,
    rows_in,
    stats,
):
    blocks, tokens = info.shape[0], info.shape[2]
    slots = blocks * CAP_ROWS
    width = kept_rows.shape[1]
    pairs = tokens // (2 * SPAN)

    for offset, grads, lse in ((0, g_0, l_0), (1, g_1, l_1), (2, g_2, l_2), (3, g_3, l_3)):

        def pack(group, carry, offset=offset, grads=grads, lse=lse):
            source = group * ROUNDS + lax.bitwise_xor(place[0], offset)
            hot = hot_rows(info[source, 3:4, :], slots)
            tall = [tall_parts(grads, group, tokens, tokens), tall_parts(lse, group, 0, tokens)]
            tall.append(jnp.zeros((tokens, HEAD_DIM - 2 * PARTS), F32))
            rows = jnp.concatenate(
                [grads[group, 0:tokens, :], jnp.concatenate(tall, axis=1).astype(BF)], axis=1
            )
            part = dot_nn(hot, rows).astype(BF)
            lanes[:, pl.ds(source, 1)] = part.reshape(blocks, 1, CAP_ROWS, width)
            return carry

        lax.fori_loop(0, blocks // ROUNDS, pack, 0, unroll=4)

    sums[0:SPAN, :] = jnp.zeros((SPAN, width), F32)

    def place_rows(block, carry):
        cols = jnp.transpose(info[block])
        hot = hot_cols(cols[:, 2:3], slots)
        part = dot_nn(hot, lanes[block].reshape(slots, width))
        rows_in[block] = part[:, :HEAD_DIM].astype(BF)
        flat = jnp.transpose(part[:, HEAD_DIM:])
        stats[block, 0:1, :] = flat[0:1] + flat[1:2] + flat[2:3]
        stats[block, 1:2, :] = flat[PARTS : PARTS + 1] + (
            flat[PARTS + 1 : PARTS + 2] + flat[PARTS + 2 : PARTS + 3]
        )
        start = pl.multiple_of(SPAN + block * tokens, SPAN)
        keys = kept_rows[pl.ds(start, tokens), :HEAD_DIM]
        keep_columns(factors, ids, start, keys, cols)
        return carry

    lax.fori_loop(0, blocks, place_rows, 0, unroll=4)
    for held in (factors, ids):
        held[0:SPAN, :] = held[blocks * tokens : blocks * tokens + SPAN, :]

    def attend(step, carry):
        todo = [(step * BACKWARD_BATCH + at // pairs, at % pairs) for at in range(BACKWARD_BATCH * pairs)]
        first = []
        for block, pair in todo:
            start = pl.multiple_of(block * tokens + pair * 2 * SPAN, SPAN)
            here = slice(pair * 2 * SPAN, (pair + 1) * 2 * SPAN)
            rows = kept_rows[pl.ds(start, 3 * SPAN), :]
            keys = rows[:, :HEAD_DIM]
            queries = rows[SPAN:, :HEAD_DIM]
            grads = rows_in[block, here, :]
            raw = dot_nt(keys, queries)
            back = dot_nt(rows[:, HEAD_DIM:], grads)
            first.append((start, keys, queries, grads, raw, back))
        second = []
        for (block, pair), (start, keys, queries, grads, raw, back) in zip(todo, first):
            here = slice(pair * 2 * SPAN, (pair + 1) * 2 * SPAN)
            factor = factors[pl.ds(start, 3 * SPAN), :]
            scores, masks = pair_scores(
                raw,
                factor,
                ids[pl.ds(start, 3 * SPAN), :],
                info[block, 0:1, here],
                info[block, 1:2, here],
            )
            pull = stats[block, 0:1, here]
            total_lse = stats[block, 1:2, here]
            weights = [jnp.exp(score - total_lse) for score in scores]
            weights_all = jnp.concatenate(weights).astype(BF)
            grad_score = jnp.concatenate(
                [
                    jnp.where(
                        mask, weight * (back[chunk * SPAN : (chunk + 1) * SPAN] - pull), 0.0
                    )
                    for chunk, (mask, weight) in enumerate(zip(masks, weights))
                ]
            )
            slope = jnp.sum(grad_score * raw, axis=1, keepdims=True)
            drift = slope * (factor * factor * factor * HEAD_DIM) * keys.astype(F32)
            second.append(((grad_score * factor).astype(BF), weights_all, drift))
        for (start, keys, queries, grads, _, _), (grad_raw, weights_all, drift) in zip(
            first, second
        ):
            grad_val = dot_nn(weights_all, grads)
            grad_key = dot_nn(grad_raw, queries) - drift
            grad_query = dot_tn(grad_raw, keys)
            sums[pl.ds(start, SPAN), :] += jnp.concatenate(
                [grad_key[:SPAN], grad_val[:SPAN]], axis=1
            )
            after = pl.multiple_of(start + SPAN, SPAN)
            sums[pl.ds(after, 2 * SPAN), :] = jnp.concatenate(
                [grad_query + grad_key[SPAN:], grad_val[SPAN:]], axis=1
            )
        return carry

    lax.fori_loop(0, blocks // BACKWARD_BATCH, attend, 0)
    sums[blocks * tokens : blocks * tokens + SPAN, :] += sums[0:SPAN, :]

    def unplace(block, carry):
        hot = hot_rows(info[block, 2:3, :], slots)
        start = pl.multiple_of(SPAN + block * tokens, SPAN)
        part = dot_nn(hot, sums[pl.ds(start, tokens), :].astype(BF)).astype(BF)
        lanes[:, pl.ds(block, 1)] = part.reshape(blocks, 1, CAP_ROWS, width)
        return carry

    lax.fori_loop(0, blocks, unplace, 0, unroll=4)

    for offset, out in enumerate((out_0, out_1, out_2, out_3)):

        def unpack(group, carry, offset=offset, out=out):
            source = group * ROUNDS + lax.bitwise_xor(place[0], offset)
            cols = jnp.transpose(info[source])
            hot = hot_cols(cols[:, 3:4], slots)
            start = pl.multiple_of(group * tokens, tokens)
            part = dot_nn(hot, lanes[source].reshape(slots, width))
            out[pl.ds(start, tokens), :] = part.astype(BF)
            return carry

        lax.fori_loop(0, blocks // ROUNDS, unpack, 0, unroll=4)


def in_vmem(count):
    return [pl.BlockSpec(memory_space=pltpu.VMEM)] * count


def run_kernel(kernel, name, operands, shapes, scratch, scalar):
    first = [pl.BlockSpec(memory_space=pltpu.SMEM)] if scalar else []
    return pl.pallas_call(
        kernel,
        out_shape=tuple(jax.ShapeDtypeStruct(shape, BF) for shape in shapes),
        in_specs=first + in_vmem(len(operands) - len(first)),
        out_specs=tuple(in_vmem(len(shapes))),
        scratch_shapes=[pltpu.VMEM(shape, dtype) for shape, dtype in scratch],
        compiler_params=pltpu.CompilerParams(vmem_limit_bytes=48 << 20),
        cost_estimate=pl.CostEstimate(
            flops=20 * 10**9 if scalar else 10**7,
            bytes_accessed=12 * 10**6 if scalar else 2 * 10**6,
            transcendentals=10**6 if scalar else 10**4,
        ),
        name=name,
    )(*operands)


def run_forward(turn, rows, info):
    blocks, _, tokens = info.shape
    width = rows[0].shape[1]
    tall = tokens + PARTS * tokens // HEAD_DIM
    return run_kernel(
        forward_kernel,
        "hash_forward",
        (turn, *rows, info),
        [(blocks // ROUNDS, tall, HEAD_DIM)] * ROUNDS + [(SPAN + blocks * tokens, width)],
        [((blocks, blocks, CAP_ROWS, width), BF), ((blocks, tokens, width), BF)]
        + [((SPAN + blocks * tokens, HEAD_DIM), F32)] * 2,
        True,
    )


def run_backward(turn, grads, lse, kept_rows, info):
    blocks, _, tokens = info.shape
    width = kept_rows.shape[1]
    return run_kernel(
        backward_kernel,
        "hash_backward",
        (turn, *grads, *lse, kept_rows, info),
        [(blocks * tokens // ROUNDS, width)] * ROUNDS,
        [((blocks, blocks, CAP_ROWS, width), BF), ((SPAN + blocks * tokens, width), F32)]
        + [((SPAN + blocks * tokens, HEAD_DIM), F32)] * 2
        + [((blocks, tokens, HEAD_DIM), BF), ((blocks, 8, tokens), F32)],
        True,
    )


def merge_pair(a, b):
    return run_kernel(pair_kernel, "merge_pair", (a, b), [a.shape], [], False)[0]


def merge_final(a, b, c):
    groups, tall, width = a.shape
    tokens = tall // (HEAD_DIM + PARTS) * HEAD_DIM
    shapes = [(groups, tokens, width), (groups, tall - tokens, width)]
    return run_kernel(final_kernel, "merge_final", (a, b, c), shapes, [], False)


def peers(mask):
    size = HEADS * ROUNDS
    return [(i, i ^ mask) for i in range(size)]


def swap(x, mask):
    return lax.ppermute(x, "seq", peers(mask))


def columns():
    return [[head * ROUNDS + turn for head in range(HEADS)] for turn in range(ROUNDS)]


def rows_of():
    return [[head * ROUNDS + turn for turn in range(ROUNDS)] for head in range(HEADS)]


def gather_group(x):
    side = swap(x, 2)
    return (x, swap(x, 1), side, swap(side, 1))


def sum_group(parts):
    near = parts[0] + swap(parts[1].astype(BF), 1).astype(F32)
    far = parts[2] + swap(parts[3].astype(BF), 1).astype(F32)
    return near + swap(far.astype(BF), 2).astype(F32)


def row_major(x):
    return with_layout_constraint(x.astype(BF), Layout(major_to_minor=(0, 1)))


def exchange(x, groups=None):
    return lax.all_to_all(
        x, "seq", split_axis=0, concat_axis=0, tiled=True, axis_index_groups=groups
    )


def rounded(x):
    return lax.reduce_precision(x, 8, 7)


def split_three(wide):
    high = rounded(wide)
    rest = wide - high
    mid = rounded(rest)
    return jnp.stack([high, mid, rest - mid])


def slots_sent(target, tokens, capacity):
    device = target // tokens
    early = jnp.arange(tokens)[None, :] < jnp.arange(tokens)[:, None]
    same = (device[:, None] == device[None, :]) & early
    return device * capacity + jnp.sum(same.astype(jnp.int32), axis=1)


def start_of(token_ids, doc_ends):
    ends = doc_ends[None, :]
    return jnp.max(jnp.where(ends <= token_ids[:, None], ends, 0), axis=1)


def shards_fast(
    x_first,
    x_second,
    w_qk,
    w_value,
    w_out,
    gain_attn,
    bias_attn,
    gain_ffn,
    bias_ffn,
    w_up,
    bias_up,
    w_down,
    bias_down,
    sort_order,
    inverse,
    lengths,
    dy_first,
    dy_second,
):
    devices = lax.axis_size("seq")
    tokens, features = x_first.shape
    capacity = 2 * tokens // devices
    shard = features // devices
    place = lax.axis_index("seq")
    doc_ends = jnp.cumsum(lengths)

    per_round = []
    vectors = rounded(
        jnp.concatenate([gain_attn, bias_attn, gain_ffn, bias_ffn, bias_up, bias_down])
    )
    vectors = jnp.pad(vectors, (0, 2 * tokens - vectors.shape[0])).reshape(2, tokens)
    for turn in range(ROUNDS):
        ids = sort_order[turn]
        rows = jnp.stack(
            [
                ids,
                start_of(ids, doc_ends),
                recv_slots(ids, tokens, capacity),
                slots_sent(inverse[turn], tokens, capacity),
            ]
        ).astype(F32)
        split = jnp.stack([ids // SPAN * SPAN, ids % SPAN]).astype(F32)
        per_round.append(jnp.concatenate([rows, vectors, split]))
    info = jnp.tile(jnp.stack(per_round), (HEADS, 1, 1))
    info = exchange(info)
    got = info[:, 4:6].reshape(devices, 2 * tokens)

    def vector(first, size):
        return got[:, first : first + size].reshape(devices * size)

    gain_one, shift_one = vector(0, shard), vector(shard, shard)
    gain_two, shift_two = vector(2 * shard, shard), vector(3 * shard, shard)
    wide = bias_up.shape[0]
    b_up = vector(4 * shard, wide)
    b_down = vector(4 * shard + wide, shard)
    pair = jnp.stack(
        [w_qk.reshape(shard, HEADS, HEAD_DIM), w_value.reshape(shard, HEADS, HEAD_DIM)], axis=2
    ).reshape(shard, 2 * features)
    m_pair = lax.all_gather(pair.astype(BF), "seq", axis=0, tiled=True)
    half = HEADS * wide
    up_cols = jnp.transpose(
        w_up.astype(BF).reshape(shard, HEADS, ROUNDS, wide), (2, 0, 1, 3)
    ).reshape(ROUNDS, shard, half)
    out_rows = jnp.broadcast_to(w_out.astype(BF), (ROUNDS, shard, features))
    near_rows = exchange(jnp.concatenate([up_cols, out_rows], axis=2), rows_of())
    near_rows = near_rows.reshape(ROUNDS * shard, half + features)
    b_up = lax.dynamic_index_in_dim(
        b_up.reshape(HEADS, ROUNDS, wide), place % ROUNDS, axis=1, keepdims=False
    ).reshape(HEADS * wide)

    normed_one, hat_one, inv_one = layer_norm(x_second, gain_one, shift_one)
    grad_f = dy_second.astype(BF)
    normed_one, near_rows, grad_f_all = lax.optimization_barrier(
        (normed_one.astype(BF), near_rows, gather_group(grad_f))
    )
    grad_f_all = jnp.concatenate(grad_f_all)
    rows = linear(normed_one, m_pair).astype(BF)
    rows = jnp.transpose(rows.reshape(tokens, HEADS, 2 * HEAD_DIM), (1, 0, 2))
    own = exchange(rows, columns()).reshape(HEADS * tokens, 2 * HEAD_DIM)
    own, near_rows = lax.optimization_barrier((own, near_rows))
    m_ffn = lax.all_gather(
        jnp.concatenate([near_rows, w_down.astype(BF)], axis=1),
        "seq",
        axis=0,
        tiled=True,
        axis_index_groups=columns(),
    )
    m_up, m_out, m_down = (m_ffn[:, at : at + features] for at in (0, half, half + features))
    turn = (place % ROUNDS).astype(jnp.int32).reshape(1)
    *sent, kept_rows = run_forward(turn, gather_group(own), info)
    far = merge_pair(sent[2], swap(sent[3], 1))
    mixed, total_lse = merge_final(sent[0], swap(sent[1], 1), swap(far, 2))
    mixed = exchange(mixed, columns())
    grad_hidden = outer_cols(grad_f_all, m_down)
    mixed, normed_one, grad_hidden, total_lse = lax.optimization_barrier(
        (mixed, normed_one, grad_hidden, gather_group(total_lse))
    )
    normed_col = lax.all_gather(
        normed_one, "seq", axis=0, tiled=True, axis_index_groups=columns()
    )
    mixed = jnp.transpose(mixed, (1, 0, 2)).reshape(tokens, features)
    y_first = x_first + linear(mixed, m_out)
    normed_two, hat_two, inv_two = layer_norm(y_first, gain_two, shift_two)
    normed_two = normed_two.astype(BF)
    normed_all = jnp.concatenate(gather_group(normed_two))
    pre_up = linear(normed_all, m_up) + b_up
    hidden, gelu_back = jax.vjp(partial(jax.nn.gelu, approximate=True), pre_up)
    hidden = hidden.astype(BF)
    branch = sum_group(linear(hidden, m_down).reshape(ROUNDS, tokens, features))
    y_second = x_second + (branch + b_down)
    grad_down = inner_rows(hidden, grad_f_all)
    grad_bias_down = jnp.sum(grad_f.astype(F32), axis=0)
    grad_pre = gelu_back(grad_hidden)[0].astype(BF)
    grad_up = inner_rows(normed_all, grad_pre)
    grad_bias_up = jnp.sum(grad_pre.astype(F32), axis=0)
    grad_two = sum_group(outer_cols(grad_pre, m_up).reshape(ROUNDS, tokens, features))
    grad_gain_ffn = jnp.sum(grad_two * hat_two, axis=0)
    grad_bias_ffn = jnp.sum(grad_two, axis=0)
    dx_first = dy_first + norm_back(grad_two, hat_two, inv_two, gain_two)
    grad_attn = dx_first.astype(BF)
    grad_out = inner_rows(mixed, grad_attn)
    fourth = features // ROUNDS
    grad_mixed = outer_cols(grad_attn, m_out).astype(BF)
    pull = jnp.sum(
        (grad_mixed.astype(F32) * mixed.astype(F32)).reshape(tokens, HEADS, HEAD_DIM), axis=-1
    )
    parts = split_three(jnp.transpose(pull))
    parts = jnp.pad(parts, ((0, PARTS - 3), (0, 0), (0, 0)))
    parts = jnp.transpose(parts.reshape(PARTS, HEADS, -1, HEAD_DIM), (1, 2, 0, 3))
    parts = parts.reshape(HEADS, -1, HEAD_DIM).astype(BF)
    grad_mixed = jnp.transpose(grad_mixed.reshape(tokens, HEADS, HEAD_DIM), (1, 0, 2))
    grad_mixed = exchange(jnp.concatenate([grad_mixed, parts], axis=1), columns())
    grad_out = sum_group(
        [
            lax.dynamic_slice_in_dim(grad_out, ((place % ROUNDS) ^ near) * fourth, fourth, axis=1)
            for near in range(ROUNDS)
        ]
    )
    merged = jnp.concatenate([row_major(x) for x in (grad_up, grad_out, grad_down)], axis=1)
    grad_mixed, merged = lax.optimization_barrier((grad_mixed, merged))
    grad_mixed = list(gather_group(grad_mixed))
    merged, normed_col, grad_mixed[1] = lax.optimization_barrier(
        (merged, normed_col, grad_mixed[1])
    )
    merged = lax.psum_scatter(
        merged, "seq", scatter_dimension=0, tiled=True, axis_index_groups=columns()
    )
    s_down = merged[:, half + fourth :].astype(F32)
    merged = merged[:, : half + fourth].reshape(ROUNDS, shard, -1)
    pieces = [
        lax.dynamic_index_in_dim(merged, (place % ROUNDS) ^ near, axis=0, keepdims=False)
        for near in range(ROUNDS)
    ]
    pieces = [swap(piece, near) if near else piece for near, piece in enumerate(pieces)]

    def in_order(first, last):
        mine = place % ROUNDS
        found = []
        for peer in range(ROUNDS):
            options = [pieces[peer ^ at][:, first:last] for at in range(ROUNDS)]
            low = jnp.where(mine == 0, options[0], options[1])
            high = jnp.where(mine == 2, options[2], options[3])
            found.append(jnp.where(mine < 2, low, high))
        return jnp.stack(found, axis=1).astype(F32)

    s_up = in_order(0, half).reshape(shard, ROUNDS, HEADS, wide)
    s_up = jnp.transpose(s_up, (0, 2, 1, 3)).reshape(shard, ROUNDS * half)
    s_out = in_order(half, half + fourth).reshape(shard, features)

    grad_head = run_backward(
        turn, grad_mixed, total_lse, kept_rows, info
    )
    grad_head = sum_group([x.astype(F32) for x in grad_head]).astype(BF)
    grad_rows = exchange(grad_head.reshape(HEADS, tokens, 2 * HEAD_DIM), columns())
    s_pair = inner_rows(normed_col, grad_head).astype(BF).reshape(devices, shard, 2 * HEAD_DIM)
    grad_rows, s_pair, s_up, s_out, s_down = lax.optimization_barrier(
        (grad_rows, s_pair, s_up, s_out, s_down)
    )
    grad_rows = jnp.transpose(grad_rows, (1, 0, 2)).reshape(tokens, 2 * features)
    s_pair = exchange(s_pair)
    s_pair = jnp.sum(
        s_pair.reshape(HEADS, ROUNDS, shard, 2, HEAD_DIM).astype(F32), axis=1
    ).transpose(2, 1, 0, 3)
    s_qk = s_pair[0].reshape(shard, features)
    s_value = s_pair[1].reshape(shard, features)
    grad_one = outer_cols(grad_rows, m_pair)
    grad_gain_attn = jnp.sum(grad_one * hat_one, axis=0)
    grad_bias_attn = jnp.sum(grad_one, axis=0)
    dx_second = dy_second + norm_back(grad_one, hat_one, inv_one, gain_one)
    is_mine = (jnp.arange(ROUNDS) == place % ROUNDS).astype(F32)
    grad_bias_up = grad_bias_up.reshape(HEADS, 1, wide) * is_mine[None, :, None]
    small = jnp.concatenate(
        [
            grad_gain_attn.reshape(devices, -1),
            grad_bias_attn.reshape(devices, -1),
            grad_gain_ffn.reshape(devices, -1),
            grad_bias_ffn.reshape(devices, -1),
            grad_bias_up.reshape(devices, -1),
            grad_bias_down.reshape(devices, -1),
        ],
        axis=1,
    )
    small, s_qk, s_value = lax.optimization_barrier((small, s_qk, s_value))
    small = jnp.sum(exchange(small[:, None]), axis=(0, 1))
    s_gattn, s_battn, s_gffn, s_bffn = (small[i * shard : (i + 1) * shard] for i in range(4))
    s_bup = small[4 * shard : 4 * shard + wide]
    s_bdown = small[4 * shard + wide :]
    return (
        y_first,
        y_second,
        dx_first,
        dx_second,
        s_qk,
        s_value,
        s_out,
        s_gattn,
        s_battn,
        s_gffn,
        s_bffn,
        s_up,
        s_bup,
        s_down,
        s_bdown,
    )


def solution(mesh):
    in_specs = (
        P("seq", None),
        P("seq", None),
        P("seq", None),
        P("seq", None),
        P("seq", None),
        P("seq"),
        P("seq"),
        P("seq"),
        P("seq"),
        P("seq", None),
        P("seq"),
        P("seq", None),
        P("seq"),
        P(None, "seq"),
        P(None, "seq"),
        P(),
        P("seq", None),
        P("seq", None),
    )
    out_specs = (
        P("seq", None),
        P("seq", None),
        P("seq", None),
        P("seq", None),
        P("seq", None),
        P("seq", None),
        P("seq", None),
        P("seq"),
        P("seq"),
        P("seq"),
        P("seq"),
        P("seq", None),
        P("seq"),
        P("seq", None),
        P("seq"),
    )
    fast = mesh.shape["seq"] == HEADS * ROUNDS
    return jax.shard_map(shards_fast if fast else shards, mesh=mesh, in_specs=in_specs, out_specs=out_specs, check_vma=False)
```

```python
from functools import partial
import math

import jax
import jax.numpy as jnp
from jax import lax
from jax.experimental import pallas as pl
from jax.experimental.layout import Layout, with_layout_constraint
from jax.experimental.pallas import tpu as pltpu
from jax.sharding import PartitionSpec as P

HEADS = 8
HEAD_DIM = 128
SPAN = 64
ROUNDS = 4

EPSILON = 1e-05
SCALE = 1.0 / math.sqrt(HEAD_DIM)
BF = jnp.bfloat16
F32 = jnp.float32


def shifted(x, axis, by):
    size = lax.axis_size(axis)
    return lax.ppermute(x, axis, [(i, (i + by) % size) for i in range(size)])


def as_sent(x):
    return jax.tree.map(lambda a: a.astype(jnp.bfloat16) if a.dtype == jnp.float32 else a, x)


def layer_norm(inputs, norm_gain, norm_shift):
    centered = inputs - jnp.mean(inputs, axis=-1, keepdims=True)
    inv_std = lax.rsqrt(jnp.mean(centered * centered, axis=-1, keepdims=True) + EPSILON)
    normed = centered * inv_std
    return (normed * norm_gain + norm_shift, normed, inv_std)


def norm_back(grad_rows, normed, inv_std, norm_gain):
    grad_hat = grad_rows * norm_gain
    return inv_std * (
        grad_hat
        - jnp.mean(grad_hat, axis=-1, keepdims=True)
        - normed * jnp.mean(grad_hat * normed, axis=-1, keepdims=True)
    )


def linear(matrix_a, matrix_b):
    return jnp.dot(matrix_a, matrix_b, preferred_element_type=jnp.float32)


def inner_rows(matrix_a, matrix_b):
    return lax.dot_general(
        matrix_a, matrix_b, (((0,), (0,)), ((), ())), preferred_element_type=jnp.float32
    )


def outer_cols(matrix_a, matrix_b):
    return lax.dot_general(
        matrix_a, matrix_b, (((1,), (1,)), ((), ())), preferred_element_type=jnp.float32
    )


def segment_of(token_ids, doc_ends):
    return jnp.sum((token_ids[:, None] >= doc_ends[None, :]).astype(jnp.int32), axis=1)


def send_slots(target, tokens, devices, capacity):
    device = target // tokens
    onehot = (device[:, None] == jnp.arange(devices, dtype=jnp.int32)[None, :]).astype(jnp.int32)
    rank_in = jnp.sum(jnp.cumsum(onehot, axis=0) * onehot, axis=1) - 1
    return device * capacity + rank_in


def recv_slots(source_ids, tokens, capacity):
    device = source_ids // tokens
    earlier = (device[:, None] == device[None, :]) & (source_ids[None, :] < source_ids[:, None])
    return device * capacity + jnp.sum(earlier.astype(jnp.int32), axis=1)


def packed(inputs, slot_ids, devices, capacity):
    filled = (
        jnp.zeros((devices * capacity,) + inputs.shape[1:], inputs.dtype).at[slot_ids].set(inputs)
    )
    return filled.reshape((devices, capacity) + inputs.shape[1:])


def unpacked(received, slot_ids):
    return received.reshape((-1,) + received.shape[2:])[slot_ids]


def spanned(inputs, before):
    blocks = inputs.shape[0] // SPAN
    current = inputs.reshape((blocks, SPAN) + inputs.shape[1:])
    earlier = jnp.concatenate([before[None], current[:-1]], axis=0)
    return (current, jnp.concatenate([earlier, current], axis=1))


def arrange(got_qk, got_value, recv_slot):
    sorted_qk = unpacked(got_qk, recv_slot)
    sorted_value = unpacked(got_value, recv_slot)
    last_block = jnp.stack([sorted_qk[-SPAN:], sorted_value[-SPAN:]])
    return (sorted_qk, sorted_value, last_block)


def score_parts(sorted_rows, query_ids, before_ids, doc_ends):
    sorted_qk, sorted_value, before_qk, before_value = sorted_rows
    current, key_rows = spanned(sorted_qk, before_qk)
    _, value_keys = spanned(sorted_value, before_value)
    current_ids, key_ids = spanned(query_ids, before_ids)
    current_seg, key_seg = spanned(
        segment_of(query_ids, doc_ends), segment_of(before_ids, doc_ends)
    )
    blocks = current.shape[0]
    q_heads = current.reshape(blocks, SPAN, HEADS, HEAD_DIM)
    k_heads = key_rows.reshape(blocks, 2 * SPAN, HEADS, HEAD_DIM)
    v_heads = value_keys.reshape(blocks, 2 * SPAN, HEADS, HEAD_DIM)
    raw_dots = jnp.einsum("gihd,gjhd->ghij", q_heads, k_heads, preferred_element_type=jnp.float32)
    k_float = k_heads.astype(jnp.float32)
    key_norm = lax.rsqrt(jnp.sum(k_float * k_float, axis=-1))
    factor = jnp.transpose(key_norm, (0, 2, 1))[:, :, None, :] / math.sqrt(HEAD_DIM)
    allowed = (
        (key_ids[:, None, :] <= current_ids[:, :, None])
        & (key_seg[:, None, :] == current_seg[:, :, None])
    )[:, None]
    itself = (key_ids[:, None, :] == current_ids[:, :, None])[:, None]
    scores = jnp.where(itself, -100000.0, jnp.where(allowed, raw_dots * factor, -1000000000.0))
    log_total = jax.nn.logsumexp(scores, axis=-1)
    attn_probs = jnp.exp(scores - log_total[..., None])
    kept_mask = allowed & jnp.logical_not(itself)
    return (
        q_heads,
        k_heads,
        v_heads,
        k_float,
        key_norm,
        factor,
        kept_mask,
        raw_dots,
        attn_probs,
        log_total,
    )


def attend_out(pieces):
    (
        q_heads,
        k_heads,
        v_heads,
        k_float,
        key_norm,
        factor,
        kept_mask,
        raw_dots,
        attn_probs,
        log_total,
    ) = pieces
    blocks = q_heads.shape[0]
    out_heads = jnp.einsum(
        "ghij,gjhd->gihd",
        attn_probs.astype(jnp.bfloat16),
        v_heads,
        preferred_element_type=jnp.float32,
    )
    return (
        out_heads.reshape(blocks * SPAN, -1),
        jnp.transpose(log_total, (0, 2, 1)).reshape(blocks * SPAN, HEADS),
    )


def attend_back(pieces, grad_rows, grad_total):
    (
        q_heads,
        k_heads,
        v_heads,
        k_float,
        key_norm,
        factor,
        kept_mask,
        raw_dots,
        attn_probs,
        log_total,
    ) = pieces
    blocks = q_heads.shape[0]
    grad_heads = grad_rows.astype(jnp.bfloat16).reshape(blocks, SPAN, HEADS, HEAD_DIM)
    grad_lse = jnp.transpose(grad_total.reshape(blocks, SPAN, HEADS), (0, 2, 1))
    grad_prob = jnp.einsum(
        "gihd,gjhd->ghij", grad_heads, v_heads, preferred_element_type=jnp.float32
    )
    grad_val = jnp.einsum(
        "ghij,gihd->gjhd",
        attn_probs.astype(jnp.bfloat16),
        grad_heads,
        preferred_element_type=jnp.float32,
    )
    row_dot = jnp.sum(attn_probs * grad_prob, axis=-1, keepdims=True)
    grad_score = jnp.where(kept_mask, attn_probs * (grad_prob - row_dot + grad_lse[..., None]), 0.0)
    grad_raw = (grad_score * factor).astype(jnp.bfloat16)
    grad_norm = jnp.transpose(jnp.sum(grad_score * raw_dots, axis=2), (0, 2, 1)) / math.sqrt(
        HEAD_DIM
    )
    norm_cube = key_norm * key_norm * key_norm
    grad_query = jnp.einsum(
        "ghij,gjhd->gihd", grad_raw, k_heads, preferred_element_type=jnp.float32
    )
    grad_key = (
        jnp.einsum("ghij,gihd->gjhd", grad_raw, q_heads, preferred_element_type=jnp.float32)
        - (grad_norm * norm_cube)[..., None] * k_float
    )
    return (
        grad_query.reshape(blocks, SPAN, -1),
        grad_key.reshape(blocks, 2 * SPAN, -1),
        grad_val.reshape(blocks, 2 * SPAN, -1),
    )


def shards(
    x_first,
    x_second,
    w_qk,
    w_value,
    w_out,
    gain_attn,
    bias_attn,
    gain_ffn,
    bias_ffn,
    w_up,
    bias_up,
    w_down,
    bias_down,
    sort_order,
    inverse,
    lengths,
    dy_first,
    dy_second,
):
    devices = lax.axis_size("seq")
    tokens = x_first.shape[0]
    capacity = 2 * tokens // devices
    gathered = (
        lax.all_gather(w_qk.astype(jnp.bfloat16), "seq", axis=0, tiled=True),
        lax.all_gather(w_value.astype(jnp.bfloat16), "seq", axis=0, tiled=True),
        lax.all_gather(w_out.astype(jnp.bfloat16), "seq", axis=0, tiled=True),
        lax.all_gather(gain_attn.astype(jnp.bfloat16), "seq", axis=0, tiled=True),
        lax.all_gather(bias_attn.astype(jnp.bfloat16), "seq", axis=0, tiled=True),
        lax.all_gather(gain_ffn.astype(jnp.bfloat16), "seq", axis=0, tiled=True),
        lax.all_gather(bias_ffn.astype(jnp.bfloat16), "seq", axis=0, tiled=True),
        lax.all_gather(w_up.astype(jnp.bfloat16), "seq", axis=0, tiled=True),
        lax.all_gather(bias_up.astype(jnp.bfloat16), "seq", axis=0, tiled=True),
        lax.all_gather(w_down.astype(jnp.bfloat16), "seq", axis=0, tiled=True),
        lax.all_gather(bias_down.astype(jnp.bfloat16), "seq", axis=0, tiled=True),
    )
    m_qk, m_value, m_out, g_attn, b_attn, g_ffn, b_ffn, m_up, b_up, m_down, b_down = gathered
    gain_one = g_attn.astype(jnp.float32)
    gain_two = g_ffn.astype(jnp.float32)
    doc_ends = jnp.cumsum(lengths)
    send_list = [send_slots(inverse[turn], tokens, devices, capacity) for turn in range(ROUNDS)]
    recv_list = [recv_slots(sort_order[turn], tokens, capacity) for turn in range(ROUNDS)]
    before_ids = shifted(sort_order[:, tokens - SPAN :], "seq", 1)
    normed_one, hat_one, inv_one = layer_norm(x_second, gain_one, b_attn.astype(jnp.float32))
    normed_one = normed_one.astype(jnp.bfloat16)
    qk_rows = linear(normed_one, m_qk).astype(jnp.bfloat16)
    value_rows = linear(normed_one, m_value).astype(jnp.bfloat16)
    stashed = []
    round_outs = []
    round_lse = []
    for turn in range(ROUNDS):
        got_qk, got_value = (
            lax.all_to_all(
                packed(qk_rows, send_list[turn], devices, capacity),
                "seq",
                split_axis=0,
                concat_axis=0,
                tiled=True,
            ),
            lax.all_to_all(
                packed(value_rows, send_list[turn], devices, capacity),
                "seq",
                split_axis=0,
                concat_axis=0,
                tiled=True,
            ),
        )
        sorted_qk, sorted_value, last_block = arrange(got_qk, got_value, recv_list[turn])
        before_block = shifted(last_block, "seq", 1)
        sorted_rows = (sorted_qk, sorted_value, before_block[0], before_block[1])
        pieces = score_parts(sorted_rows, sort_order[turn], before_ids[turn], doc_ends)
        out_sorted, lse_sorted = attend_out(pieces)
        back_out, back_lse = (
            lax.all_to_all(
                packed(out_sorted, recv_list[turn], devices, capacity),
                "seq",
                split_axis=0,
                concat_axis=0,
                tiled=True,
            ),
            lax.all_to_all(
                packed(lse_sorted, recv_list[turn], devices, capacity),
                "seq",
                split_axis=0,
                concat_axis=0,
                tiled=True,
            ),
        )
        round_outs.append(unpacked(back_out, send_list[turn]))
        round_lse.append(unpacked(back_lse, send_list[turn]))
        stashed.append(sorted_rows)
    lse_all = jnp.stack(round_lse)
    out_all = jnp.stack(round_outs).reshape(ROUNDS, tokens, HEADS, HEAD_DIM)
    merge = jnp.exp(lse_all - jax.nn.logsumexp(lse_all, axis=0))
    mixed = jnp.sum(merge[..., None] * out_all, axis=0).reshape(tokens, -1).astype(jnp.bfloat16)
    y_first = x_first + linear(mixed, m_out)
    normed_two, hat_two, inv_two = layer_norm(y_first, gain_two, b_ffn.astype(jnp.float32))
    normed_two = normed_two.astype(jnp.bfloat16)
    pre_up = linear(normed_two, m_up) + b_up.astype(jnp.float32)
    hidden, gelu_back = jax.vjp(partial(jax.nn.gelu, approximate=True), pre_up)
    hidden = hidden.astype(jnp.bfloat16)
    y_second = x_second + (linear(hidden, m_down) + b_down.astype(jnp.float32))
    grad_f = dy_second.astype(jnp.bfloat16)
    grad_down = inner_rows(hidden, grad_f)
    grad_bias_down = jnp.sum(grad_f.astype(jnp.float32), axis=0)
    grad_pre = gelu_back(outer_cols(grad_f, m_down))[0].astype(jnp.bfloat16)
    grad_up = inner_rows(normed_two, grad_pre)
    grad_bias_up = jnp.sum(grad_pre.astype(jnp.float32), axis=0)
    grad_two = outer_cols(grad_pre, m_up)
    grad_gain_ffn = jnp.sum(grad_two * hat_two, axis=0)
    grad_bias_ffn = jnp.sum(grad_two, axis=0)
    dx_first = dy_first + norm_back(grad_two, hat_two, inv_two, gain_two)
    grad_attn = dx_first.astype(jnp.bfloat16)
    grad_out = inner_rows(mixed, grad_attn)
    grad_mixed = outer_cols(grad_attn, m_out).reshape(tokens, HEADS, HEAD_DIM)
    along = jnp.sum(grad_mixed[None] * out_all, axis=-1)
    grad_lse_all = merge * (along - jnp.sum(merge * along, axis=0, keepdims=True))
    grad_qk_sum = jnp.zeros((tokens, HEADS * HEAD_DIM), jnp.float32)
    grad_value_sum = jnp.zeros((tokens, HEADS * HEAD_DIM), jnp.float32)
    for turn in range(ROUNDS):
        grad_round = (merge[turn][..., None] * grad_mixed).reshape(tokens, -1)
        got_out, got_lse = (
            lax.all_to_all(
                packed(grad_round, send_list[turn], devices, capacity),
                "seq",
                split_axis=0,
                concat_axis=0,
                tiled=True,
            ),
            lax.all_to_all(
                packed(grad_lse_all[turn], send_list[turn], devices, capacity),
                "seq",
                split_axis=0,
                concat_axis=0,
                tiled=True,
            ),
        )
        sorted_grad_out = unpacked(got_out, recv_list[turn])
        sorted_grad_lse = unpacked(got_lse, recv_list[turn])
        sorted_rows = stashed[turn]
        pieces = score_parts(sorted_rows, sort_order[turn], before_ids[turn], doc_ends)
        grad_query, grad_key, grad_val = attend_back(pieces, sorted_grad_out, sorted_grad_lse)
        spill = shifted(
            jnp.stack([grad_key[0, :SPAN], grad_val[0, :SPAN]]).astype(jnp.bfloat16), "seq", -1
        ).astype(jnp.float32)
        key_add = jnp.concatenate([grad_key[1:, :SPAN], spill[0][None]], axis=0)
        value_add = jnp.concatenate([grad_val[1:, :SPAN], spill[1][None]], axis=0)
        sorted_grad_qk = (grad_query + grad_key[:, SPAN:] + key_add).reshape(tokens, -1)
        sorted_grad_value = (grad_val[:, SPAN:] + value_add).reshape(tokens, -1)
        back_qk, back_value = (
            lax.all_to_all(
                as_sent(packed(sorted_grad_qk, recv_list[turn], devices, capacity)),
                "seq",
                split_axis=0,
                concat_axis=0,
                tiled=True,
            ),
            lax.all_to_all(
                as_sent(packed(sorted_grad_value, recv_list[turn], devices, capacity)),
                "seq",
                split_axis=0,
                concat_axis=0,
                tiled=True,
            ),
        )
        grad_qk_sum = grad_qk_sum + unpacked(back_qk, send_list[turn])
        grad_value_sum = grad_value_sum + unpacked(back_value, send_list[turn])
    grad_qk_rows = grad_qk_sum.astype(jnp.bfloat16)
    grad_value_rows = grad_value_sum.astype(jnp.bfloat16)
    grad_qk = inner_rows(normed_one, grad_qk_rows)
    grad_value = inner_rows(normed_one, grad_value_rows)
    grad_one = outer_cols(grad_qk_rows, m_qk) + outer_cols(grad_value_rows, m_value)
    grad_gain_attn = jnp.sum(grad_one * hat_one, axis=0)
    grad_bias_attn = jnp.sum(grad_one, axis=0)
    dx_second = dy_second + norm_back(grad_one, hat_one, inv_one, gain_one)
    s_qk, s_value, s_out, s_gattn, s_battn, s_gffn, s_bffn, s_up, s_bup, s_down, s_bdown = (
        lax.psum_scatter(grad_qk, "seq", scatter_dimension=0, tiled=True),
        lax.psum_scatter(grad_value, "seq", scatter_dimension=0, tiled=True),
        lax.psum_scatter(grad_out, "seq", scatter_dimension=0, tiled=True),
        lax.psum_scatter(grad_gain_attn, "seq", scatter_dimension=0, tiled=True),
        lax.psum_scatter(grad_bias_attn, "seq", scatter_dimension=0, tiled=True),
        lax.psum_scatter(grad_gain_ffn, "seq", scatter_dimension=0, tiled=True),
        lax.psum_scatter(grad_bias_ffn, "seq", scatter_dimension=0, tiled=True),
        lax.psum_scatter(grad_up, "seq", scatter_dimension=0, tiled=True),
        lax.psum_scatter(grad_bias_up, "seq", scatter_dimension=0, tiled=True),
        lax.psum_scatter(grad_down, "seq", scatter_dimension=0, tiled=True),
        lax.psum_scatter(grad_bias_down, "seq", scatter_dimension=0, tiled=True),
    )
    return (
        y_first,
        y_second,
        dx_first,
        dx_second,
        s_qk,
        s_value,
        s_out,
        s_gattn,
        s_battn,
        s_gffn,
        s_bffn,
        s_up,
        s_bup,
        s_down,
        s_bdown,
    )


CAP_ROWS = 16
FORWARD_BATCH = 4
BACKWARD_BATCH = 2
PARTS = 8


def dot_nn(a, b):
    return lax.dot_general(a, b, (((1,), (0,)), ((), ())), preferred_element_type=F32)


def dot_nt(a, b):
    return lax.dot_general(a, b, (((1,), (1,)), ((), ())), preferred_element_type=F32)


def dot_tn(a, b):
    return lax.dot_general(a, b, (((0,), (0,)), ((), ())), preferred_element_type=F32)


def hot_rows(slot_row, slots):
    ids = lax.broadcasted_iota(jnp.int32, (slots, slot_row.shape[1]), 0).astype(F32)
    return jnp.where(ids == slot_row, 1.0, 0.0).astype(BF)


def hot_cols(slot_col, slots):
    ids = lax.broadcasted_iota(jnp.int32, (slot_col.shape[0], slots), 1).astype(F32)
    return jnp.where(ids == slot_col, 1.0, 0.0).astype(BF)


def keep_columns(factors, ids, start, keys, cols):
    rows = keys.shape[0]
    wide = keys.astype(F32)
    square = wide * wide
    high = square.astype(BF)
    low = (square - high.astype(F32)).astype(BF)
    ones = jnp.ones((HEAD_DIM, HEAD_DIM), BF)
    total = dot_nn(high, ones) + dot_nn(low, ones)
    factors[pl.ds(start, rows), :] = lax.rsqrt(total) * SCALE
    pick = lax.broadcasted_iota(jnp.int32, (PARTS, HEAD_DIM), 0) >= 6
    ids[pl.ds(start, rows), :] = dot_nn(cols.astype(BF), jnp.where(pick, 1.0, 0.0).astype(BF))


def pair_scores(raw, factor, key_ids, query_ids, query_starts):
    lane = lax.broadcasted_iota(jnp.int32, query_ids.shape, 1)
    first = jnp.where(lane < SPAN, query_ids, -1.0)
    second = jnp.where(lane >= SPAN, query_ids, -1.0)
    scores, masks = [], []
    for chunk, limits in enumerate((first, query_ids, second)):
        here = slice(chunk * SPAN, (chunk + 1) * SPAN)
        ids = key_ids[here]
        kept = (ids < limits) & (ids >= query_starts)
        score = jnp.where(kept, raw[here] * factor[here], -1000000000.0)
        if chunk > 0:
            score = jnp.where(ids == query_ids, -100000.0, score)
        scores.append(score)
        masks.append(kept)
    return scores, masks


def three_parts(wide):
    high = wide.astype(BF).astype(F32)
    rest = wide - high
    mid = rest.astype(BF).astype(F32)
    return high, mid, rest - mid


def forward_kernel(
    place,
    x_0,
    x_1,
    x_2,
    x_3,
    info,
    out_0,
    out_1,
    out_2,
    out_3,
    kept_rows,
    lanes,
    heads_out,
    factors,
    ids,
):
    blocks, tokens = info.shape[0], info.shape[2]
    slots = blocks * CAP_ROWS
    width = x_0.shape[1]
    pairs = tokens // (2 * SPAN)
    turn = place[0]
    rounds = ROUNDS

    for offset, rows in enumerate((x_0, x_1, x_2, x_3)):

        def pack(group, carry, offset=offset, rows=rows):
            source = group * rounds + lax.bitwise_xor(turn, offset)
            hot = hot_rows(info[source, 3:4, :], slots)
            start = pl.multiple_of(group * tokens, tokens)
            part = dot_nn(hot, rows[pl.ds(start, tokens), :]).astype(BF)
            lanes[:, pl.ds(source, 1)] = part.reshape(blocks, 1, CAP_ROWS, width)
            return carry

        lax.fori_loop(0, blocks // rounds, pack, 0, unroll=4)

    def place_rows(block, carry):
        cols = jnp.transpose(info[block])
        hot = hot_cols(cols[:, 2:3], slots)
        part = dot_nn(hot, lanes[block].reshape(slots, width)).astype(BF)
        start = pl.multiple_of(SPAN + block * tokens, SPAN)
        kept_rows[pl.ds(start, tokens), :] = part
        keep_columns(factors, ids, start, part[:, :HEAD_DIM], cols)
        return carry

    lax.fori_loop(0, blocks, place_rows, 0, unroll=4)
    for held in (kept_rows, factors, ids):
        held[0:SPAN, :] = held[blocks * tokens : blocks * tokens + SPAN, :]
    heads_out[:, :, HEAD_DIM:] = jnp.zeros((blocks, tokens, width - HEAD_DIM), BF)

    def attend(step, carry):
        todo = [(step * FORWARD_BATCH + at // pairs, at % pairs) for at in range(FORWARD_BATCH * pairs)]
        first = []
        for block, pair in todo:
            start = pl.multiple_of(block * tokens + pair * 2 * SPAN, SPAN)
            rows = kept_rows[pl.ds(start, 3 * SPAN), :]
            raw = dot_nt(rows[:, :HEAD_DIM], rows[SPAN:, :HEAD_DIM])
            first.append((start, rows[:, HEAD_DIM:], raw))
        second = []
        lse = []
        for (block, pair), (start, values, raw) in zip(todo, first):
            here = slice(pair * 2 * SPAN, (pair + 1) * 2 * SPAN)
            scores, _ = pair_scores(
                raw,
                factors[pl.ds(start, 3 * SPAN), :],
                ids[pl.ds(start, 3 * SPAN), :],
                info[block, 0:1, here],
                info[block, 1:2, here],
            )
            top = jnp.max(
                jnp.maximum(jnp.maximum(scores[0], scores[1]), scores[2]), axis=0, keepdims=True
            )
            weights = [jnp.exp(score - top) for score in scores]
            total = jnp.sum(weights[0] + weights[1] + weights[2], axis=0, keepdims=True)
            scale = 1.0 / total
            second.append(jnp.concatenate([weight * scale for weight in weights]).astype(BF))
            lse.append(top + jnp.log(total))
        for (block, pair), (start, values, raw), probs in zip(todo, first, second):
            here = slice(pair * 2 * SPAN, (pair + 1) * 2 * SPAN)
            heads_out[block, here, :HEAD_DIM] = dot_tn(probs, values).astype(BF)
        row = lax.broadcasted_iota(jnp.int32, (PARTS, tokens), 0)
        for at in range(FORWARD_BATCH):
            block = step * FORWARD_BATCH + at
            high, mid, low = three_parts(
                jnp.concatenate(lse[at * pairs : (at + 1) * pairs], axis=1)
            )
            flat = jnp.where(
                row == 0, high, jnp.where(row == 1, mid, jnp.where(row == 2, low, 0.0))
            )
            heads_out[block, :, HEAD_DIM : HEAD_DIM + PARTS] = jnp.transpose(flat).astype(BF)
        return carry

    lax.fori_loop(0, blocks // FORWARD_BATCH, attend, 0)

    def unplace(block, carry):
        hot = hot_rows(info[block, 2:3, :], slots)
        part = dot_nn(hot, heads_out[block]).astype(BF)
        lanes[:, pl.ds(block, 1)] = part.reshape(blocks, 1, CAP_ROWS, width)
        return carry

    lax.fori_loop(0, blocks, unplace, 0, unroll=4)

    for offset, out in enumerate((out_0, out_1, out_2, out_3)):

        def unpack(group, carry, offset=offset, out=out):
            source = group * rounds + lax.bitwise_xor(turn, offset)
            cols = jnp.transpose(info[source])
            hot = hot_cols(cols[:, 3:4], slots)
            part = dot_nn(hot, lanes[source].reshape(slots, width))
            out[group, 0:tokens, :] = part[:, :HEAD_DIM].astype(BF)
            flat = jnp.transpose(part[:, HEAD_DIM:])[0:PARTS, :].astype(BF)
            for piece in range(tokens // HEAD_DIM):
                first = tokens + piece * PARTS
                out[group, first : first + PARTS, :] = flat[
                    :, piece * HEAD_DIM : (piece + 1) * HEAD_DIM
                ]
            return carry

        lax.fori_loop(0, blocks // rounds, unpack, 0, unroll=4)


def tall_parts(ref, group, first, tokens):
    flat = jnp.concatenate(
        [
            ref[group, first + piece * PARTS : first + (piece + 1) * PARTS, :].astype(F32)
            for piece in range(tokens // HEAD_DIM)
        ],
        axis=1,
    )
    return jnp.transpose(flat)


def put_parts(ref, group, first, column):
    tokens = column.shape[0]
    high, mid, low = three_parts(column)
    lane = lax.broadcasted_iota(jnp.int32, (tokens, PARTS), 1)
    tall = jnp.where(lane == 0, high, jnp.where(lane == 1, mid, jnp.where(lane == 2, low, 0.0)))
    flat = jnp.transpose(tall).astype(BF)
    for piece in range(tokens // HEAD_DIM):
        at = first + piece * PARTS
        ref[group, at : at + PARTS, :] = flat[:, piece * HEAD_DIM : (piece + 1) * HEAD_DIM]


def combined(refs, group):
    tokens = refs[0].shape[1] // (HEAD_DIM + PARTS) * HEAD_DIM
    lse = []
    for ref in refs:
        tall = tall_parts(ref, group, tokens, tokens)
        lse.append(tall[:, 0:1] + tall[:, 1:2] + tall[:, 2:3])
    top = lse[0]
    for other in lse[1:]:
        top = jnp.maximum(top, other)
    weights = [jnp.exp(one - top) for one in lse]
    total = sum(weights[1:], weights[0])
    scale = 1.0 / total
    rows = [
        (weight * scale) * ref[group, 0:tokens, :].astype(F32)
        for weight, ref in zip(weights, refs)
    ]
    return sum(rows[1:], rows[0]), top + jnp.log(total)


def pair_kernel(a, b, out):
    tokens = out.shape[1] // (HEAD_DIM + PARTS) * HEAD_DIM
    for group in range(out.shape[0]):
        rows, lse = combined((a, b), group)
        out[group, 0:tokens, :] = rows.astype(BF)
        put_parts(out, group, tokens, lse)


def final_kernel(a, b, c, mixed, total_lse):
    for group in range(mixed.shape[0]):
        rows, lse = combined((a, b, c), group)
        mixed[group] = rows.astype(BF)
        put_parts(total_lse, group, 0, lse)


def backward_kernel(
    place,
    g_0,
    g_1,
    g_2,
    g_3,
    l_0,
    l_1,
    l_2,
    l_3,
    kept_rows,
    info,
    out_0,
    out_1,
    out_2,
    out_3,
    lanes,
    sums,
    factors,
    ids,
    rows_in,
    stats,
):
    blocks, tokens = info.shape[0], info.shape[2]
    slots = blocks * CAP_ROWS
    width = kept_rows.shape[1]
    pairs = tokens // (2 * SPAN)

    for offset, grads, lse in ((0, g_0, l_0), (1, g_1, l_1), (2, g_2, l_2), (3, g_3, l_3)):

        def pack(group, carry, offset=offset, grads=grads, lse=lse):
            source = group * ROUNDS + lax.bitwise_xor(place[0], offset)
            hot = hot_rows(info[source, 3:4, :], slots)
            tall = [tall_parts(grads, group, tokens, tokens), tall_parts(lse, group, 0, tokens)]
            tall.append(jnp.zeros((tokens, HEAD_DIM - 2 * PARTS), F32))
            rows = jnp.concatenate(
                [grads[group, 0:tokens, :], jnp.concatenate(tall, axis=1).astype(BF)], axis=1
            )
            part = dot_nn(hot, rows).astype(BF)
            lanes[:, pl.ds(source, 1)] = part.reshape(blocks, 1, CAP_ROWS, width)
            return carry

        lax.fori_loop(0, blocks // ROUNDS, pack, 0, unroll=4)

    sums[0:SPAN, :] = jnp.zeros((SPAN, width), F32)

    def place_rows(block, carry):
        cols = jnp.transpose(info[block])
        hot = hot_cols(cols[:, 2:3], slots)
        part = dot_nn(hot, lanes[block].reshape(slots, width))
        rows_in[block] = part[:, :HEAD_DIM].astype(BF)
        flat = jnp.transpose(part[:, HEAD_DIM:])
        stats[block, 0:1, :] = flat[0:1] + flat[1:2] + flat[2:3]
        stats[block, 1:2, :] = flat[PARTS : PARTS + 1] + (
            flat[PARTS + 1 : PARTS + 2] + flat[PARTS + 2 : PARTS + 3]
        )
        start = pl.multiple_of(SPAN + block * tokens, SPAN)
        keys = kept_rows[pl.ds(start, tokens), :HEAD_DIM]
        keep_columns(factors, ids, start, keys, cols)
        return carry

    lax.fori_loop(0, blocks, place_rows, 0, unroll=4)
    for held in (factors, ids):
        held[0:SPAN, :] = held[blocks * tokens : blocks * tokens + SPAN, :]

    def attend(step, carry):
        todo = [(step * BACKWARD_BATCH + at // pairs, at % pairs) for at in range(BACKWARD_BATCH * pairs)]
        first = []
        for block, pair in todo:
            start = pl.multiple_of(block * tokens + pair * 2 * SPAN, SPAN)
            here = slice(pair * 2 * SPAN, (pair + 1) * 2 * SPAN)
            rows = kept_rows[pl.ds(start, 3 * SPAN), :]
            keys = rows[:, :HEAD_DIM]
            queries = rows[SPAN:, :HEAD_DIM]
            grads = rows_in[block, here, :]
            raw = dot_nt(keys, queries)
            back = dot_nt(rows[:, HEAD_DIM:], grads)
            first.append((start, keys, queries, grads, raw, back))
        second = []
        for (block, pair), (start, keys, queries, grads, raw, back) in zip(todo, first):
            here = slice(pair * 2 * SPAN, (pair + 1) * 2 * SPAN)
            factor = factors[pl.ds(start, 3 * SPAN), :]
            scores, masks = pair_scores(
                raw,
                factor,
                ids[pl.ds(start, 3 * SPAN), :],
                info[block, 0:1, here],
                info[block, 1:2, here],
            )
            pull = stats[block, 0:1, here]
            total_lse = stats[block, 1:2, here]
            weights = [jnp.exp(score - total_lse) for score in scores]
            weights_all = jnp.concatenate(weights).astype(BF)
            grad_score = jnp.concatenate(
                [
                    jnp.where(
                        mask, weight * (back[chunk * SPAN : (chunk + 1) * SPAN] - pull), 0.0
                    )
                    for chunk, (mask, weight) in enumerate(zip(masks, weights))
                ]
            )
            slope = jnp.sum(grad_score * raw, axis=1, keepdims=True)
            drift = slope * (factor * factor * factor * HEAD_DIM) * keys.astype(F32)
            second.append(((grad_score * factor).astype(BF), weights_all, drift))
        for (start, keys, queries, grads, _, _), (grad_raw, weights_all, drift) in zip(
            first, second
        ):
            grad_val = dot_nn(weights_all, grads)
            grad_key = dot_nn(grad_raw, queries) - drift
            grad_query = dot_tn(grad_raw, keys)
            sums[pl.ds(start, SPAN), :] += jnp.concatenate(
                [grad_key[:SPAN], grad_val[:SPAN]], axis=1
            )
            after = pl.multiple_of(start + SPAN, SPAN)
            sums[pl.ds(after, 2 * SPAN), :] = jnp.concatenate(
                [grad_query + grad_key[SPAN:], grad_val[SPAN:]], axis=1
            )
        return carry

    lax.fori_loop(0, blocks // BACKWARD_BATCH, attend, 0)
    sums[blocks * tokens : blocks * tokens + SPAN, :] += sums[0:SPAN, :]

    def unplace(block, carry):
        hot = hot_rows(info[block, 2:3, :], slots)
        start = pl.multiple_of(SPAN + block * tokens, SPAN)
        part = dot_nn(hot, sums[pl.ds(start, tokens), :].astype(BF)).astype(BF)
        lanes[:, pl.ds(block, 1)] = part.reshape(blocks, 1, CAP_ROWS, width)
        return carry

    lax.fori_loop(0, blocks, unplace, 0, unroll=4)

    for offset, out in enumerate((out_0, out_1, out_2, out_3)):

        def unpack(group, carry, offset=offset, out=out):
            source = group * ROUNDS + lax.bitwise_xor(place[0], offset)
            cols = jnp.transpose(info[source])
            hot = hot_cols(cols[:, 3:4], slots)
            start = pl.multiple_of(group * tokens, tokens)
            part = dot_nn(hot, lanes[source].reshape(slots, width))
            out[pl.ds(start, tokens), :] = part.astype(BF)
            return carry

        lax.fori_loop(0, blocks // ROUNDS, unpack, 0, unroll=4)


def in_vmem(count):
    return [pl.BlockSpec(memory_space=pltpu.VMEM)] * count


def run_kernel(kernel, name, operands, shapes, scratch, scalar):
    first = [pl.BlockSpec(memory_space=pltpu.SMEM)] if scalar else []
    return pl.pallas_call(
        kernel,
        out_shape=tuple(jax.ShapeDtypeStruct(shape, BF) for shape in shapes),
        in_specs=first + in_vmem(len(operands) - len(first)),
        out_specs=tuple(in_vmem(len(shapes))),
        scratch_shapes=[pltpu.VMEM(shape, dtype) for shape, dtype in scratch],
        compiler_params=pltpu.CompilerParams(vmem_limit_bytes=48 << 20),
        cost_estimate=pl.CostEstimate(
            flops=20 * 10**9 if scalar else 10**7,
            bytes_accessed=12 * 10**6 if scalar else 2 * 10**6,
            transcendentals=10**6 if scalar else 10**4,
        ),
        name=name,
    )(*operands)


def run_forward(turn, rows, info):
    blocks, _, tokens = info.shape
    width = rows[0].shape[1]
    tall = tokens + PARTS * tokens // HEAD_DIM
    return run_kernel(
        forward_kernel,
        "hash_forward",
        (turn, *rows, info),
        [(blocks // ROUNDS, tall, HEAD_DIM)] * ROUNDS + [(SPAN + blocks * tokens, width)],
        [((blocks, blocks, CAP_ROWS, width), BF), ((blocks, tokens, width), BF)]
        + [((SPAN + blocks * tokens, HEAD_DIM), F32)] * 2,
        True,
    )


def run_backward(turn, grads, lse, kept_rows, info):
    blocks, _, tokens = info.shape
    width = kept_rows.shape[1]
    return run_kernel(
        backward_kernel,
        "hash_backward",
        (turn, *grads, *lse, kept_rows, info),
        [(blocks * tokens // ROUNDS, width)] * ROUNDS,
        [((blocks, blocks, CAP_ROWS, width), BF), ((SPAN + blocks * tokens, width), F32)]
        + [((SPAN + blocks * tokens, HEAD_DIM), F32)] * 2
        + [((blocks, tokens, HEAD_DIM), BF), ((blocks, 8, tokens), F32)],
        True,
    )


def merge_pair(a, b):
    return run_kernel(pair_kernel, "merge_pair", (a, b), [a.shape], [], False)[0]


def merge_final(a, b, c):
    groups, tall, width = a.shape
    tokens = tall // (HEAD_DIM + PARTS) * HEAD_DIM
    shapes = [(groups, tokens, width), (groups, tall - tokens, width)]
    return run_kernel(final_kernel, "merge_final", (a, b, c), shapes, [], False)


def peers(mask):
    size = HEADS * ROUNDS
    return [(i, i ^ mask) for i in range(size)]


def swap(x, mask):
    return lax.ppermute(x, "seq", peers(mask))


def columns():
    return [[head * ROUNDS + turn for head in range(HEADS)] for turn in range(ROUNDS)]


def rows_of():
    return [[head * ROUNDS + turn for turn in range(ROUNDS)] for head in range(HEADS)]


def gather_group(x):
    side = swap(x, 2)
    return (x, swap(x, 1), side, swap(side, 1))


def sum_group(parts):
    near = parts[0] + swap(parts[1].astype(BF), 1).astype(F32)
    far = parts[2] + swap(parts[3].astype(BF), 1).astype(F32)
    return near + swap(far.astype(BF), 2).astype(F32)


def row_major(x):
    return with_layout_constraint(x.astype(BF), Layout(major_to_minor=(0, 1)))


def exchange(x, groups=None):
    return lax.all_to_all(
        x, "seq", split_axis=0, concat_axis=0, tiled=True, axis_index_groups=groups
    )


def rounded(x):
    return lax.reduce_precision(x, 8, 7)


def split_three(wide):
    high = rounded(wide)
    rest = wide - high
    mid = rounded(rest)
    return jnp.stack([high, mid, rest - mid])


def slots_sent(target, tokens, capacity):
    device = target // tokens
    early = jnp.arange(tokens)[None, :] < jnp.arange(tokens)[:, None]
    same = (device[:, None] == device[None, :]) & early
    return device * capacity + jnp.sum(same.astype(jnp.int32), axis=1)


def start_of(token_ids, doc_ends):
    ends = doc_ends[None, :]
    return jnp.max(jnp.where(ends <= token_ids[:, None], ends, 0), axis=1)


def shards_fast(
    x_first,
    x_second,
    w_qk,
    w_value,
    w_out,
    gain_attn,
    bias_attn,
    gain_ffn,
    bias_ffn,
    w_up,
    bias_up,
    w_down,
    bias_down,
    sort_order,
    inverse,
    lengths,
    dy_first,
    dy_second,
):
    devices = lax.axis_size("seq")
    tokens, features = x_first.shape
    capacity = 2 * tokens // devices
    shard = features // devices
    place = lax.axis_index("seq")
    doc_ends = jnp.cumsum(lengths)

    per_round = []
    vectors = rounded(
        jnp.concatenate([gain_attn, bias_attn, gain_ffn, bias_ffn, bias_up, bias_down])
    )
    vectors = jnp.pad(vectors, (0, 2 * tokens - vectors.shape[0])).reshape(2, tokens)
    for turn in range(ROUNDS):
        ids = sort_order[turn]
        rows = jnp.stack(
            [
                ids,
                start_of(ids, doc_ends),
                recv_slots(ids, tokens, capacity),
                slots_sent(inverse[turn], tokens, capacity),
            ]
        ).astype(F32)
        split = jnp.stack([ids // SPAN * SPAN, ids % SPAN]).astype(F32)
        per_round.append(jnp.concatenate([rows, vectors, split]))
    info = jnp.tile(jnp.stack(per_round), (HEADS, 1, 1))
    info = exchange(info)
    got = info[:, 4:6].reshape(devices, 2 * tokens)

    def vector(first, size):
        return got[:, first : first + size].reshape(devices * size)

    gain_one, shift_one = vector(0, shard), vector(shard, shard)
    gain_two, shift_two = vector(2 * shard, shard), vector(3 * shard, shard)
    wide = bias_up.shape[0]
    b_up = vector(4 * shard, wide)
    b_down = vector(4 * shard + wide, shard)
    m_pair = lax.all_gather(
        jnp.concatenate([w_qk.astype(BF), w_value.astype(BF)], axis=1), "seq", axis=0, tiled=True
    )
    half = HEADS * wide
    up_cols = jnp.transpose(
        w_up.astype(BF).reshape(shard, HEADS, ROUNDS, wide), (2, 0, 1, 3)
    ).reshape(ROUNDS, shard, half)
    out_rows = jnp.broadcast_to(w_out.astype(BF), (ROUNDS, shard, features))
    near_rows = exchange(jnp.concatenate([up_cols, out_rows], axis=2), rows_of())
    near_rows = near_rows.reshape(ROUNDS * shard, half + features)
    b_up = lax.dynamic_index_in_dim(
        b_up.reshape(HEADS, ROUNDS, wide), place % ROUNDS, axis=1, keepdims=False
    ).reshape(HEADS * wide)

    normed_one, hat_one, inv_one = layer_norm(x_second, gain_one, shift_one)
    grad_f = dy_second.astype(BF)
    normed_one, near_rows, grad_f_all = lax.optimization_barrier(
        (normed_one.astype(BF), near_rows, gather_group(grad_f))
    )
    grad_f_all = jnp.concatenate(grad_f_all)
    rows = linear(normed_one, m_pair).astype(BF)
    rows = jnp.transpose(rows.reshape(tokens, 2, HEADS, HEAD_DIM), (2, 0, 1, 3))
    own = exchange(rows.reshape(HEADS, tokens, 2 * HEAD_DIM), columns()).reshape(HEADS * tokens, 2 * HEAD_DIM)
    own, near_rows = lax.optimization_barrier((own, near_rows))
    m_ffn = lax.all_gather(
        jnp.concatenate([near_rows, w_down.astype(BF)], axis=1),
        "seq",
        axis=0,
        tiled=True,
        axis_index_groups=columns(),
    )
    turn = (place % ROUNDS).astype(jnp.int32).reshape(1)
    *sent, kept_rows = run_forward(turn, gather_group(own), info)
    far = merge_pair(sent[2], swap(sent[3], 1))
    mixed, total_lse = merge_final(sent[0], swap(sent[1], 1), swap(far, 2))
    mixed = exchange(mixed, columns())
    m_ffn, normed_one = lax.optimization_barrier((m_ffn, normed_one))
    m_up, m_out, m_down = (m_ffn[:, at : at + features] for at in (0, half, half + features))
    grad_hidden = outer_cols(grad_f_all, m_down)
    mixed, grad_hidden, total_lse = lax.optimization_barrier(
        (mixed, grad_hidden, gather_group(total_lse))
    )
    normed_col = lax.all_gather(
        normed_one, "seq", axis=0, tiled=True, axis_index_groups=columns()
    )
    mixed = jnp.transpose(mixed, (1, 0, 2)).reshape(tokens, features)
    y_first = x_first + linear(mixed, m_out)
    normed_two, hat_two, inv_two = layer_norm(y_first, gain_two, shift_two)
    normed_two = normed_two.astype(BF)
    side = swap(normed_two, 2)
    halves = (
        jnp.concatenate([normed_two, swap(normed_two, 1)]),
        jnp.concatenate([side, swap(side, 1)]),
    )
    found = []
    for at, rows in enumerate(halves):
        pre_up = linear(rows, m_up) + b_up
        hidden, gelu_back = jax.vjp(partial(jax.nn.gelu, approximate=True), pre_up)
        grad_pre = grad_hidden[at * 2 * tokens : (at + 1) * 2 * tokens]
        grad_pre = gelu_back(grad_pre)[0].astype(BF)
        grad_two = outer_cols(grad_pre, m_up)
        found.append((hidden.astype(BF), grad_pre, grad_two[:tokens], grad_two[tokens:]))
    normed_all = jnp.concatenate(halves)
    hidden, grad_pre = (jnp.concatenate([found[0][at], found[1][at]]) for at in range(2))
    grad_down = inner_rows(hidden, grad_f_all)
    grad_bias_down = jnp.sum(grad_f.astype(F32), axis=0)
    grad_up = inner_rows(normed_all, grad_pre)
    grad_bias_up = jnp.sum(grad_pre.astype(F32), axis=0)
    grad_two = sum_group([*found[0][2:], *found[1][2:]])
    grad_gain_ffn = jnp.sum(grad_two * hat_two, axis=0)
    grad_bias_ffn = jnp.sum(grad_two, axis=0)
    dx_first = dy_first + norm_back(grad_two, hat_two, inv_two, gain_two)
    grad_attn = dx_first.astype(BF)
    grad_out = inner_rows(mixed, grad_attn)
    fourth = features // ROUNDS
    grad_mixed = outer_cols(grad_attn, m_out).astype(BF)
    pull = jnp.sum(
        (grad_mixed.astype(F32) * mixed.astype(F32)).reshape(tokens, HEADS, HEAD_DIM), axis=-1
    )
    parts = split_three(jnp.transpose(pull))
    parts = jnp.pad(parts, ((0, PARTS - 3), (0, 0), (0, 0)))
    parts = jnp.transpose(parts.reshape(PARTS, HEADS, -1, HEAD_DIM), (1, 2, 0, 3))
    parts = parts.reshape(HEADS, -1, HEAD_DIM).astype(BF)
    grad_mixed = jnp.transpose(grad_mixed.reshape(tokens, HEADS, HEAD_DIM), (1, 0, 2))
    grad_mixed, normed_col = lax.optimization_barrier(
        (jnp.concatenate([grad_mixed, parts], axis=1), normed_col)
    )
    grad_mixed = exchange(grad_mixed, columns())
    grad_out = sum_group(
        [
            lax.dynamic_slice_in_dim(grad_out, ((place % ROUNDS) ^ near) * fourth, fourth, axis=1)
            for near in range(ROUNDS)
        ]
    )
    merged = jnp.concatenate([row_major(x) for x in (grad_up, grad_out, grad_down)], axis=1)
    grad_mixed, merged = lax.optimization_barrier((grad_mixed, merged))
    grad_mixed = list(gather_group(grad_mixed))
    merged, normed_col, grad_mixed[1] = lax.optimization_barrier(
        (merged, normed_col, grad_mixed[1])
    )
    merged = lax.psum_scatter(
        merged, "seq", scatter_dimension=0, tiled=True, axis_index_groups=columns()
    )
    s_down = merged[:, half + fourth :].astype(F32)
    merged = merged[:, : half + fourth].reshape(ROUNDS, shard, -1)
    pieces = [
        lax.dynamic_index_in_dim(merged, (place % ROUNDS) ^ near, axis=0, keepdims=False)
        for near in range(ROUNDS)
    ]
    pieces = [swap(piece, near) if near else piece for near, piece in enumerate(pieces)]

    def in_order(first, last):
        mine = place % ROUNDS
        found = []
        for peer in range(ROUNDS):
            options = [pieces[peer ^ at][:, first:last] for at in range(ROUNDS)]
            low = jnp.where(mine == 0, options[0], options[1])
            high = jnp.where(mine == 2, options[2], options[3])
            found.append(jnp.where(mine < 2, low, high))
        return jnp.stack(found, axis=1).astype(F32)

    s_up = in_order(0, half).reshape(shard, ROUNDS, HEADS, wide)
    s_up = jnp.transpose(s_up, (0, 2, 1, 3)).reshape(shard, ROUNDS * half)
    s_out = in_order(half, half + fourth).reshape(shard, features)

    grad_head = run_backward(
        turn, grad_mixed, total_lse, kept_rows, info
    )
    near_head = grad_head[0].astype(F32) + swap(grad_head[1], 1).astype(F32)
    far_head = grad_head[2].astype(F32) + swap(grad_head[3], 1).astype(F32)
    far_head, hidden = lax.optimization_barrier((far_head.astype(BF), hidden))
    far_head = swap(far_head, 2)
    branch = linear(hidden, m_down).reshape(ROUNDS, tokens, features)
    branch_near = branch[0] + swap(branch[1].astype(BF), 1).astype(F32)
    branch_far = (branch[2] + swap(branch[3].astype(BF), 1).astype(F32)).astype(BF)
    far_head, near_head, branch_near, branch_far, grad_bias_up, grad_bias_down = (
        lax.optimization_barrier(
            (far_head, near_head, branch_near, branch_far, grad_bias_up, grad_bias_down)
        )
    )
    grad_head = (near_head + far_head.astype(F32)).astype(BF)
    branch = branch_near + swap(branch_far, 2).astype(F32)
    y_second = x_second + (branch + b_down)
    grad_rows = exchange(grad_head.reshape(HEADS, tokens, 2 * HEAD_DIM), columns())
    s_pair = inner_rows(normed_col, grad_head).astype(BF).reshape(devices, shard, 2 * HEAD_DIM)
    grad_rows, s_pair, s_up, s_out, s_down, y_second = lax.optimization_barrier(
        (grad_rows, s_pair, s_up, s_out, s_down, y_second)
    )
    grad_rows = grad_rows.reshape(HEADS, tokens, 2, HEAD_DIM)
    grad_rows = jnp.transpose(grad_rows, (1, 2, 0, 3)).reshape(tokens, 2 * features)
    grad_one = outer_cols(grad_rows, m_pair)
    grad_gain_attn = jnp.sum(grad_one * hat_one, axis=0)
    grad_bias_attn = jnp.sum(grad_one, axis=0)
    dx_second = dy_second + norm_back(grad_one, hat_one, inv_one, gain_one)
    is_mine = (jnp.arange(ROUNDS) == place % ROUNDS).astype(F32)
    grad_bias_up = grad_bias_up.reshape(HEADS, 1, wide) * is_mine[None, :, None]
    small = jnp.concatenate(
        [
            grad_gain_attn.reshape(devices, -1),
            grad_bias_attn.reshape(devices, -1),
            grad_gain_ffn.reshape(devices, -1),
            grad_bias_ffn.reshape(devices, -1),
            grad_bias_up.reshape(devices, -1),
            grad_bias_down.reshape(devices, -1),
        ],
        axis=1,
    )
    count = small.shape[1]
    lines = -(-3 * count // (2 * HEAD_DIM))
    small = jnp.transpose(split_three(small), (1, 0, 2)).reshape(devices, 3 * count)
    small = jnp.pad(small, ((0, 0), (0, lines * 2 * HEAD_DIM - 3 * count)))
    small = small.astype(BF).reshape(devices, lines, 2 * HEAD_DIM)
    both = exchange(jnp.concatenate([s_pair, small], axis=1))
    small = both[:, shard:].reshape(devices, -1)[:, : 3 * count].astype(F32)
    small = jnp.sum(small.reshape(devices * 3, count), axis=0)
    s_pair = both[:, :shard].reshape(HEADS, ROUNDS, shard, 2, HEAD_DIM)
    s_pair = jnp.sum(s_pair.astype(F32), axis=1).transpose(2, 1, 0, 3)
    s_qk = s_pair[0].reshape(shard, features)
    s_value = s_pair[1].reshape(shard, features)
    s_gattn, s_battn, s_gffn, s_bffn = (small[i * shard : (i + 1) * shard] for i in range(4))
    s_bup = small[4 * shard : 4 * shard + wide]
    s_bdown = small[4 * shard + wide :]
    return (
        y_first,
        y_second,
        dx_first,
        dx_second,
        s_qk,
        s_value,
        s_out,
        s_gattn,
        s_battn,
        s_gffn,
        s_bffn,
        s_up,
        s_bup,
        s_down,
        s_bdown,
    )


def solution(mesh):
    in_specs = (
        P("seq", None),
        P("seq", None),
        P("seq", None),
        P("seq", None),
        P("seq", None),
        P("seq"),
        P("seq"),
        P("seq"),
        P("seq"),
        P("seq", None),
        P("seq"),
        P("seq", None),
        P("seq"),
        P(None, "seq"),
        P(None, "seq"),
        P(),
        P("seq", None),
        P("seq", None),
    )
    out_specs = (
        P("seq", None),
        P("seq", None),
        P("seq", None),
        P("seq", None),
        P("seq", None),
        P("seq", None),
        P("seq", None),
        P("seq"),
        P("seq"),
        P("seq"),
        P("seq"),
        P("seq", None),
        P("seq"),
        P("seq", None),
        P("seq"),
    )
    fast = mesh.shape["seq"] == HEADS * ROUNDS
    return jax.shard_map(shards_fast if fast else shards, mesh=mesh, in_specs=in_specs, out_specs=out_specs, check_vma=False)
```

```python
from functools import partial
import math

import jax
import jax.numpy as jnp
from jax import lax
from jax.experimental import pallas as pl
from jax.experimental.layout import Layout, with_layout_constraint
from jax.experimental.pallas import tpu as pltpu
from jax.sharding import PartitionSpec as P

HEADS = 8
HEAD_DIM = 128
SPAN = 64
ROUNDS = 4

EPSILON = 1e-05
SCALE = 1.0 / math.sqrt(HEAD_DIM)
BF = jnp.bfloat16
F32 = jnp.float32


def shifted(x, axis, by):
    size = lax.axis_size(axis)
    return lax.ppermute(x, axis, [(i, (i + by) % size) for i in range(size)])


def as_sent(x):
    return jax.tree.map(lambda a: a.astype(jnp.bfloat16) if a.dtype == jnp.float32 else a, x)


def layer_norm(inputs, norm_gain, norm_shift):
    centered = inputs - jnp.mean(inputs, axis=-1, keepdims=True)
    inv_std = lax.rsqrt(jnp.mean(centered * centered, axis=-1, keepdims=True) + EPSILON)
    normed = centered * inv_std
    return (normed * norm_gain + norm_shift, normed, inv_std)


def norm_back(grad_rows, normed, inv_std, norm_gain):
    grad_hat = grad_rows * norm_gain
    return inv_std * (
        grad_hat
        - jnp.mean(grad_hat, axis=-1, keepdims=True)
        - normed * jnp.mean(grad_hat * normed, axis=-1, keepdims=True)
    )


def linear(matrix_a, matrix_b):
    return jnp.dot(matrix_a, matrix_b, preferred_element_type=jnp.float32)


def inner_rows(matrix_a, matrix_b):
    return lax.dot_general(
        matrix_a, matrix_b, (((0,), (0,)), ((), ())), preferred_element_type=jnp.float32
    )


def outer_cols(matrix_a, matrix_b):
    return lax.dot_general(
        matrix_a, matrix_b, (((1,), (1,)), ((), ())), preferred_element_type=jnp.float32
    )


def segment_of(token_ids, doc_ends):
    return jnp.sum((token_ids[:, None] >= doc_ends[None, :]).astype(jnp.int32), axis=1)


def send_slots(target, tokens, devices, capacity):
    device = target // tokens
    onehot = (device[:, None] == jnp.arange(devices, dtype=jnp.int32)[None, :]).astype(jnp.int32)
    rank_in = jnp.sum(jnp.cumsum(onehot, axis=0) * onehot, axis=1) - 1
    return device * capacity + rank_in


def recv_slots(source_ids, tokens, capacity):
    device = source_ids // tokens
    earlier = (device[:, None] == device[None, :]) & (source_ids[None, :] < source_ids[:, None])
    return device * capacity + jnp.sum(earlier.astype(jnp.int32), axis=1)


def packed(inputs, slot_ids, devices, capacity):
    filled = (
        jnp.zeros((devices * capacity,) + inputs.shape[1:], inputs.dtype).at[slot_ids].set(inputs)
    )
    return filled.reshape((devices, capacity) + inputs.shape[1:])


def unpacked(received, slot_ids):
    return received.reshape((-1,) + received.shape[2:])[slot_ids]


def spanned(inputs, before):
    blocks = inputs.shape[0] // SPAN
    current = inputs.reshape((blocks, SPAN) + inputs.shape[1:])
    earlier = jnp.concatenate([before[None], current[:-1]], axis=0)
    return (current, jnp.concatenate([earlier, current], axis=1))


def arrange(got_qk, got_value, recv_slot):
    sorted_qk = unpacked(got_qk, recv_slot)
    sorted_value = unpacked(got_value, recv_slot)
    last_block = jnp.stack([sorted_qk[-SPAN:], sorted_value[-SPAN:]])
    return (sorted_qk, sorted_value, last_block)


def score_parts(sorted_rows, query_ids, before_ids, doc_ends):
    sorted_qk, sorted_value, before_qk, before_value = sorted_rows
    current, key_rows = spanned(sorted_qk, before_qk)
    _, value_keys = spanned(sorted_value, before_value)
    current_ids, key_ids = spanned(query_ids, before_ids)
    current_seg, key_seg = spanned(
        segment_of(query_ids, doc_ends), segment_of(before_ids, doc_ends)
    )
    blocks = current.shape[0]
    q_heads = current.reshape(blocks, SPAN, HEADS, HEAD_DIM)
    k_heads = key_rows.reshape(blocks, 2 * SPAN, HEADS, HEAD_DIM)
    v_heads = value_keys.reshape(blocks, 2 * SPAN, HEADS, HEAD_DIM)
    raw_dots = jnp.einsum("gihd,gjhd->ghij", q_heads, k_heads, preferred_element_type=jnp.float32)
    k_float = k_heads.astype(jnp.float32)
    key_norm = lax.rsqrt(jnp.sum(k_float * k_float, axis=-1))
    factor = jnp.transpose(key_norm, (0, 2, 1))[:, :, None, :] / math.sqrt(HEAD_DIM)
    allowed = (
        (key_ids[:, None, :] <= current_ids[:, :, None])
        & (key_seg[:, None, :] == current_seg[:, :, None])
    )[:, None]
    itself = (key_ids[:, None, :] == current_ids[:, :, None])[:, None]
    scores = jnp.where(itself, -100000.0, jnp.where(allowed, raw_dots * factor, -1000000000.0))
    log_total = jax.nn.logsumexp(scores, axis=-1)
    attn_probs = jnp.exp(scores - log_total[..., None])
    kept_mask = allowed & jnp.logical_not(itself)
    return (
        q_heads,
        k_heads,
        v_heads,
        k_float,
        key_norm,
        factor,
        kept_mask,
        raw_dots,
        attn_probs,
        log_total,
    )


def attend_out(pieces):
    (
        q_heads,
        k_heads,
        v_heads,
        k_float,
        key_norm,
        factor,
        kept_mask,
        raw_dots,
        attn_probs,
        log_total,
    ) = pieces
    blocks = q_heads.shape[0]
    out_heads = jnp.einsum(
        "ghij,gjhd->gihd",
        attn_probs.astype(jnp.bfloat16),
        v_heads,
        preferred_element_type=jnp.float32,
    )
    return (
        out_heads.reshape(blocks * SPAN, -1),
        jnp.transpose(log_total, (0, 2, 1)).reshape(blocks * SPAN, HEADS),
    )


def attend_back(pieces, grad_rows, grad_total):
    (
        q_heads,
        k_heads,
        v_heads,
        k_float,
        key_norm,
        factor,
        kept_mask,
        raw_dots,
        attn_probs,
        log_total,
    ) = pieces
    blocks = q_heads.shape[0]
    grad_heads = grad_rows.astype(jnp.bfloat16).reshape(blocks, SPAN, HEADS, HEAD_DIM)
    grad_lse = jnp.transpose(grad_total.reshape(blocks, SPAN, HEADS), (0, 2, 1))
    grad_prob = jnp.einsum(
        "gihd,gjhd->ghij", grad_heads, v_heads, preferred_element_type=jnp.float32
    )
    grad_val = jnp.einsum(
        "ghij,gihd->gjhd",
        attn_probs.astype(jnp.bfloat16),
        grad_heads,
        preferred_element_type=jnp.float32,
    )
    row_dot = jnp.sum(attn_probs * grad_prob, axis=-1, keepdims=True)
    grad_score = jnp.where(kept_mask, attn_probs * (grad_prob - row_dot + grad_lse[..., None]), 0.0)
    grad_raw = (grad_score * factor).astype(jnp.bfloat16)
    grad_norm = jnp.transpose(jnp.sum(grad_score * raw_dots, axis=2), (0, 2, 1)) / math.sqrt(
        HEAD_DIM
    )
    norm_cube = key_norm * key_norm * key_norm
    grad_query = jnp.einsum(
        "ghij,gjhd->gihd", grad_raw, k_heads, preferred_element_type=jnp.float32
    )
    grad_key = (
        jnp.einsum("ghij,gihd->gjhd", grad_raw, q_heads, preferred_element_type=jnp.float32)
        - (grad_norm * norm_cube)[..., None] * k_float
    )
    return (
        grad_query.reshape(blocks, SPAN, -1),
        grad_key.reshape(blocks, 2 * SPAN, -1),
        grad_val.reshape(blocks, 2 * SPAN, -1),
    )


def shards(
    x_first,
    x_second,
    w_qk,
    w_value,
    w_out,
    gain_attn,
    bias_attn,
    gain_ffn,
    bias_ffn,
    w_up,
    bias_up,
    w_down,
    bias_down,
    sort_order,
    inverse,
    lengths,
    dy_first,
    dy_second,
):
    devices = lax.axis_size("seq")
    tokens = x_first.shape[0]
    capacity = 2 * tokens // devices
    gathered = (
        lax.all_gather(w_qk.astype(jnp.bfloat16), "seq", axis=0, tiled=True),
        lax.all_gather(w_value.astype(jnp.bfloat16), "seq", axis=0, tiled=True),
        lax.all_gather(w_out.astype(jnp.bfloat16), "seq", axis=0, tiled=True),
        lax.all_gather(gain_attn.astype(jnp.bfloat16), "seq", axis=0, tiled=True),
        lax.all_gather(bias_attn.astype(jnp.bfloat16), "seq", axis=0, tiled=True),
        lax.all_gather(gain_ffn.astype(jnp.bfloat16), "seq", axis=0, tiled=True),
        lax.all_gather(bias_ffn.astype(jnp.bfloat16), "seq", axis=0, tiled=True),
        lax.all_gather(w_up.astype(jnp.bfloat16), "seq", axis=0, tiled=True),
        lax.all_gather(bias_up.astype(jnp.bfloat16), "seq", axis=0, tiled=True),
        lax.all_gather(w_down.astype(jnp.bfloat16), "seq", axis=0, tiled=True),
        lax.all_gather(bias_down.astype(jnp.bfloat16), "seq", axis=0, tiled=True),
    )
    m_qk, m_value, m_out, g_attn, b_attn, g_ffn, b_ffn, m_up, b_up, m_down, b_down = gathered
    gain_one = g_attn.astype(jnp.float32)
    gain_two = g_ffn.astype(jnp.float32)
    doc_ends = jnp.cumsum(lengths)
    send_list = [send_slots(inverse[turn], tokens, devices, capacity) for turn in range(ROUNDS)]
    recv_list = [recv_slots(sort_order[turn], tokens, capacity) for turn in range(ROUNDS)]
    before_ids = shifted(sort_order[:, tokens - SPAN :], "seq", 1)
    normed_one, hat_one, inv_one = layer_norm(x_second, gain_one, b_attn.astype(jnp.float32))
    normed_one = normed_one.astype(jnp.bfloat16)
    qk_rows = linear(normed_one, m_qk).astype(jnp.bfloat16)
    value_rows = linear(normed_one, m_value).astype(jnp.bfloat16)
    stashed = []
    round_outs = []
    round_lse = []
    for turn in range(ROUNDS):
        got_qk, got_value = (
            lax.all_to_all(
                packed(qk_rows, send_list[turn], devices, capacity),
                "seq",
                split_axis=0,
                concat_axis=0,
                tiled=True,
            ),
            lax.all_to_all(
                packed(value_rows, send_list[turn], devices, capacity),
                "seq",
                split_axis=0,
                concat_axis=0,
                tiled=True,
            ),
        )
        sorted_qk, sorted_value, last_block = arrange(got_qk, got_value, recv_list[turn])
        before_block = shifted(last_block, "seq", 1)
        sorted_rows = (sorted_qk, sorted_value, before_block[0], before_block[1])
        pieces = score_parts(sorted_rows, sort_order[turn], before_ids[turn], doc_ends)
        out_sorted, lse_sorted = attend_out(pieces)
        back_out, back_lse = (
            lax.all_to_all(
                packed(out_sorted, recv_list[turn], devices, capacity),
                "seq",
                split_axis=0,
                concat_axis=0,
                tiled=True,
            ),
            lax.all_to_all(
                packed(lse_sorted, recv_list[turn], devices, capacity),
                "seq",
                split_axis=0,
                concat_axis=0,
                tiled=True,
            ),
        )
        round_outs.append(unpacked(back_out, send_list[turn]))
        round_lse.append(unpacked(back_lse, send_list[turn]))
        stashed.append(sorted_rows)
    lse_all = jnp.stack(round_lse)
    out_all = jnp.stack(round_outs).reshape(ROUNDS, tokens, HEADS, HEAD_DIM)
    merge = jnp.exp(lse_all - jax.nn.logsumexp(lse_all, axis=0))
    mixed = jnp.sum(merge[..., None] * out_all, axis=0).reshape(tokens, -1).astype(jnp.bfloat16)
    y_first = x_first + linear(mixed, m_out)
    normed_two, hat_two, inv_two = layer_norm(y_first, gain_two, b_ffn.astype(jnp.float32))
    normed_two = normed_two.astype(jnp.bfloat16)
    pre_up = linear(normed_two, m_up) + b_up.astype(jnp.float32)
    hidden, gelu_back = jax.vjp(partial(jax.nn.gelu, approximate=True), pre_up)
    hidden = hidden.astype(jnp.bfloat16)
    y_second = x_second + (linear(hidden, m_down) + b_down.astype(jnp.float32))
    grad_f = dy_second.astype(jnp.bfloat16)
    grad_down = inner_rows(hidden, grad_f)
    grad_bias_down = jnp.sum(grad_f.astype(jnp.float32), axis=0)
    grad_pre = gelu_back(outer_cols(grad_f, m_down))[0].astype(jnp.bfloat16)
    grad_up = inner_rows(normed_two, grad_pre)
    grad_bias_up = jnp.sum(grad_pre.astype(jnp.float32), axis=0)
    grad_two = outer_cols(grad_pre, m_up)
    grad_gain_ffn = jnp.sum(grad_two * hat_two, axis=0)
    grad_bias_ffn = jnp.sum(grad_two, axis=0)
    dx_first = dy_first + norm_back(grad_two, hat_two, inv_two, gain_two)
    grad_attn = dx_first.astype(jnp.bfloat16)
    grad_out = inner_rows(mixed, grad_attn)
    grad_mixed = outer_cols(grad_attn, m_out).reshape(tokens, HEADS, HEAD_DIM)
    along = jnp.sum(grad_mixed[None] * out_all, axis=-1)
    grad_lse_all = merge * (along - jnp.sum(merge * along, axis=0, keepdims=True))
    grad_qk_sum = jnp.zeros((tokens, HEADS * HEAD_DIM), jnp.float32)
    grad_value_sum = jnp.zeros((tokens, HEADS * HEAD_DIM), jnp.float32)
    for turn in range(ROUNDS):
        grad_round = (merge[turn][..., None] * grad_mixed).reshape(tokens, -1)
        got_out, got_lse = (
            lax.all_to_all(
                packed(grad_round, send_list[turn], devices, capacity),
                "seq",
                split_axis=0,
                concat_axis=0,
                tiled=True,
            ),
            lax.all_to_all(
                packed(grad_lse_all[turn], send_list[turn], devices, capacity),
                "seq",
                split_axis=0,
                concat_axis=0,
                tiled=True,
            ),
        )
        sorted_grad_out = unpacked(got_out, recv_list[turn])
        sorted_grad_lse = unpacked(got_lse, recv_list[turn])
        sorted_rows = stashed[turn]
        pieces = score_parts(sorted_rows, sort_order[turn], before_ids[turn], doc_ends)
        grad_query, grad_key, grad_val = attend_back(pieces, sorted_grad_out, sorted_grad_lse)
        spill = shifted(
            jnp.stack([grad_key[0, :SPAN], grad_val[0, :SPAN]]).astype(jnp.bfloat16), "seq", -1
        ).astype(jnp.float32)
        key_add = jnp.concatenate([grad_key[1:, :SPAN], spill[0][None]], axis=0)
        value_add = jnp.concatenate([grad_val[1:, :SPAN], spill[1][None]], axis=0)
        sorted_grad_qk = (grad_query + grad_key[:, SPAN:] + key_add).reshape(tokens, -1)
        sorted_grad_value = (grad_val[:, SPAN:] + value_add).reshape(tokens, -1)
        back_qk, back_value = (
            lax.all_to_all(
                as_sent(packed(sorted_grad_qk, recv_list[turn], devices, capacity)),
                "seq",
                split_axis=0,
                concat_axis=0,
                tiled=True,
            ),
            lax.all_to_all(
                as_sent(packed(sorted_grad_value, recv_list[turn], devices, capacity)),
                "seq",
                split_axis=0,
                concat_axis=0,
                tiled=True,
            ),
        )
        grad_qk_sum = grad_qk_sum + unpacked(back_qk, send_list[turn])
        grad_value_sum = grad_value_sum + unpacked(back_value, send_list[turn])
    grad_qk_rows = grad_qk_sum.astype(jnp.bfloat16)
    grad_value_rows = grad_value_sum.astype(jnp.bfloat16)
    grad_qk = inner_rows(normed_one, grad_qk_rows)
    grad_value = inner_rows(normed_one, grad_value_rows)
    grad_one = outer_cols(grad_qk_rows, m_qk) + outer_cols(grad_value_rows, m_value)
    grad_gain_attn = jnp.sum(grad_one * hat_one, axis=0)
    grad_bias_attn = jnp.sum(grad_one, axis=0)
    dx_second = dy_second + norm_back(grad_one, hat_one, inv_one, gain_one)
    s_qk, s_value, s_out, s_gattn, s_battn, s_gffn, s_bffn, s_up, s_bup, s_down, s_bdown = (
        lax.psum_scatter(grad_qk, "seq", scatter_dimension=0, tiled=True),
        lax.psum_scatter(grad_value, "seq", scatter_dimension=0, tiled=True),
        lax.psum_scatter(grad_out, "seq", scatter_dimension=0, tiled=True),
        lax.psum_scatter(grad_gain_attn, "seq", scatter_dimension=0, tiled=True),
        lax.psum_scatter(grad_bias_attn, "seq", scatter_dimension=0, tiled=True),
        lax.psum_scatter(grad_gain_ffn, "seq", scatter_dimension=0, tiled=True),
        lax.psum_scatter(grad_bias_ffn, "seq", scatter_dimension=0, tiled=True),
        lax.psum_scatter(grad_up, "seq", scatter_dimension=0, tiled=True),
        lax.psum_scatter(grad_bias_up, "seq", scatter_dimension=0, tiled=True),
        lax.psum_scatter(grad_down, "seq", scatter_dimension=0, tiled=True),
        lax.psum_scatter(grad_bias_down, "seq", scatter_dimension=0, tiled=True),
    )
    return (
        y_first,
        y_second,
        dx_first,
        dx_second,
        s_qk,
        s_value,
        s_out,
        s_gattn,
        s_battn,
        s_gffn,
        s_bffn,
        s_up,
        s_bup,
        s_down,
        s_bdown,
    )


CAP_ROWS = 16
FORWARD_BATCH = 8
BACKWARD_BATCH = 2
PARTS = 8


def dot_nn(a, b):
    return lax.dot_general(a, b, (((1,), (0,)), ((), ())), preferred_element_type=F32)


def dot_nt(a, b):
    return lax.dot_general(a, b, (((1,), (1,)), ((), ())), preferred_element_type=F32)


def dot_tn(a, b):
    return lax.dot_general(a, b, (((0,), (0,)), ((), ())), preferred_element_type=F32)


def hot_rows(slot_row, slots):
    ids = lax.broadcasted_iota(jnp.int32, (slots, slot_row.shape[1]), 0).astype(F32)
    return jnp.where(ids == slot_row, 1.0, 0.0).astype(BF)


def hot_cols(slot_col, slots):
    ids = lax.broadcasted_iota(jnp.int32, (slot_col.shape[0], slots), 1).astype(F32)
    return jnp.where(ids == slot_col, 1.0, 0.0).astype(BF)


def keep_columns(factors, ids, start, keys, cols):
    rows = keys.shape[0]
    wide = keys.astype(F32)
    square = wide * wide
    high = square.astype(BF)
    low = (square - high.astype(F32)).astype(BF)
    ones = jnp.ones((HEAD_DIM, HEAD_DIM), BF)
    total = dot_nn(high, ones) + dot_nn(low, ones)
    factors[pl.ds(start, rows), :] = lax.rsqrt(total) * SCALE
    pick = lax.broadcasted_iota(jnp.int32, (PARTS, HEAD_DIM), 0) >= 6
    ids[pl.ds(start, rows), :] = dot_nn(cols.astype(BF), jnp.where(pick, 1.0, 0.0).astype(BF))


def pair_scores(raw, factor, key_ids, query_ids, query_starts):
    lane = lax.broadcasted_iota(jnp.int32, query_ids.shape, 1)
    first = jnp.where(lane < SPAN, query_ids, -1.0)
    second = jnp.where(lane >= SPAN, query_ids, -1.0)
    scores, masks = [], []
    for chunk, limits in enumerate((first, query_ids, second)):
        here = slice(chunk * SPAN, (chunk + 1) * SPAN)
        ids = key_ids[here]
        kept = (ids < limits) & (ids >= query_starts)
        score = jnp.where(kept, raw[here] * factor[here], -1000000000.0)
        if chunk > 0:
            score = jnp.where(ids == query_ids, -100000.0, score)
        scores.append(score)
        masks.append(kept)
    return scores, masks


def three_parts(wide):
    high = wide.astype(BF).astype(F32)
    rest = wide - high
    mid = rest.astype(BF).astype(F32)
    return high, mid, rest - mid


def forward_kernel(
    place,
    x_0,
    x_1,
    x_2,
    x_3,
    info,
    out_0,
    out_1,
    out_2,
    out_3,
    kept_rows,
    lanes,
    heads_out,
    factors,
    ids,
):
    blocks, tokens = info.shape[0], info.shape[2]
    slots = blocks * CAP_ROWS
    width = x_0.shape[1]
    pairs = tokens // (2 * SPAN)
    turn = place[0]
    rounds = ROUNDS

    for offset, rows in enumerate((x_0, x_1, x_2, x_3)):

        def pack(group, carry, offset=offset, rows=rows):
            source = group * rounds + lax.bitwise_xor(turn, offset)
            hot = hot_rows(info[source, 3:4, :], slots)
            start = pl.multiple_of(group * tokens, tokens)
            part = dot_nn(hot, rows[pl.ds(start, tokens), :]).astype(BF)
            lanes[:, pl.ds(source, 1)] = part.reshape(blocks, 1, CAP_ROWS, width)
            return carry

        lax.fori_loop(0, blocks // rounds, pack, 0, unroll=4)

    def place_rows(block, carry):
        cols = jnp.transpose(info[block])
        hot = hot_cols(cols[:, 2:3], slots)
        part = dot_nn(hot, lanes[block].reshape(slots, width)).astype(BF)
        start = pl.multiple_of(SPAN + block * tokens, SPAN)
        kept_rows[pl.ds(start, tokens), :] = part
        keep_columns(factors, ids, start, part[:, :HEAD_DIM], cols)
        return carry

    lax.fori_loop(0, blocks, place_rows, 0, unroll=4)
    for held in (kept_rows, factors, ids):
        held[0:SPAN, :] = held[blocks * tokens : blocks * tokens + SPAN, :]
    heads_out[:, :, HEAD_DIM:] = jnp.zeros((blocks, tokens, width - HEAD_DIM), BF)

    def attend(step, carry):
        todo = [(step * FORWARD_BATCH + at // pairs, at % pairs) for at in range(FORWARD_BATCH * pairs)]
        first = []
        for block, pair in todo:
            start = pl.multiple_of(block * tokens + pair * 2 * SPAN, SPAN)
            rows = kept_rows[pl.ds(start, 3 * SPAN), :]
            raw = dot_nt(rows[:, :HEAD_DIM], rows[SPAN:, :HEAD_DIM])
            first.append((start, rows[:, HEAD_DIM:], raw))
        second = []
        lse = []
        for (block, pair), (start, values, raw) in zip(todo, first):
            here = slice(pair * 2 * SPAN, (pair + 1) * 2 * SPAN)
            scores, _ = pair_scores(
                raw,
                factors[pl.ds(start, 3 * SPAN), :],
                ids[pl.ds(start, 3 * SPAN), :],
                info[block, 0:1, here],
                info[block, 1:2, here],
            )
            top = jnp.max(
                jnp.maximum(jnp.maximum(scores[0], scores[1]), scores[2]), axis=0, keepdims=True
            )
            weights = [jnp.exp(score - top) for score in scores]
            total = jnp.sum(weights[0] + weights[1] + weights[2], axis=0, keepdims=True)
            scale = 1.0 / total
            second.append(jnp.concatenate([weight * scale for weight in weights]).astype(BF))
            lse.append(top + jnp.log(total))
        for (block, pair), (start, values, raw), probs in zip(todo, first, second):
            here = slice(pair * 2 * SPAN, (pair + 1) * 2 * SPAN)
            heads_out[block, here, :HEAD_DIM] = dot_tn(probs, values).astype(BF)
        row = lax.broadcasted_iota(jnp.int32, (PARTS, tokens), 0)
        for at in range(FORWARD_BATCH):
            block = step * FORWARD_BATCH + at
            high, mid, low = three_parts(
                jnp.concatenate(lse[at * pairs : (at + 1) * pairs], axis=1)
            )
            flat = jnp.where(
                row == 0, high, jnp.where(row == 1, mid, jnp.where(row == 2, low, 0.0))
            )
            heads_out[block, :, HEAD_DIM : HEAD_DIM + PARTS] = jnp.transpose(flat).astype(BF)
        return carry

    lax.fori_loop(0, blocks // FORWARD_BATCH, attend, 0)

    def unplace(block, carry):
        hot = hot_rows(info[block, 2:3, :], slots)
        part = dot_nn(hot, heads_out[block]).astype(BF)
        lanes[:, pl.ds(block, 1)] = part.reshape(blocks, 1, CAP_ROWS, width)
        return carry

    lax.fori_loop(0, blocks, unplace, 0, unroll=4)

    for offset, out in enumerate((out_0, out_1, out_2, out_3)):

        def unpack(group, carry, offset=offset, out=out):
            source = group * rounds + lax.bitwise_xor(turn, offset)
            cols = jnp.transpose(info[source])
            hot = hot_cols(cols[:, 3:4], slots)
            part = dot_nn(hot, lanes[source].reshape(slots, width))
            out[group, 0:tokens, :] = part[:, :HEAD_DIM].astype(BF)
            flat = jnp.transpose(part[:, HEAD_DIM:])[0:PARTS, :].astype(BF)
            for piece in range(tokens // HEAD_DIM):
                first = tokens + piece * PARTS
                out[group, first : first + PARTS, :] = flat[
                    :, piece * HEAD_DIM : (piece + 1) * HEAD_DIM
                ]
            return carry

        lax.fori_loop(0, blocks // rounds, unpack, 0, unroll=4)


def flat_parts(ref, group, first, tokens):
    return jnp.concatenate(
        [
            ref[group, first + piece * PARTS : first + (piece + 1) * PARTS, :].astype(F32)
            for piece in range(tokens // HEAD_DIM)
        ],
        axis=1,
    )


def tall_parts(ref, group, first, tokens):
    return jnp.transpose(flat_parts(ref, group, first, tokens))


def put_parts(ref, group, first, line):
    tokens = line.shape[1]
    high, mid, low = three_parts(line)
    row = lax.broadcasted_iota(jnp.int32, (PARTS, tokens), 0)
    flat = jnp.where(row == 0, high, jnp.where(row == 1, mid, jnp.where(row == 2, low, 0.0)))
    flat = flat.astype(BF)
    for piece in range(tokens // HEAD_DIM):
        at = first + piece * PARTS
        ref[group, at : at + PARTS, :] = flat[:, piece * HEAD_DIM : (piece + 1) * HEAD_DIM]


def merge_weights(refs, groups):
    tokens = refs[0].shape[1] // (HEAD_DIM + PARTS) * HEAD_DIM
    found = []
    for group in range(groups):
        flats = [flat_parts(ref, group, tokens, tokens) for ref in refs]
        lse = [one[0:1] + one[1:2] + one[2:3] for one in flats]
        top = lse[0]
        for other in lse[1:]:
            top = jnp.maximum(top, other)
        weights = [jnp.exp(one - top) for one in lse]
        total = sum(weights[1:], weights[0])
        scale = 1.0 / total
        lines = [weight * scale for weight in weights]
        lines.append(jnp.zeros((PARTS - len(lines), tokens), F32))
        found.append((jnp.transpose(jnp.concatenate(lines, axis=0)), top + jnp.log(total)))
    return tokens, found


def merged_rows(refs, group, tokens, weights):
    rows = [
        weights[:, at : at + 1] * ref[group, 0:tokens, :].astype(F32)
        for at, ref in enumerate(refs)
    ]
    return sum(rows[1:], rows[0]).astype(BF)


def pair_kernel(a, b, out):
    tokens, found = merge_weights((a, b), out.shape[0])
    for group, (weights, lse) in enumerate(found):
        put_parts(out, group, tokens, lse)
    for group, (weights, lse) in enumerate(found):
        out[group, 0:tokens, :] = merged_rows((a, b), group, tokens, weights)


def final_kernel(a, b, c, mixed, total_lse):
    tokens, found = merge_weights((a, b, c), mixed.shape[0])
    for group, (weights, lse) in enumerate(found):
        put_parts(total_lse, group, 0, lse)
    for group, (weights, lse) in enumerate(found):
        mixed[group] = merged_rows((a, b, c), group, tokens, weights)


def backward_kernel(
    place,
    g_0,
    g_1,
    g_2,
    g_3,
    l_0,
    l_1,
    l_2,
    l_3,
    kept_rows,
    info,
    out_0,
    out_1,
    out_2,
    out_3,
    lanes,
    sums,
    factors,
    ids,
    rows_in,
    stats,
):
    blocks, tokens = info.shape[0], info.shape[2]
    slots = blocks * CAP_ROWS
    width = kept_rows.shape[1]
    pairs = tokens // (2 * SPAN)

    for offset, grads, lse in ((0, g_0, l_0), (1, g_1, l_1), (2, g_2, l_2), (3, g_3, l_3)):

        def pack(group, carry, offset=offset, grads=grads, lse=lse):
            source = group * ROUNDS + lax.bitwise_xor(place[0], offset)
            hot = hot_rows(info[source, 3:4, :], slots)
            tall = [tall_parts(grads, group, tokens, tokens), tall_parts(lse, group, 0, tokens)]
            tall.append(jnp.zeros((tokens, HEAD_DIM - 2 * PARTS), F32))
            rows = jnp.concatenate(
                [grads[group, 0:tokens, :], jnp.concatenate(tall, axis=1).astype(BF)], axis=1
            )
            part = dot_nn(hot, rows).astype(BF)
            lanes[:, pl.ds(source, 1)] = part.reshape(blocks, 1, CAP_ROWS, width)
            return carry

        lax.fori_loop(0, blocks // ROUNDS, pack, 0, unroll=4)

    sums[0:SPAN, :] = jnp.zeros((SPAN, width), F32)

    def place_rows(block, carry):
        cols = jnp.transpose(info[block])
        hot = hot_cols(cols[:, 2:3], slots)
        part = dot_nn(hot, lanes[block].reshape(slots, width))
        rows_in[block] = part[:, :HEAD_DIM].astype(BF)
        flat = jnp.transpose(part[:, HEAD_DIM:])
        stats[block, 0:1, :] = flat[0:1] + flat[1:2] + flat[2:3]
        stats[block, 1:2, :] = flat[PARTS : PARTS + 1] + (
            flat[PARTS + 1 : PARTS + 2] + flat[PARTS + 2 : PARTS + 3]
        )
        start = pl.multiple_of(SPAN + block * tokens, SPAN)
        keys = kept_rows[pl.ds(start, tokens), :HEAD_DIM]
        keep_columns(factors, ids, start, keys, cols)
        return carry

    lax.fori_loop(0, blocks, place_rows, 0, unroll=4)
    for held in (factors, ids):
        held[0:SPAN, :] = held[blocks * tokens : blocks * tokens + SPAN, :]

    def attend(step, carry):
        todo = [(step * BACKWARD_BATCH + at // pairs, at % pairs) for at in range(BACKWARD_BATCH * pairs)]
        first = []
        for block, pair in todo:
            start = pl.multiple_of(block * tokens + pair * 2 * SPAN, SPAN)
            here = slice(pair * 2 * SPAN, (pair + 1) * 2 * SPAN)
            rows = kept_rows[pl.ds(start, 3 * SPAN), :]
            keys = rows[:, :HEAD_DIM]
            queries = rows[SPAN:, :HEAD_DIM]
            grads = rows_in[block, here, :]
            raw = dot_nt(keys, queries)
            back = dot_nt(rows[:, HEAD_DIM:], grads)
            first.append((start, keys, queries, grads, raw, back))
        second = []
        for (block, pair), (start, keys, queries, grads, raw, back) in zip(todo, first):
            here = slice(pair * 2 * SPAN, (pair + 1) * 2 * SPAN)
            factor = factors[pl.ds(start, 3 * SPAN), :]
            scores, masks = pair_scores(
                raw,
                factor,
                ids[pl.ds(start, 3 * SPAN), :],
                info[block, 0:1, here],
                info[block, 1:2, here],
            )
            pull = stats[block, 0:1, here]
            total_lse = stats[block, 1:2, here]
            weights = [jnp.exp(score - total_lse) for score in scores]
            weights_all = jnp.concatenate(weights).astype(BF)
            grad_score = jnp.concatenate(
                [
                    jnp.where(
                        mask, weight * (back[chunk * SPAN : (chunk + 1) * SPAN] - pull), 0.0
                    )
                    for chunk, (mask, weight) in enumerate(zip(masks, weights))
                ]
            )
            slope = jnp.sum(grad_score * raw, axis=1, keepdims=True)
            drift = slope * (factor * factor * factor * HEAD_DIM) * keys.astype(F32)
            second.append(((grad_score * factor).astype(BF), weights_all, drift))
        for (start, keys, queries, grads, _, _), (grad_raw, weights_all, drift) in zip(
            first, second
        ):
            grad_val = dot_nn(weights_all, grads)
            grad_key = dot_nn(grad_raw, queries) - drift
            grad_query = dot_tn(grad_raw, keys)
            sums[pl.ds(start, SPAN), :] += jnp.concatenate(
                [grad_key[:SPAN], grad_val[:SPAN]], axis=1
            )
            after = pl.multiple_of(start + SPAN, SPAN)
            sums[pl.ds(after, 2 * SPAN), :] = jnp.concatenate(
                [grad_query + grad_key[SPAN:], grad_val[SPAN:]], axis=1
            )
        return carry

    lax.fori_loop(0, blocks // BACKWARD_BATCH, attend, 0)
    sums[blocks * tokens : blocks * tokens + SPAN, :] += sums[0:SPAN, :]

    def unplace(block, carry):
        hot = hot_rows(info[block, 2:3, :], slots)
        start = pl.multiple_of(SPAN + block * tokens, SPAN)
        part = dot_nn(hot, sums[pl.ds(start, tokens), :].astype(BF)).astype(BF)
        lanes[:, pl.ds(block, 1)] = part.reshape(blocks, 1, CAP_ROWS, width)
        return carry

    lax.fori_loop(0, blocks, unplace, 0, unroll=4)

    for offset, out in enumerate((out_0, out_1, out_2, out_3)):

        def unpack(group, carry, offset=offset, out=out):
            source = group * ROUNDS + lax.bitwise_xor(place[0], offset)
            cols = jnp.transpose(info[source])
            hot = hot_cols(cols[:, 3:4], slots)
            start = pl.multiple_of(group * tokens, tokens)
            part = dot_nn(hot, lanes[source].reshape(slots, width))
            out[pl.ds(start, tokens), :] = part.astype(BF)
            return carry

        lax.fori_loop(0, blocks // ROUNDS, unpack, 0, unroll=4)


def in_vmem(count):
    return [pl.BlockSpec(memory_space=pltpu.VMEM)] * count


def run_kernel(kernel, name, operands, shapes, scratch, scalar):
    first = [pl.BlockSpec(memory_space=pltpu.SMEM)] if scalar else []
    return pl.pallas_call(
        kernel,
        out_shape=tuple(jax.ShapeDtypeStruct(shape, BF) for shape in shapes),
        in_specs=first + in_vmem(len(operands) - len(first)),
        out_specs=tuple(in_vmem(len(shapes))),
        scratch_shapes=[pltpu.VMEM(shape, dtype) for shape, dtype in scratch],
        compiler_params=pltpu.CompilerParams(vmem_limit_bytes=48 << 20),
        cost_estimate=pl.CostEstimate(
            flops=20 * 10**9 if scalar else 10**7,
            bytes_accessed=12 * 10**6 if scalar else 2 * 10**6,
            transcendentals=10**6 if scalar else 10**4,
        ),
        name=name,
    )(*operands)


def run_forward(turn, rows, info):
    blocks, _, tokens = info.shape
    width = rows[0].shape[1]
    tall = tokens + PARTS * tokens // HEAD_DIM
    return run_kernel(
        forward_kernel,
        "hash_forward",
        (turn, *rows, info),
        [(blocks // ROUNDS, tall, HEAD_DIM)] * ROUNDS + [(SPAN + blocks * tokens, width)],
        [((blocks, blocks, CAP_ROWS, width), BF), ((blocks, tokens, width), BF)]
        + [((SPAN + blocks * tokens, HEAD_DIM), F32)] * 2,
        True,
    )


def run_backward(turn, grads, lse, kept_rows, info):
    blocks, _, tokens = info.shape
    width = kept_rows.shape[1]
    return run_kernel(
        backward_kernel,
        "hash_backward",
        (turn, *grads, *lse, kept_rows, info),
        [(blocks * tokens // ROUNDS, width)] * ROUNDS,
        [((blocks, blocks, CAP_ROWS, width), BF), ((SPAN + blocks * tokens, width), F32)]
        + [((SPAN + blocks * tokens, HEAD_DIM), F32)] * 2
        + [((blocks, tokens, HEAD_DIM), BF), ((blocks, 8, tokens), F32)],
        True,
    )


def merge_pair(a, b):
    return run_kernel(pair_kernel, "merge_pair", (a, b), [a.shape], [], False)[0]


def merge_final(a, b, c):
    groups, tall, width = a.shape
    tokens = tall // (HEAD_DIM + PARTS) * HEAD_DIM
    shapes = [(groups, tokens, width), (groups, tall - tokens, width)]
    return run_kernel(final_kernel, "merge_final", (a, b, c), shapes, [], False)


def peers(mask):
    size = HEADS * ROUNDS
    return [(i, i ^ mask) for i in range(size)]


def swap(x, mask):
    return lax.ppermute(x, "seq", peers(mask))


def columns():
    return [[head * ROUNDS + turn for head in range(HEADS)] for turn in range(ROUNDS)]


def rows_of():
    return [[head * ROUNDS + turn for turn in range(ROUNDS)] for head in range(HEADS)]


def gather_group(x):
    side = swap(x, 2)
    return (x, swap(x, 1), side, swap(side, 1))


def sum_group(parts):
    near = parts[0] + swap(parts[1].astype(BF), 1).astype(F32)
    far = parts[2] + swap(parts[3].astype(BF), 1).astype(F32)
    return near + swap(far.astype(BF), 2).astype(F32)


def row_major(x):
    return with_layout_constraint(x.astype(BF), Layout(major_to_minor=(0, 1)))


def exchange(x, groups=None):
    return lax.all_to_all(
        x, "seq", split_axis=0, concat_axis=0, tiled=True, axis_index_groups=groups
    )


def rounded(x):
    return lax.reduce_precision(x, 8, 7)


def split_three(wide):
    high = rounded(wide)
    rest = wide - high
    mid = rounded(rest)
    return jnp.stack([high, mid, rest - mid])


def slots_sent(target, tokens, capacity):
    device = target // tokens
    early = jnp.arange(tokens)[None, :] < jnp.arange(tokens)[:, None]
    same = (device[:, None] == device[None, :]) & early
    return device * capacity + jnp.sum(same.astype(jnp.int32), axis=1)


def start_of(token_ids, doc_ends):
    ends = doc_ends[None, :]
    return jnp.max(jnp.where(ends <= token_ids[:, None], ends, 0), axis=1)


def shards_fast(
    x_first,
    x_second,
    w_qk,
    w_value,
    w_out,
    gain_attn,
    bias_attn,
    gain_ffn,
    bias_ffn,
    w_up,
    bias_up,
    w_down,
    bias_down,
    sort_order,
    inverse,
    lengths,
    dy_first,
    dy_second,
):
    devices = lax.axis_size("seq")
    tokens, features = x_first.shape
    capacity = 2 * tokens // devices
    shard = features // devices
    place = lax.axis_index("seq")
    doc_ends = jnp.cumsum(lengths)

    per_round = []
    vectors = rounded(
        jnp.concatenate([gain_attn, bias_attn, gain_ffn, bias_ffn, bias_up, bias_down])
    )
    vectors = jnp.pad(vectors, (0, 2 * tokens - vectors.shape[0])).reshape(2, tokens)
    for turn in range(ROUNDS):
        ids = sort_order[turn]
        rows = jnp.stack(
            [
                ids,
                start_of(ids, doc_ends),
                recv_slots(ids, tokens, capacity),
                slots_sent(inverse[turn], tokens, capacity),
            ]
        ).astype(F32)
        split = jnp.stack([ids // SPAN * SPAN, ids % SPAN]).astype(F32)
        per_round.append(jnp.concatenate([rows, vectors, split]))
    info = jnp.tile(jnp.stack(per_round), (HEADS, 1, 1))
    info = exchange(info)
    got = info[:, 4:6].reshape(devices, 2 * tokens)

    def vector(first, size):
        return got[:, first : first + size].reshape(devices * size)

    gain_one, shift_one = vector(0, shard), vector(shard, shard)
    gain_two, shift_two = vector(2 * shard, shard), vector(3 * shard, shard)
    wide = bias_up.shape[0]
    b_up = vector(4 * shard, wide)
    b_down = vector(4 * shard + wide, shard)
    m_pair = lax.all_gather(
        jnp.concatenate([w.astype(BF) for w in (w_qk, w_value, w_out)], axis=1),
        "seq",
        axis=0,
        tiled=True,
    )
    m_pair, m_out = m_pair[:, : 2 * features], m_pair[:, 2 * features :]
    half = HEADS * wide
    up_cols = jnp.transpose(
        w_up.astype(BF).reshape(shard, HEADS, ROUNDS, wide), (2, 0, 1, 3)
    ).reshape(ROUNDS, shard, half)
    near_rows = exchange(up_cols, rows_of()).reshape(ROUNDS * shard, half)
    b_up = lax.dynamic_index_in_dim(
        b_up.reshape(HEADS, ROUNDS, wide), place % ROUNDS, axis=1, keepdims=False
    ).reshape(HEADS * wide)

    normed_one, hat_one, inv_one = layer_norm(x_second, gain_one, shift_one)
    grad_f = dy_second.astype(BF)
    normed_one, near_rows, grad_f_all = lax.optimization_barrier(
        (normed_one.astype(BF), near_rows, gather_group(grad_f))
    )
    grad_f_all = jnp.concatenate(grad_f_all)
    rows = linear(normed_one, m_pair).astype(BF)
    rows = jnp.transpose(rows.reshape(tokens, 2, HEADS, HEAD_DIM), (2, 0, 1, 3))
    own = exchange(rows.reshape(HEADS, tokens, 2 * HEAD_DIM), columns()).reshape(HEADS * tokens, 2 * HEAD_DIM)
    own, near_rows = lax.optimization_barrier((own, near_rows))
    m_ffn = lax.all_gather(
        jnp.concatenate([near_rows, w_down.astype(BF)], axis=1),
        "seq",
        axis=0,
        tiled=True,
        axis_index_groups=columns(),
    )
    turn = (place % ROUNDS).astype(jnp.int32).reshape(1)
    *sent, kept_rows = run_forward(turn, gather_group(own), info)
    far = merge_pair(sent[2], swap(sent[3], 1))
    mixed, total_lse = merge_final(sent[0], swap(sent[1], 1), swap(far, 2))
    mixed = exchange(mixed, columns())
    m_ffn, normed_one = lax.optimization_barrier((m_ffn, normed_one))
    m_up, m_down = m_ffn[:, :half], m_ffn[:, half:]
    grad_hidden = outer_cols(grad_f_all, m_down)
    mixed, grad_hidden, total_lse = lax.optimization_barrier(
        (mixed, grad_hidden, gather_group(total_lse))
    )
    normed_col = lax.all_gather(
        normed_one, "seq", axis=0, tiled=True, axis_index_groups=columns()
    )
    mixed = jnp.transpose(mixed, (1, 0, 2)).reshape(tokens, features)
    y_first = x_first + linear(mixed, m_out)
    normed_two, hat_two, inv_two = layer_norm(y_first, gain_two, shift_two)
    normed_two = normed_two.astype(BF)
    side = swap(normed_two, 2)
    halves = (
        jnp.concatenate([normed_two, swap(normed_two, 1)]),
        jnp.concatenate([side, swap(side, 1)]),
    )
    found = []
    for at, rows in enumerate(halves):
        pre_up = linear(rows, m_up) + b_up
        hidden, gelu_back = jax.vjp(partial(jax.nn.gelu, approximate=True), pre_up)
        grad_pre = grad_hidden[at * 2 * tokens : (at + 1) * 2 * tokens]
        grad_pre = gelu_back(grad_pre)[0].astype(BF)
        grad_two = outer_cols(grad_pre, m_up)
        found.append((hidden.astype(BF), grad_pre, grad_two[:tokens], grad_two[tokens:]))
    normed_all = jnp.concatenate(halves)
    hidden, grad_pre = (jnp.concatenate([found[0][at], found[1][at]]) for at in range(2))
    grad_down = inner_rows(hidden, grad_f_all)
    grad_bias_down = jnp.sum(grad_f.astype(F32), axis=0)
    normed_all, normed_col = lax.optimization_barrier((normed_all, normed_col))
    grad_up = inner_rows(normed_all, grad_pre)
    grad_bias_up = jnp.sum(grad_pre.astype(F32), axis=0)
    grad_two = sum_group([*found[0][2:], *found[1][2:]])
    grad_gain_ffn = jnp.sum(grad_two * hat_two, axis=0)
    grad_bias_ffn = jnp.sum(grad_two, axis=0)
    dx_first = dy_first + norm_back(grad_two, hat_two, inv_two, gain_two)
    grad_attn = dx_first.astype(BF)
    grad_out = inner_rows(mixed, grad_attn)
    fourth = features // ROUNDS
    grad_mixed = outer_cols(grad_attn, m_out).astype(BF)
    pull = jnp.sum(
        (grad_mixed.astype(F32) * mixed.astype(F32)).reshape(tokens, HEADS, HEAD_DIM), axis=-1
    )
    parts = split_three(jnp.transpose(pull))
    parts = jnp.pad(parts, ((0, PARTS - 3), (0, 0), (0, 0)))
    parts = jnp.transpose(parts.reshape(PARTS, HEADS, -1, HEAD_DIM), (1, 2, 0, 3))
    parts = parts.reshape(HEADS, -1, HEAD_DIM).astype(BF)
    grad_mixed = jnp.transpose(grad_mixed.reshape(tokens, HEADS, HEAD_DIM), (1, 0, 2))
    grad_mixed, normed_col = lax.optimization_barrier(
        (jnp.concatenate([grad_mixed, parts], axis=1), normed_col)
    )
    grad_mixed = exchange(grad_mixed, columns())
    grad_out = sum_group(
        [
            lax.dynamic_slice_in_dim(grad_out, ((place % ROUNDS) ^ near) * fourth, fourth, axis=1)
            for near in range(ROUNDS)
        ]
    )
    merged = jnp.concatenate([row_major(x) for x in (grad_up, grad_out, grad_down)], axis=1)
    grad_mixed, merged = lax.optimization_barrier((grad_mixed, merged))
    grad_mixed = list(gather_group(grad_mixed))
    merged, normed_col, grad_mixed[1] = lax.optimization_barrier(
        (merged, normed_col, grad_mixed[1])
    )
    merged = lax.psum_scatter(
        merged, "seq", scatter_dimension=0, tiled=True, axis_index_groups=columns()
    )
    s_down = merged[:, half + fourth :].astype(F32)
    merged = merged[:, : half + fourth].reshape(ROUNDS, shard, -1)
    pieces = [
        lax.dynamic_index_in_dim(merged, (place % ROUNDS) ^ near, axis=0, keepdims=False)
        for near in range(ROUNDS)
    ]
    pieces = [swap(piece, near) if near else piece for near, piece in enumerate(pieces)]

    def in_order(first, last):
        mine = place % ROUNDS
        found = []
        for peer in range(ROUNDS):
            options = [pieces[peer ^ at][:, first:last] for at in range(ROUNDS)]
            low = jnp.where(mine == 0, options[0], options[1])
            high = jnp.where(mine == 2, options[2], options[3])
            found.append(jnp.where(mine < 2, low, high))
        return jnp.stack(found, axis=1).astype(F32)

    s_up = in_order(0, half).reshape(shard, ROUNDS, HEADS, wide)
    s_up = jnp.transpose(s_up, (0, 2, 1, 3)).reshape(shard, ROUNDS * half)
    s_out = in_order(half, half + fourth).reshape(shard, features)

    grad_head = run_backward(
        turn, grad_mixed, total_lse, kept_rows, info
    )
    near_head = grad_head[0].astype(F32) + swap(grad_head[1], 1).astype(F32)
    far_head = grad_head[2].astype(F32) + swap(grad_head[3], 1).astype(F32)
    far_head, hidden = lax.optimization_barrier((far_head.astype(BF), hidden))
    far_head = swap(far_head, 2)
    branch = linear(hidden, m_down).reshape(ROUNDS, tokens, features)
    branch_near = branch[0] + swap(branch[1].astype(BF), 1).astype(F32)
    branch_far = (branch[2] + swap(branch[3].astype(BF), 1).astype(F32)).astype(BF)
    far_head, near_head, branch_near, branch_far, grad_bias_up, grad_bias_down = (
        lax.optimization_barrier(
            (far_head, near_head, branch_near, branch_far, grad_bias_up, grad_bias_down)
        )
    )
    grad_head = (near_head + far_head.astype(F32)).astype(BF)
    branch = branch_near + swap(branch_far, 2).astype(F32)
    y_second = x_second + (branch + b_down)
    grad_rows = exchange(grad_head.reshape(HEADS, tokens, 2 * HEAD_DIM), columns())
    s_pair = inner_rows(normed_col, grad_head).astype(BF).reshape(devices, shard, 2 * HEAD_DIM)
    grad_rows, s_pair, s_up, s_out, s_down, y_second = lax.optimization_barrier(
        (grad_rows, s_pair, s_up, s_out, s_down, y_second)
    )
    grad_rows = grad_rows.reshape(HEADS, tokens, 2, HEAD_DIM)
    grad_rows = jnp.transpose(grad_rows, (1, 2, 0, 3)).reshape(tokens, 2 * features)
    grad_one = outer_cols(grad_rows, m_pair)
    grad_gain_attn = jnp.sum(grad_one * hat_one, axis=0)
    grad_bias_attn = jnp.sum(grad_one, axis=0)
    dx_second = dy_second + norm_back(grad_one, hat_one, inv_one, gain_one)
    is_mine = (jnp.arange(ROUNDS) == place % ROUNDS).astype(F32)
    grad_bias_up = grad_bias_up.reshape(HEADS, 1, wide) * is_mine[None, :, None]
    small = jnp.concatenate(
        [
            grad_gain_attn.reshape(devices, -1),
            grad_bias_attn.reshape(devices, -1),
            grad_gain_ffn.reshape(devices, -1),
            grad_bias_ffn.reshape(devices, -1),
            grad_bias_up.reshape(devices, -1),
            grad_bias_down.reshape(devices, -1),
        ],
        axis=1,
    )
    count = small.shape[1]
    lines = -(-3 * count // (2 * HEAD_DIM))
    small = jnp.transpose(split_three(small), (1, 0, 2)).reshape(devices, 3 * count)
    small = jnp.pad(small, ((0, 0), (0, lines * 2 * HEAD_DIM - 3 * count)))
    small = small.astype(BF).reshape(devices, lines, 2 * HEAD_DIM)
    both = exchange(jnp.concatenate([s_pair, small], axis=1))
    small = both[:, shard:].reshape(devices, -1)[:, : 3 * count].astype(F32)
    small = jnp.sum(small.reshape(devices * 3, count), axis=0)
    s_pair = both[:, :shard].reshape(HEADS, ROUNDS, shard, 2, HEAD_DIM)
    s_pair = jnp.sum(s_pair.astype(F32), axis=1).transpose(2, 1, 0, 3)
    s_qk = s_pair[0].reshape(shard, features)
    s_value = s_pair[1].reshape(shard, features)
    s_gattn, s_battn, s_gffn, s_bffn = (small[i * shard : (i + 1) * shard] for i in range(4))
    s_bup = small[4 * shard : 4 * shard + wide]
    s_bdown = small[4 * shard + wide :]
    return (
        y_first,
        y_second,
        dx_first,
        dx_second,
        s_qk,
        s_value,
        s_out,
        s_gattn,
        s_battn,
        s_gffn,
        s_bffn,
        s_up,
        s_bup,
        s_down,
        s_bdown,
    )


def solution(mesh):
    in_specs = (
        P("seq", None),
        P("seq", None),
        P("seq", None),
        P("seq", None),
        P("seq", None),
        P("seq"),
        P("seq"),
        P("seq"),
        P("seq"),
        P("seq", None),
        P("seq"),
        P("seq", None),
        P("seq"),
        P(None, "seq"),
        P(None, "seq"),
        P(),
        P("seq", None),
        P("seq", None),
    )
    out_specs = (
        P("seq", None),
        P("seq", None),
        P("seq", None),
        P("seq", None),
        P("seq", None),
        P("seq", None),
        P("seq", None),
        P("seq"),
        P("seq"),
        P("seq"),
        P("seq"),
        P("seq", None),
        P("seq"),
        P("seq", None),
        P("seq"),
    )
    fast = mesh.shape["seq"] == HEADS * ROUNDS
    return jax.shard_map(shards_fast if fast else shards, mesh=mesh, in_specs=in_specs, out_specs=out_specs, check_vma=False)
```
